32 devices in a mesh: dp: 8 (over z, y), mp: 4 (over x, core).
Axes of the slice: x: 2, y: 2, z: 4, core: 2. Of those that a mesh axis runs over, the one named last changes fastest.
Arguments:
- tokens: bfloat16 [32, 256, 1152], P('dp'), may hold values from -6 to 6
- condition: bfloat16 [32, 1152], P('dp'), may hold values from -6 to 6
- cotangent: bfloat16 [32, 256, 1152], P('dp'), may hold values from -12 to 12
- kept_index: int32 [32, 128], P('dp'), may hold values from 0 to 255, as said below
- skip_index: int32 [32, 128], P('dp'), may hold values from 0 to 255, as said below
- step_count: int32 [1], replicated, may hold values from 1 to 20
- ada_weight: float32 [1152, 6, 1152], P('dp', None, 'mp'), may hold values from -0.1875 to 0.1875
- qkv_weight: float32 [3, 1152, 1152], P(None, 'dp', 'mp'), may hold values from -0.1875 to 0.1875
- proj_weight: float32 [1152, 1152], P('mp', 'dp'), may hold values from -1 to 1
- fc1_weight: float32 [1152, 4608], P('dp', 'mp'), may hold values from -0.1875 to 0.1875
- fc2_weight: float32 [4608, 1152], P('mp', 'dp'), may hold values from -0.09375 to 0.09375
- ada_moment: float32 [1152, 6, 1152], P('dp', None, 'mp'), may hold values from -80 to 80
- qkv_moment: float32 [3, 1152, 1152], P(None, 'dp', 'mp'), may hold values from -80 to 80
- proj_moment: float32 [1152, 1152], P('mp', 'dp'), may hold values from -80 to 80
- fc1_moment: float32 [1152, 4608], P('dp', 'mp'), may hold values from -80 to 80
- fc2_moment: float32 [4608, 1152], P('mp', 'dp'), may hold values from -80 to 80
- ada_average: float32 [1152, 6, 1152], P('dp', None, 'mp'), may hold values from -0.1875 to 0.1875
- qkv_average: float32 [3, 1152, 1152], P(None, 'dp', 'mp'), may hold values from -0.1875 to 0.1875
- proj_average: float32 [1152, 1152], P('mp', 'dp'), may hold values from -1 to 1
- fc1_average: float32 [1152, 4608], P('dp', 'mp'), may hold values from -0.1875 to 0.1875
- fc2_average: float32 [4608, 1152], P('mp', 'dp'), may hold values from -0.09375 to 0.09375
Outputs:
- block_out: bfloat16 [32, 256, 1152], P('dp')
- tokens_grad: float32 [32, 256, 1152], P('dp')
- condition_grad: float32 [32, 1152], P('dp')
- ada_master: float32 [1152, 6, 1152], P('dp', None, 'mp')
- qkv_master: float32 [3, 1152, 1152], P(None, 'dp', 'mp')
- proj_master: float32 [1152, 1152], P('mp', 'dp')
- fc1_master: float32 [1152, 4608], P('dp', 'mp')
- fc2_master: float32 [4608, 1152], P('mp', 'dp')
- ada_momentum: float32 [1152, 6, 1152], P('dp', None, 'mp')
- qkv_momentum: float32 [3, 1152, 1152], P(None, 'dp', 'mp')
- proj_momentum: float32 [1152, 1152], P('mp', 'dp')
- fc1_momentum: float32 [1152, 4608], P('dp', 'mp')
- fc2_momentum: float32 [4608, 1152], P('mp', 'dp')
- ada_ema: float32 [1152, 6, 1152], P('dp', None, 'mp')
- qkv_ema: float32 [3, 1152, 1152], P(None, 'dp', 'mp')
- proj_ema: float32 [1152, 1152], P('mp', 'dp')
- fc1_ema: float32 [1152, 4608], P('dp', 'mp')
- fc2_ema: float32 [4608, 1152], P('mp', 'dp')
The draws below stay inside these ranges and needn't reach their ends.
Inputs may be any that keep to these rules, and one draw needn't show every extreme that they name: `kept_index`: row b lists 128 distinct positions of image b in increasing order; row b of skip_index lists the other 128 positions in increasing order. `skip_index`: row b lists the positions of image b that kept_index does not, in increasing order.
All inputs are finite; a program needn't handle non-finite values.
Results may differ from the reference program's by a relative error of at most 0.012.
The reference program's roundings to bfloat16 on the way count: a program that leaves them out, or rounds other values in their place, can miss the bound.
Values may be sent and summed in bfloat16 or wider, within the bound.
No kernel may reach another device: no remote copies, remote signals or barrier semaphores. Data moves between devices by JAX's collectives and lax.ppermute only.
A program may use at most 192 MiB of HBM per device.

```python
import math
import jax
import jax.numpy as jnp
from jax import lax

D = 1152
HEADS = 16
HEAD_DIM = 72
FF = 4608
MODS = 6
SEQ = 256
KEPT = 128
IMG_DEV = 4
IMAGES = 32
N_DP = 8


def route_order(key):
    folded = jax.random.fold_in(key, 11)
    subkeys = jax.random.split(folded, IMAGES)
    return jax.vmap(lambda single: jax.random.permutation(single, SEQ))(subkeys)


def draw_kept_index(key, part):
    shuffled = route_order(key)
    return jnp.sort(shuffled[:, :KEPT], axis=1).astype(jnp.int32)


def draw_skip_index(key, part):
    shuffled = route_order(key)
    return jnp.sort(shuffled[:, KEPT:], axis=1).astype(jnp.int32)


def unit_values(key, shape):
    values = jax.random.normal(key, shape, jnp.float32)
    return values


def row_scales(key, rows):
    return jax.random.uniform(key, (rows,), jnp.float32, 0.7, 1.4)


def draw_tokens(key, part):
    values = unit_values(jax.random.fold_in(key, 21), (IMAGES, SEQ, D))
    scales = row_scales(jax.random.fold_in(key, 22), IMAGES)
    return jnp.clip(values * scales[:, None, None], -6.0, 6.0).astype(jnp.bfloat16)


def draw_condition(key, part):
    values = unit_values(jax.random.fold_in(key, 31), (IMAGES, D))
    return jnp.clip(values, -6.0, 6.0).astype(jnp.bfloat16)


def draw_cotangent(key, part):
    values = unit_values(jax.random.fold_in(key, 41), (IMAGES, SEQ, D))
    scales = row_scales(jax.random.fold_in(key, 42), IMAGES)
    pairing = jax.random.permutation(jax.random.fold_in(key, 43), N_DP)
    image_block = jnp.arange(IMAGES, dtype=jnp.int32) // IMG_DEV
    column_block = jnp.arange(D, dtype=jnp.int32) // (D // N_DP)
    hit = (pairing[image_block][:, None] == column_block[None, :]).astype(jnp.float32)
    boost = 1.0 + 2.0 * hit
    return jnp.clip(values * scales[:, None, None] * boost[:, None, :], -12.0, 12.0).astype(jnp.bfloat16)


def block_levels(key, dims, shards, low, top_value):
    loudness = 1.0
    for dim, shards_of in shards:
        draws = jax.random.uniform(jax.random.fold_in(jax.random.fold_in(key, 6), dim), (shards_of,), jnp.float32, low / len(shards), top_value / len(shards))
        loudness = loudness * jnp.repeat(jnp.exp(draws), dims[dim] // shards_of).reshape((-1,) + (1,) * (len(dims) - 1 - dim))
    return loudness


def noise(own_key, dims, spread, reach, shards=(), held_as=jnp.bfloat16):
    drawn = spread * jax.random.normal(own_key, dims, jnp.float32)
    if shards:
        drawn = drawn * block_levels(own_key, dims, shards, -0.22, 0.18)
    return jnp.clip(drawn, -reach, reach).astype(held_as)


def setup_inputs(seed: int = 0) -> dict:
    keys = jax.random.split(jax.random.key(seed), 22)
    tokens = draw_tokens(jax.random.fold_in(keys[21], 71), 0)
    condition = draw_condition(jax.random.fold_in(keys[21], 71), 0)
    cotangent = draw_cotangent(jax.random.fold_in(keys[21], 71), 0)
    kept_index = draw_kept_index(jax.random.fold_in(keys[21], 71), 0)
    skip_index = draw_skip_index(jax.random.fold_in(keys[21], 71), 0)
    step_count = jax.random.randint(keys[5], (1,), 1, 21).astype(jnp.int32)
    ada_weight = noise(keys[6], (D, MODS, D), D ** -0.5, 0.1875, ((0, 8), (2, 4)), jnp.float32)
    qkv_weight = noise(keys[7], (3, D, D), D ** -0.5, 0.1875, ((1, 8), (2, 4)), jnp.float32)
    proj_weight = noise(keys[8], (D, D), (D // 32) ** -0.5, 1.0, ((0, 4), (1, 8)), jnp.float32)
    fc1_weight = noise(keys[9], (D, FF), D ** -0.5, 0.1875, ((0, 8), (1, 4)), jnp.float32)
    fc2_weight = noise(keys[10], (FF, D), FF ** -0.5, 0.09375, ((0, 4), (1, 8)), jnp.float32)
    ada_moment = noise(keys[11], (D, MODS, D), (0.2 * (IMAGES * KEPT) ** 0.5), 80.0, ((0, 8), (2, 4)), jnp.float32)
    qkv_moment = noise(keys[12], (3, D, D), (0.2 * (IMAGES * KEPT) ** 0.5), 80.0, ((1, 8), (2, 4)), jnp.float32)
    proj_moment = noise(keys[13], (D, D), (0.2 * (IMAGES * KEPT) ** 0.5), 80.0, ((0, 4), (1, 8)), jnp.float32)
    fc1_moment = noise(keys[14], (D, FF), (0.2 * (IMAGES * KEPT) ** 0.5), 80.0, ((0, 8), (1, 4)), jnp.float32)
    fc2_moment = noise(keys[15], (FF, D), (0.2 * (IMAGES * KEPT) ** 0.5), 80.0, ((0, 4), (1, 8)), jnp.float32)
    ada_average = noise(keys[16], (D, MODS, D), D ** -0.5, 0.1875, ((0, 8), (2, 4)), jnp.float32)
    qkv_average = noise(keys[17], (3, D, D), D ** -0.5, 0.1875, ((1, 8), (2, 4)), jnp.float32)
    proj_average = noise(keys[18], (D, D), (D // 32) ** -0.5, 1.0, ((0, 4), (1, 8)), jnp.float32)
    fc1_average = noise(keys[19], (D, FF), D ** -0.5, 0.1875, ((0, 8), (1, 4)), jnp.float32)
    fc2_average = noise(keys[20], (FF, D), FF ** -0.5, 0.09375, ((0, 4), (1, 8)), jnp.float32)
    return {"tokens": tokens, "condition": condition, "cotangent": cotangent, "kept_index": kept_index, "skip_index": skip_index, "step_count": step_count, "ada_weight": ada_weight, "qkv_weight": qkv_weight, "proj_weight": proj_weight, "fc1_weight": fc1_weight, "fc2_weight": fc2_weight, "ada_moment": ada_moment, "qkv_moment": qkv_moment, "proj_moment": proj_moment, "fc1_moment": fc1_moment, "fc2_moment": fc2_moment, "ada_average": ada_average, "qkv_average": qkv_average, "proj_average": proj_average, "fc1_average": fc1_average, "fc2_average": fc2_average}


epsilon = 1e-06
best_precision = lax.Precision.HIGHEST
momentum_rate = 0.9

@jax.custom_vjp
def low(v):
    return lax.optimization_barrier(v.astype(jnp.bfloat16)).astype(jnp.float32)

@jax.custom_vjp
def low_back(v):
    return v

def low_keep(v):
    return (low(v), None)

def low_pass(kept, grad):
    return (grad,)

def back_keep(v):
    return (v, None)

def back_low(kept, grad):
    return (low(grad),)
low.defvjp(low_keep, low_pass)
low_back.defvjp(back_keep, back_low)

def layer_norm(values):
    centered = values - lax.optimization_barrier(jnp.mean(values, axis=-1, keepdims=True))
    return centered * lax.rsqrt(lax.optimization_barrier(jnp.mean(centered * centered, axis=-1, keepdims=True)) + epsilon)

def pick_rows(values, index):
    return jnp.take_along_axis(values, index[:, :, None].astype(jnp.int32), axis=1)

def place_rows(kept_rows, other_rows, kept_index, skip_index):
    images = kept_index.shape[0]
    batch = jnp.arange(images, dtype=jnp.int32)[:, None]
    blank = jnp.zeros((images, kept_index.shape[1] + skip_index.shape[1], kept_rows.shape[2]), jnp.float32)
    return blank.at[batch, kept_index].set(kept_rows).at[batch, skip_index].set(other_rows)

def forward_pass(tokens, condition, weights, kept_index, skip_index):
    ada_low = low(weights[0])
    qkv_low = low(weights[1])
    proj_low = low(weights[2])
    fc1_low = low(weights[3])
    fc2_low = low(weights[4])
    images = tokens.shape[0]
    kept_count = kept_index.shape[1]
    silu_cond = low(jax.nn.silu(condition))
    modulation = low_back(jnp.einsum('bd,dkf->bkf', silu_cond, ada_low, precision=best_precision))
    shift_one = modulation[:, 0, None, :]
    scale_one = modulation[:, 1, None, :]
    gate_one = modulation[:, 2, None, :]
    shift_two = modulation[:, 3, None, :]
    scale_two = modulation[:, 4, None, :]
    gate_two = modulation[:, 5, None, :]
    kept_rows = pick_rows(tokens, kept_index)
    hidden = low(layer_norm(kept_rows) * (1.0 + scale_one) + shift_one)
    projected = low_back(low(jnp.einsum('bnd,tdf->tbnf', hidden, qkv_low, precision=best_precision)))
    split_heads = projected.reshape(3, images, kept_count, HEADS, HEAD_DIM)
    scores = low_back(jnp.einsum('bqhe,bkhe->bhqk', split_heads[0], split_heads[1], precision=best_precision) * HEAD_DIM ** (-0.5))
    probs = low(jax.nn.softmax(scores, axis=-1))
    attended = jnp.einsum('bhqk,bkhe->bqhe', probs, split_heads[2], precision=best_precision).reshape(images, kept_count, D)
    attended = low_back(low(attended))
    attn_out = low_back(jnp.einsum('bnf,fd->bnd', attended, proj_low, precision=best_precision))
    residual = kept_rows + gate_one * attn_out
    hidden_two = low(layer_norm(residual) * (1.0 + scale_two) + shift_two)
    pre_act = low_back(jnp.einsum('bnd,df->bnf', hidden_two, fc1_low, precision=best_precision))
    activated = low(jax.nn.gelu(pre_act, approximate=True))
    mlp_out = low_back(jnp.einsum('bnf,fd->bnd', activated, fc2_low, precision=best_precision))
    kept_out = residual + gate_two * mlp_out
    return place_rows(kept_out, pick_rows(tokens, skip_index), kept_index, skip_index)

def reference(tokens, condition, cotangent, kept_index, skip_index, step_count, ada_weight, qkv_weight, proj_weight, fc1_weight, fc2_weight, ada_moment, qkv_moment, proj_moment, fc1_moment, fc2_moment, ada_average, qkv_average, proj_average, fc1_average, fc2_average):

    def wrapped(tok_float, cond_float, weight_tuple):
        return forward_pass(tok_float, cond_float, weight_tuple, kept_index, skip_index)
    weight_tuple = (ada_weight, qkv_weight, proj_weight, fc1_weight, fc2_weight)
    block_out, pull_back = jax.vjp(wrapped, tokens.astype(jnp.float32), condition.astype(jnp.float32), weight_tuple)
    tokens_grad, condition_grad, grads = pull_back(cotangent.astype(jnp.float32))
    rate = 0.02 / math.sqrt(IMAGES * KEPT)
    step_float = step_count.astype(jnp.float32)[0]
    decay = (1.0 + step_float) / (10.0 + step_float)
    moments = (ada_moment, qkv_moment, proj_moment, fc1_moment, fc2_moment)
    averages = (ada_average, qkv_average, proj_average, fc1_average, fc2_average)
    masters = []
    momenta = []
    emas = []
    for index in range(5):
        new_moment = momentum_rate * moments[index] + grads[index]
        master = weight_tuple[index] - rate * (grads[index] + momentum_rate * new_moment)
        masters.append(master)
        momenta.append(new_moment)
        emas.append(decay * averages[index] + (1.0 - decay) * master)
    return (block_out.astype(jnp.bfloat16), tokens_grad, condition_grad, masters[0], masters[1], masters[2], masters[3], masters[4], momenta[0], momenta[1], momenta[2], momenta[3], momenta[4], emas[0], emas[1], emas[2], emas[3], emas[4])
```

```python
from functools import partial
import math

import jax
import jax.numpy as jnp
from jax import lax
from jax.experimental import pallas as pl
from jax.experimental.pallas import tpu as pltpu
from jax.sharding import PartitionSpec as P

HEAD_DIM = 72

epsilon = 1e-06
momentum_rate = 0.9

f32 = jnp.float32
bf16 = jnp.bfloat16


def layer_norm(values):
    centered = values - jnp.mean(values, axis=-1, keepdims=True)
    inverse = lax.rsqrt(jnp.mean(centered * centered, axis=-1, keepdims=True) + epsilon)
    return (centered * inverse, inverse)


def norm_back(normed, inverse, gradient):
    return inverse * (
        gradient
        - jnp.mean(gradient, axis=-1, keepdims=True)
        - normed * jnp.mean(gradient * normed, axis=-1, keepdims=True)
    )


def swap_core(values):
    return lax.ppermute(values, "mp", [(j, j ^ 1) for j in range(4)])


def swap_x(values):
    return lax.ppermute(values, "mp", [(j, j ^ 2) for j in range(4)])


def join_pair(own, other, core, axis=0):
    return jnp.where(
        core == 0,
        jnp.concatenate([own, other], axis),
        jnp.concatenate([other, own], axis),
    )


def spread_pair(own, core):
    return join_pair(own, swap_core(own), core)


def swap_dp(values, bit):
    size = lax.axis_size("dp")
    return lax.ppermute(values, "dp", [(i, i ^ bit) for i in range(size)])


def dp_groups():
    size = lax.axis_size("dp")
    return [4] + [2] * (size.bit_length() - 3)


def spread_round(values, axis, level):
    groups = dp_groups()
    step = math.prod(groups[:level])
    others = [swap_dp(values, step * b) for b in range(1, groups[level])]
    return jnp.concatenate([values] + others, axis)


def sum_round(values, axis, level):
    groups = dp_groups()
    step = math.prod(groups[:level])
    blocks = jnp.split(values, groups[level], axis)
    total = blocks[0]
    for b in range(1, groups[level]):
        total = total + swap_dp(blocks[b], step * b)
    return total


def turn_round(values, level):
    groups = dp_groups()
    step = math.prod(groups[:level])
    shape = values.shape
    values = values.reshape((-1, groups[level], step) + shape[1:])
    blocks = [values[:, b] for b in range(groups[level])]
    blocks = [blocks[0]] + [swap_dp(blocks[b], step * b) for b in range(1, groups[level])]
    return jnp.stack(blocks, 1).reshape(shape)


def in_order(values):
    index = lax.axis_index("dp")
    shape = values.shape
    count = shape[0].bit_length() - 1
    values = values.reshape((2,) * count + shape[1:])
    for axis in range(count):
        values = jnp.where((index >> (count - 1 - axis)) & 1, jnp.flip(values, axis), values)
    return values.reshape(shape)


def ring_tables():
    cycle = [0, 2, 4, 6, 7, 5, 3, 1]
    clockwise = [(cycle[i], cycle[(i + 1) % 8]) for i in range(8)]
    return clockwise, [(b, a) for a, b in clockwise]


def ring_place_of(index):
    return jnp.where((index & 1) == 0, index >> 1, 7 - (index >> 1))


def ring_device(place):
    place = lax.rem(place, 8)
    return jnp.where(place < 4, 2 * place, 2 * (7 - place) + 1)


def hop(values, direction):
    clockwise, backward = ring_tables()
    return lax.ppermute(values, "dp", clockwise if direction > 0 else backward)


def ring_device_at(index, distance):
    return ring_device(ring_place_of(index) + distance + 8)


class Gather:
    def __init__(self, shard, lead):
        self.lead = lead
        self.steps = 0
        self.shard = shard
        self.ahead = [shard]
        self.behind = [shard]

    def start(self):
        self.steps += 1
        moving = [hop(self.ahead[-1], self.lead)]
        if len(self.behind) < 4:
            moving.append(hop(self.behind[-1], -self.lead))
        return tuple(moving)

    def finish(self, moved):
        self.ahead.append(moved[0])
        if len(moved) > 1:
            self.behind.append(moved[1])

    def pieces(self):
        rows = self.shard.shape[0]
        distances = [-self.lead * k for k in range(5)] + [self.lead * k for k in range(1, 4)]
        places = [
            partial(lambda distance, index: ring_device_at(index, distance) * rows, distance)
            for distance in distances
        ]
        return self.ahead + self.behind[1:], places


class Scatter:
    def __init__(self, part, lead):
        self.part, self.lead = part, lead
        self.rows = part.shape[0] // 8
        self.steps = 0
        self.ahead = self.block(4 * lead)
        self.behind = self.block(-3 * lead)

    def block(self, distance):
        at = ring_device_at(lax.axis_index("dp"), distance)
        return lax.dynamic_slice_in_dim(self.part, at * self.rows, self.rows, 0)

    def add(self, moved, distance):
        return (moved.astype(f32) + self.block(distance).astype(f32)).astype(bf16)

    def start(self):
        if self.steps > 0:
            self.ahead = self.add(self.ahead, self.lead * (4 - self.steps))
            if self.steps < 3:
                self.behind = self.add(self.behind, -self.lead * (3 - self.steps))
        self.steps += 1
        ahead = hop(self.ahead, self.lead)
        if self.steps == 4:
            return (ahead, self.behind)
        return (ahead, hop(self.behind, -self.lead))

    def finish(self, moved):
        self.ahead, self.behind = moved

    def total(self):
        total = self.ahead.astype(f32) + self.behind.astype(f32)
        return total + self.block(0).astype(f32)


def gather_plain(shard):
    return lax.all_gather(shard, "dp", axis=0, tiled=True)


def scatter_plain(part):
    return lax.psum_scatter(part.astype(f32), "dp", scatter_dimension=0, tiled=True)


stage = lax.optimization_barrier


def run(kernel, name, outs, *args):
    vmem = pl.BlockSpec(memory_space=pltpu.VMEM)
    return pl.pallas_call(
        kernel,
        out_shape=[jax.ShapeDtypeStruct(shape, dtype) for shape, dtype in outs],
        in_specs=[vmem] * len(args),
        out_specs=[vmem] * len(outs),
        cost_estimate=pl.CostEstimate(flops=0, bytes_accessed=1024, transcendentals=0),
        name=name,
    )(*args)


def dot(a, b):
    return jnp.dot(a, b, preferred_element_type=f32)


def dot_last(a, b):
    return lax.dot_general(a, b, (((1,), (1,)), ((), ())), preferred_element_type=f32)


def dot_first(a, b):
    return lax.dot_general(a, b, (((0,), (0,)), ((), ())), preferred_element_type=f32)


def core_here():
    return lax.axis_index("mp") & 1


def pair_rows(total, pair):
    half = total // 2
    return pl.ds(pl.multiple_of(pair * half, half), half)


def tiles(total):
    return total // 384 if total % 384 == 0 else 1


def place_pieces(pieces, places, out):
    for piece, place in zip(pieces, places):
        rows = piece.shape[0]
        if place is None:
            out[...] = piece[...]
        else:
            start = pl.multiple_of(place(lax.axis_index("dp")), 8)
            out[pl.ds(start, rows), :] = piece[...]


def kernel_attention(places, heads, *refs):
    count = len(places)
    pieces, (kept, mods) = refs[:count], refs[count : count + 2]
    full, hidden, projected, attended, own, other = refs[count + 2 :]
    place_pieces(pieces, places, full)
    images = mods.shape[1]
    rows = kept.shape[0] // images
    local = attended.shape[1]
    depth = local // heads
    core = core_here()

    def norm(image, carry):
        at = pl.ds(pl.multiple_of(image * rows, rows), rows)
        normed, _ = layer_norm(kept[at, :].astype(f32))
        scale = mods[1, pl.ds(image, 1), :]
        hidden[at, :] = (normed * (1.0 + scale) + mods[0, pl.ds(image, 1), :]).astype(bf16)
        return carry

    lax.fori_loop(0, images, norm, 0)
    weights = full[:, : 3 * local]

    def project(pair, carry):
        at = pair_rows(kept.shape[0], pair)
        projected[at, :] = dot(hidden[at, :], weights).astype(bf16)
        return carry

    lax.fori_loop(0, 2, project, 0)

    def attend(image, carry):
        at = pl.ds(pl.multiple_of(image * rows, rows), rows)
        values = projected[at, :]
        outs = []
        for head in range(heads):
            query, key, value = [
                values[:, t * local + head * depth : t * local + (head + 1) * depth]
                for t in range(3)
            ]
            probs = head_probs(query, key, depth)
            outs.append(dot(probs.astype(bf16), value).astype(bf16))
        attended[at, :] = jnp.concatenate(outs, 1)
        return carry

    lax.fori_loop(0, images, attend, 0)
    weights = full[:, 3 * local :]
    other[...] = dot_last(attended[pair_rows(kept.shape[0], 1 - core), :], weights).astype(bf16)
    own[...] = dot_last(attended[pair_rows(kept.shape[0], core), :], weights)


def head_probs(query, key, depth):
    scores = dot_last(query, key) * depth ** (-0.5)
    exp_scores = jnp.exp(scores - jnp.max(scores, axis=-1, keepdims=True))
    return exp_scores / jnp.sum(exp_scores, axis=-1, keepdims=True)


def kernel_second_norm(kept, mods, own, moved, residual, hidden_two):
    core = core_here()
    half = mods.shape[1] // 2
    rows = residual.shape[0] // half
    for image in range(half):
        at = slice(image * rows, (image + 1) * rows)
        where = core * half + image
        row = pl.ds(pl.multiple_of(where * rows, rows), rows)
        gate, shift, scale = [mods[k, pl.ds(where, 1), :] for k in (2, 3, 4)]
        attn_out = own[at, :].astype(f32) + moved[at, :].astype(f32)
        values = kept[row, :].astype(f32) + gate * attn_out
        residual[at, :] = values
        normed, _ = layer_norm(values)
        hidden_two[at, :] = (normed * (1.0 + scale) + shift).astype(bf16)


gelu_rate = math.sqrt(2.0 / math.pi)


def gelu_parts(values):
    tanh = jnp.tanh(gelu_rate * (values + 0.044715 * (values * values * values)))
    return 0.5 * (1.0 + tanh), tanh


def kernel_feed_forward(places, *refs):
    count = len(places)
    pieces, (here, there, grad, mods) = refs[:count], refs[count : count + 4]
    full, hidden_two, pre_act, activated, mlp_grad, fc2_grad = refs[count + 4 :]
    place_pieces(pieces, places, full)
    core = core_here()
    total = hidden_two.shape[0]
    hidden_two[pair_rows(total, core), :] = here[...]
    hidden_two[pair_rows(total, 1 - core), :] = there[...]
    images = mods.shape[1]
    rows = total // images

    def scale_grad(image, carry):
        at = pl.ds(pl.multiple_of(image * rows, rows), rows)
        gate = mods[5, pl.ds(image, 1), :]
        mlp_grad[at, :] = (gate * grad[at, :].astype(f32)).astype(bf16)
        return carry

    lax.fori_loop(0, images, scale_grad, 0)
    columns = full.shape[1]
    width = columns // tiles(columns)

    def product(tile, carry):
        at = pl.ds(pl.multiple_of(tile * width, width), width)
        values = dot(hidden_two[...], full[:, at])
        pre_act[:, at] = values
        low = (values * gelu_parts(values)[0]).astype(bf16)
        activated[:, at] = low
        fc2_grad[:, at] = dot_first(mlp_grad[...], low).astype(bf16)
        return carry

    lax.fori_loop(0, tiles(columns), product, 0)


def kernel_feed_back(places, *refs):
    count = len(places)
    pieces, (mlp_grad, pre_act, fc1_full) = refs[:count], refs[count : count + 3]
    full, pre_grad, own, other = refs[count + 3 :]
    place_pieces(pieces, places, full)
    core = core_here()
    columns = full.shape[1]
    width = columns // tiles(columns)

    def product(tile, carry):
        at = pl.ds(pl.multiple_of(tile * width, width), width)
        values = pre_act[:, at]
        half, tanh = gelu_parts(values)
        slope = half + 0.5 * values * (1.0 - tanh * tanh) * gelu_rate * (
            1.0 + 3.0 * 0.044715 * (values * values)
        )
        pre_grad[:, at] = (dot(mlp_grad[...], full[:, at]) * slope).astype(bf16)
        return carry

    lax.fori_loop(0, tiles(columns), product, 0)
    total, depth = pre_grad.shape[0], fc1_full.shape[0]
    width = depth // tiles(depth)

    def back(tile, carry):
        at = pl.ds(pl.multiple_of(tile * width, width), width)
        weights = fc1_full[at, :]
        other[:, at] = dot_last(pre_grad[pair_rows(total, 1 - core), :], weights).astype(bf16)
        own[:, at] = dot_last(pre_grad[pair_rows(total, core), :], weights)
        return carry

    lax.fori_loop(0, tiles(depth), back, 0)


def kernel_second_back(
    own, moved, residual, attn_own, attn_moved, grad, mods, residual_grad, attn_grad, sums
):
    core = core_here()
    half = mods.shape[1] // 2
    rows = residual.shape[0] // half
    for image in range(half):
        at = slice(image * rows, (image + 1) * rows)
        where = core * half + image
        row = pl.ds(pl.multiple_of(where * rows, rows), rows)
        gate, scale = [mods[k, pl.ds(where, 1), :] for k in (2, 4)]
        normed, inverse = layer_norm(residual[at, :])
        gradient = own[at, :].astype(f32) + moved[at, :].astype(f32)
        sums[1, pl.ds(image, 1), :] = jnp.sum(gradient, axis=0, keepdims=True)
        sums[2, pl.ds(image, 1), :] = jnp.sum(gradient * normed, axis=0, keepdims=True)
        values = grad[row, :].astype(f32) + norm_back(normed, inverse, gradient * (1.0 + scale))
        residual_grad[at, :] = values
        attn_out = attn_own[at, :].astype(f32) + attn_moved[at, :].astype(f32)
        sums[0, pl.ds(image, 1), :] = jnp.sum(values * attn_out, axis=0, keepdims=True)
        attn_grad[at, :] = (gate * values).astype(bf16)


def kernel_attention_back(
    heads, rows, here, there, full, projected, attended, hidden, attn_grad, own, other, out_grad, grads
):
    core = core_here()
    total = out_grad.shape[0]
    local = attended.shape[1]
    depth = local // heads
    out_grad[pair_rows(total, core), :] = here[...]
    out_grad[pair_rows(total, 1 - core), :] = there[...]
    back = dot(out_grad[...], full[:, 3 * local :]).astype(bf16)
    attn_grad[:, 3 * local :] = dot_first(out_grad[...], attended[...]).astype(bf16)
    for image in range(total // rows):
        at = slice(image * rows, (image + 1) * rows)
        values = projected[at, :]
        parts = [[], [], []]
        for head in range(heads):
            query, key, value = [
                values[:, t * local + head * depth : t * local + (head + 1) * depth]
                for t in range(3)
            ]
            gradient = back[at, head * depth : (head + 1) * depth]
            probs = head_probs(query, key, depth)
            prob_grad = dot_last(gradient, value)
            score_grad = (
                probs * (prob_grad - jnp.sum(prob_grad * probs, axis=-1, keepdims=True))
            ).astype(bf16)
            parts[0].append((dot(score_grad, key) * depth ** (-0.5)).astype(bf16))
            parts[1].append((dot_first(score_grad, query) * depth ** (-0.5)).astype(bf16))
            parts[2].append(dot_first(probs.astype(bf16), gradient).astype(bf16))
        grads[at, :] = jnp.concatenate(parts[0] + parts[1] + parts[2], 1)
    weights = full[:, : 3 * local]
    other[...] = dot_last(grads[pair_rows(total, 1 - core), :], weights).astype(bf16)
    own[...] = dot_last(grads[pair_rows(total, core), :], weights)
    attn_grad[:, : 3 * local] = dot_first(hidden[...], grads[...]).astype(bf16)


def kernel_output(own, moved, residual, grad, mods, kept_out, sums):
    core = core_here()
    half = mods.shape[1] // 2
    rows = residual.shape[0] // half
    for image in range(half):
        at = slice(image * rows, (image + 1) * rows)
        where = core * half + image
        row = pl.ds(pl.multiple_of(where * rows, rows), rows)
        mlp_out = own[at, :].astype(f32) + moved[at, :].astype(f32)
        gate = mods[5, pl.ds(where, 1), :]
        kept_out[at, :] = (residual[at, :] + gate * mlp_out).astype(bf16)
        sums[pl.ds(image, 1), :] = jnp.sum(
            grad[row, :].astype(f32) * mlp_out, axis=0, keepdims=True
        )


def kernel_first_back(
    own, moved, residual_grad, kept, mods, late, last, kept_grad, mine, partner
):
    me = lax.axis_index("mp")
    core = me & 1
    half = mods.shape[1] // 2
    rows = residual_grad.shape[0] // half
    local = mine.shape[2]
    lines = [[], []]
    for image in range(half):
        at = slice(image * rows, (image + 1) * rows)
        where = core * half + image
        row = pl.ds(pl.multiple_of(where * rows, rows), rows)
        normed, inverse = layer_norm(kept[row, :].astype(f32))
        gradient = own[at, :].astype(f32) + moved[at, :].astype(f32)
        lines[0].append(jnp.sum(gradient, axis=0, keepdims=True))
        lines[1].append(jnp.sum(gradient * normed, axis=0, keepdims=True))
        scale = mods[1, pl.ds(where, 1), :]
        values = residual_grad[at, :] + norm_back(normed, inverse, gradient * (1.0 + scale))
        kept_grad[at, :] = values.astype(bf16)
    planes = [jnp.concatenate(line, 0) for line in lines]
    planes += [late[0], late[1], late[2], last[...]]
    for k, plane in enumerate(planes):
        blocks = [plane[:, j * local : (j + 1) * local] for j in range(4)]
        for out, device in ((mine, me), (partner, me ^ 1)):
            chosen = blocks[0]
            for j in range(1, 4):
                chosen = jnp.where(device == j, blocks[j], chosen)
            out[k] = chosen.astype(bf16)


def new_state(weight, moment, average, gradient, rate, steps):
    decay = (1.0 + steps) / (10.0 + steps)
    new_moment = momentum_rate * moment + gradient
    master = weight - rate * (gradient + momentum_rate * new_moment)
    return master, new_moment, decay * average + (1.0 - decay) * master


def attention_step(rate, steps, gradient, *refs):
    counts = steps[0].astype(f32)
    qkv, proj, qkv_out, proj_out = refs[:3], refs[3:6], refs[6:9], refs[9:]
    local = proj[0].shape[1]
    for t in range(3):
        values = new_state(
            *[ref[t] for ref in qkv], gradient[:, t * local : (t + 1) * local], rate, counts
        )
        for ref, value in zip(qkv_out, values):
            ref[t] = value
    values = new_state(*[ref[...] for ref in proj], gradient[:, 3 * local :], rate, counts)
    for ref, value in zip(proj_out, values):
        ref[...] = value


def step_attention(qkv, proj, gradient, rate, steps):
    whole = pl.BlockSpec(memory_space=pltpu.VMEM)
    size = qkv[0].size + proj[0].size
    return pl.pallas_call(
        partial(attention_step, rate),
        out_shape=[jax.ShapeDtypeStruct(x.shape, f32) for x in qkv + proj],
        in_specs=[pl.BlockSpec(memory_space=pltpu.SMEM)] + [whole] * 7,
        out_specs=[whole] * 6,
        cost_estimate=pl.CostEstimate(
            flops=10 * size, bytes_accessed=28 * size, transcendentals=0
        ),
        name="step_attention",
    )(steps, gradient, *qkv, *proj)


def ada_step(rate, steps, cond, mods, weight, moment, average, master, new_moment, ema):
    counts = steps[0].astype(f32)
    gradient = lax.dot_general(
        cond[...], mods[0], (((0,), (0,)), ((), ())), preferred_element_type=f32
    )
    values = new_state(weight[0], moment[0], average[0], gradient, rate, counts)
    master[0], new_moment[0], ema[0] = values


def step_ada(weight, moment, average, cond, mods, rate, steps):
    count, rows, columns = weight.shape
    spec = pl.BlockSpec((1, rows, columns), lambda k: (k, 0, 0))
    return pl.pallas_call(
        partial(ada_step, rate),
        grid=(count,),
        out_shape=[jax.ShapeDtypeStruct(weight.shape, f32)] * 3,
        in_specs=[
            pl.BlockSpec(memory_space=pltpu.SMEM),
            pl.BlockSpec(cond.shape, lambda k: (0, 0)),
            pl.BlockSpec((1,) + mods.shape[1:], lambda k: (k, 0, 0)),
        ]
        + [spec] * 3,
        out_specs=[spec] * 3,
        cost_estimate=pl.CostEstimate(
            flops=2 * weight.size * cond.shape[0], bytes_accessed=28 * weight.size, transcendentals=0
        ),
        name="step_ada",
    )(steps, cond, mods, weight, moment, average)


def per_device(
    tokens,
    condition,
    cotangent,
    kept_index,
    skip_index,
    step_count,
    ada_weight,
    qkv_weight,
    proj_weight,
    fc1_weight,
    fc2_weight,
    ada_moment,
    qkv_moment,
    proj_moment,
    fc1_moment,
    fc2_moment,
    ada_average,
    qkv_average,
    proj_average,
    fc1_average,
    fc2_average,
):
    images, seq, width = tokens.shape
    kept_count = kept_index.shape[1]
    own_d = ada_weight.shape[0]
    mods = ada_weight.shape[1]
    local = ada_weight.shape[2]
    local_heads = local // HEAD_DIM
    core = lax.axis_index("mp") % 2
    chip = lax.axis_index("mp") // 2
    dp_size = lax.axis_size("dp")
    index = lax.axis_index("dp")

    ring = dp_size == 8
    rings = []

    def tick(extras):
        active = [one for one in rings if one.steps < 4]
        moving = tuple(one.start() for one in active)
        held, moved = stage((tuple(extras()), moving))
        for one, values in zip(active, moved):
            one.finish(values)
        return held

    positions = lax.broadcasted_iota(jnp.int32, (images, seq, kept_count), 1)
    select = (kept_index[:, None, :] == positions).astype(bf16)
    is_kept = jnp.any(kept_index[:, None, :] == positions, axis=2)[:, :, None]

    def kept_of(values):
        picked = jnp.einsum("bsi,bsd->bid", select, values, preferred_element_type=f32)
        return picked.astype(bf16).reshape(images * kept_count, width)

    attn_low = jnp.concatenate(
        [qkv_weight[0], qkv_weight[1], qkv_weight[2], proj_weight.T], 1
    ).astype(bf16)
    fc1_low = fc1_weight.astype(bf16)
    fc2_low = fc2_weight.T.astype(bf16)
    ada_low = jnp.moveaxis(ada_weight.astype(bf16), 1, 0)
    cond_float = condition.astype(f32)
    silu_cond = jax.nn.silu(cond_float).astype(bf16)
    small = silu_cond.reshape(images, dp_size, own_d)
    levels = len(dp_groups())
    if ring:
        attn_ring, fc1_ring, fc2_ring = Gather(attn_low, 1), Gather(fc1_low, 1), Gather(fc2_low, -1)
        rings = [attn_ring]

    (small,) = tick(lambda: (spread_round(small, 0, 0),))

    def rest_of_cond():
        values = small
        for level in range(1, levels):
            values = spread_round(values, 0, level)
        own = lax.dynamic_index_in_dim(values, index, 1, keepdims=False)
        part = jnp.einsum("bd,kdf->kbf", own, ada_low, preferred_element_type=f32)
        return own, part, kept_of(tokens)

    cond_own, small, kept_low = tick(rest_of_cond)

    def sum_of_mods():
        values = small
        for level in reversed(range(1, levels)):
            values = sum_round(values, 1, level)
        return (values,)

    (small,) = tick(sum_of_mods)
    (mod_local,) = tick(lambda: (sum_round(small, 1, 0),))
    if ring:
        rings = [fc1_ring]
        attn_pieces, attn_places = attn_ring.pieces()
    else:
        attn_pieces, attn_places = [gather_plain(attn_low)], [None]
        fc1_pieces, fc1_places = [gather_plain(fc1_low)], [None]
        fc2_pieces, fc2_places = [gather_plain(fc2_low)], [None]

    def all_mods():
        at_core = swap_core(mod_local)
        at_x = swap_x(mod_local)
        at_both = lax.ppermute(mod_local, "mp", [(j, j ^ 3) for j in range(4)])
        pairs = [join_pair(mod_local, at_core, core, 2), join_pair(at_x, at_both, core, 2)]
        return (
            jnp.where(chip == 0, jnp.concatenate(pairs, 2), jnp.concatenate(pairs[::-1], 2)),
        )

    (modulation,) = tick(all_mods)
    total = images * kept_count
    half = total // 2

    def attention():
        return run(
            partial(kernel_attention, attn_places, local_heads),
            "attention",
            [
                ((width, attn_low.shape[1]), bf16),
                ((total, width), bf16),
                ((total, 3 * local), bf16),
                ((total, local), bf16),
                ((half, width), f32),
                ((half, width), bf16),
            ],
            *attn_pieces,
            kept_low,
            modulation,
        )

    attn_full, hidden, projected, attended, own_part, other_part = tick(attention)
    (other_part, grad_low) = tick(lambda: (swap_core(other_part), kept_of(cotangent)))

    def add_low(own, other):
        return (own + other.astype(f32)).astype(bf16)

    attn_own = add_low(own_part, other_part)
    (x_one, attn_own) = tick(lambda: (swap_x(attn_own[: half // 2]), attn_own))
    if ring:
        rings = [fc2_ring]
        fc1_pieces, fc1_places = fc1_ring.pieces()
    (x_two,) = tick(lambda: (swap_x(attn_own[half // 2 :]),))
    attn_moved = jnp.concatenate([x_one, x_two], 0)

    def second_norm():
        values, low = run(
            kernel_second_norm,
            "second_norm",
            [((half, width), f32), ((half, width), bf16)],
            kept_low,
            modulation,
            attn_own,
            attn_moved,
        )
        return values, low, swap_core(low), attn_moved

    residual, hidden_here, hidden_there, attn_moved = tick(second_norm)

    def feed_forward():
        hidden_units = fc1_low.shape[1]
        return run(
            partial(kernel_feed_forward, fc1_places),
            "feed_forward",
            [
                ((width, hidden_units), bf16),
                ((total, width), bf16),
                ((total, hidden_units), f32),
                ((total, hidden_units), bf16),
                ((total, width), bf16),
                ((width, hidden_units), bf16),
            ],
            *fc1_pieces,
            hidden_here,
            hidden_there,
            grad_low,
            modulation,
        )

    fc1_full, hidden_two, pre_act, activated, mlp_grad, fc2_grad = tick(feed_forward)
    if ring:
        fc2_sums = Scatter(fc2_grad, -1)
        rings = [fc2_ring, fc2_sums]
        tick(lambda: ())
        fc2_pieces, fc2_places = fc2_ring.pieces()
        rings = [fc2_sums]

    def feed_back():
        return run(
            partial(kernel_feed_back, fc2_places),
            "feed_back",
            [
                ((width, fc2_low.shape[1]), bf16),
                (pre_act.shape, bf16),
                ((half, width), f32),
                ((half, width), bf16),
            ],
            *fc2_pieces,
            mlp_grad,
            pre_act,
            fc1_full,
        )

    fc2_full, pre_grad, own_part, other_part = tick(feed_back)

    def fc1_product():
        grad = dot_first(hidden_two, pre_grad)
        return swap_core(other_part), grad.astype(bf16)

    other_part, fc1_grad = tick(fc1_product)
    if ring:
        fc1_sums = Scatter(fc1_grad, 1)
        rings = [fc2_sums, fc1_sums]
    hidden_own = add_low(own_part, other_part)

    def tick_one():
        part = dot_last(activated, fc2_full)
        return swap_x(hidden_own), part, hidden_own

    hidden_moved, mlp_part, hidden_own = tick(tick_one)

    def tick_two():
        values, low, sums = run(
            kernel_second_back,
            "second_back",
            [((half, width), f32), ((half, width), bf16), ((3, images // 2, width), f32)],
            hidden_own,
            hidden_moved,
            residual,
            attn_own,
            attn_moved,
            grad_low,
            modulation,
        )
        mlp_own = lax.dynamic_slice_in_dim(mlp_part, core * half, half, 0)
        mlp_other = lax.dynamic_slice_in_dim(mlp_part, (1 - core) * half, half, 0)
        return values, low, swap_core(low), sums, mlp_own, swap_core(mlp_other.astype(bf16))

    residual_grad, out_here, out_there, late_mods, own_mlp, other_mlp = tick(tick_two)
    mlp_own = add_low(own_mlp, other_mlp)

    def tick_three():
        back = pl.pallas_call(
            partial(kernel_attention_back, local_heads, kept_count),
            out_shape=[
                jax.ShapeDtypeStruct(attn_full.shape, bf16),
                jax.ShapeDtypeStruct((half, width), f32),
                jax.ShapeDtypeStruct((half, width), bf16),
            ],
            in_specs=[pl.BlockSpec(memory_space=pltpu.VMEM)] * 6,
            out_specs=[pl.BlockSpec(memory_space=pltpu.VMEM)] * 3,
            scratch_shapes=[
                pltpu.VMEM((total, width), bf16),
                pltpu.VMEM((total, 3 * local), bf16),
            ],
            cost_estimate=pl.CostEstimate(flops=0, bytes_accessed=1024, transcendentals=0),
            name="attention_back",
        )(out_here, out_there, attn_full, projected, attended, hidden)
        return *back, swap_x(mlp_own), mlp_own

    attn_grad, own_part, other_part, mlp_moved, mlp_own = tick(tick_three)
    if ring:
        attn_sums = Scatter(attn_grad, 1)
        rings = [fc1_sums, attn_sums]

    def tick_three_more():
        kept_out, last = run(
            kernel_output,
            "output",
            [((half, width), bf16), ((images // 2, width), f32)],
            mlp_own,
            mlp_moved,
            residual,
            grad_low,
            modulation,
        )
        return kept_out, last

    def tick_four():
        own = add_low(own_part, swap_core(other_part))
        return swap_x(own), own, *tick_three_more()

    x_part, own_part, kept_out, last_mods = tick(tick_four)
    if ring:
        rings = [attn_sums]
        fc1_shard, fc2_shard = fc1_sums.total(), fc2_sums.total()
    else:
        fc1_shard, fc2_shard = scatter_plain(fc1_grad), scatter_plain(fc2_grad)

    def tick_five():
        kept_grad, mine, partner = run(
            kernel_first_back,
            "first_back",
            [
                ((half, width), bf16),
                ((mods, images // 2, local), bf16),
                ((mods, images // 2, local), bf16),
            ],
            own_part,
            x_part,
            residual_grad,
            kept_low,
            modulation,
            late_mods,
            last_mods,
        )
        mod_pair = join_pair(mine, swap_core(partner), core, 1)
        return mod_pair, spread_pair(kept_grad, core), spread_pair(kept_out, core)

    small, kept_grad, kept_out = tick(tick_five)
    kept_grad, kept_out = [x.reshape(images, kept_count, width) for x in (kept_grad, kept_out)]

    rate = 0.02 / math.sqrt(images * dp_size * kept_count)
    def tick_six():
        placed = jnp.einsum("bsi,bid->bsd", select, kept_grad, preferred_element_type=f32)
        out = jnp.where(is_kept, placed, cotangent.astype(f32))
        values = spread_round(small, 1, 0)
        return out, values, *new_state(
            fc2_weight.T,
            fc2_moment.T,
            fc2_average.T,
            fc2_shard,
            rate,
            step_count[0].astype(f32),
        )

    tokens_grad, small, fc2_master, fc2_momentum, fc2_ema = tick(tick_six)

    def tick_seven():
        values = small
        for level in range(1, levels):
            values = spread_round(values, 1, level)
        placed = jnp.einsum("bsi,bid->bsd", select, kept_out, preferred_element_type=f32)
        out = jnp.where(is_kept, placed.astype(bf16), tokens)
        return out, values, *new_state(
            fc1_weight,
            fc1_moment,
            fc1_average,
            fc1_shard,
            rate,
            step_count[0].astype(f32),
        )

    block_out, mod_grad_all, fc1_master, fc1_momentum, fc1_ema = tick(tick_seven)
    attn_shard = attn_sums.total() if ring else scatter_plain(attn_grad)
    silu_part = jnp.einsum("kbf,kdf->bd", mod_grad_all, ada_low, preferred_element_type=f32)
    silu_part = silu_part + swap_core(silu_part)
    silu_part = silu_part + swap_x(silu_part)
    ada_state = [jnp.moveaxis(x, 1, 0) for x in (ada_weight, ada_moment, ada_average)]
    ada_new = step_ada(*ada_state, cond_own, mod_grad_all, rate, step_count)
    ada_master, ada_momentum, ada_ema = [jnp.moveaxis(x, 0, 1) for x in ada_new]
    silu_blocks = silu_part.reshape(dp_size, images, own_d)
    for level in reversed(range(levels)):
        silu_blocks = turn_round(silu_blocks, level)
    silu_blocks = in_order(silu_blocks)
    silu_grad = jnp.moveaxis(silu_blocks, 0, 1).reshape(images, width)
    silu_value, silu_pull = jax.vjp(jax.nn.silu, cond_float)
    condition_grad = silu_pull(silu_grad)[0]

    qkv_master, qkv_momentum, qkv_ema, proj_master, proj_momentum, proj_ema = step_attention(
        (qkv_weight, qkv_moment, qkv_average),
        (proj_weight.T, proj_moment.T, proj_average.T),
        attn_shard,
        rate,
        step_count,
    )
    return (
        block_out,
        tokens_grad,
        condition_grad,
        ada_master,
        qkv_master,
        proj_master.T,
        fc1_master,
        fc2_master.T,
        ada_momentum,
        qkv_momentum,
        proj_momentum.T,
        fc1_momentum,
        fc2_momentum.T,
        ada_ema,
        qkv_ema,
        proj_ema.T,
        fc1_ema,
        fc2_ema.T,
    )


def solution(mesh):
    weights = (
        P("dp", None, "mp"),
        P(None, "dp", "mp"),
        P("mp", "dp"),
        P("dp", "mp"),
        P("mp", "dp"),
    )
    rows = P("dp", None, None)
    pairs = P("dp", None)
    return jax.shard_map(
        per_device,
        mesh=mesh,
        in_specs=(rows, pairs, rows, pairs, pairs, P()) + weights * 3,
        out_specs=(rows, rows, pairs) + weights * 3,
        check_vma=False,
    )
```

```python
from functools import partial
import math

import jax
import jax.numpy as jnp
from jax import lax
from jax.experimental import pallas as pl
from jax.experimental.pallas import tpu as pltpu
from jax.sharding import PartitionSpec as P

HEAD_DIM = 72

epsilon = 1e-06
momentum_rate = 0.9

f32 = jnp.float32
bf16 = jnp.bfloat16


def layer_norm(values):
    centered = values - jnp.mean(values, axis=-1, keepdims=True)
    inverse = lax.rsqrt(jnp.mean(centered * centered, axis=-1, keepdims=True) + epsilon)
    return (centered * inverse, inverse)


def norm_back(normed, inverse, gradient):
    return inverse * (
        gradient
        - jnp.mean(gradient, axis=-1, keepdims=True)
        - normed * jnp.mean(gradient * normed, axis=-1, keepdims=True)
    )


def swap_core(values):
    return lax.ppermute(values, "mp", [(j, j ^ 1) for j in range(4)])


def swap_x(values):
    return lax.ppermute(values, "mp", [(j, j ^ 2) for j in range(4)])


def join_pair(own, other, core, axis=0):
    return jnp.where(
        core == 0,
        jnp.concatenate([own, other], axis),
        jnp.concatenate([other, own], axis),
    )


def spread_pair(own, core):
    return join_pair(own, swap_core(own), core)


def swap_dp(values, bit):
    size = lax.axis_size("dp")
    return lax.ppermute(values, "dp", [(i, i ^ bit) for i in range(size)])


def dp_groups():
    size = lax.axis_size("dp")
    return [4] + [2] * (size.bit_length() - 3)


def spread_round(values, axis, level):
    groups = dp_groups()
    step = math.prod(groups[:level])
    others = [swap_dp(values, step * b) for b in range(1, groups[level])]
    return jnp.concatenate([values] + others, axis)


def sum_round(values, axis, level):
    groups = dp_groups()
    step = math.prod(groups[:level])
    blocks = jnp.split(values, groups[level], axis)
    total = blocks[0]
    for b in range(1, groups[level]):
        total = total + swap_dp(blocks[b], step * b)
    return total


def turn_round(values, level):
    groups = dp_groups()
    step = math.prod(groups[:level])
    shape = values.shape
    values = values.reshape((-1, groups[level], step) + shape[1:])
    blocks = [values[:, b] for b in range(groups[level])]
    blocks = [blocks[0]] + [swap_dp(blocks[b], step * b) for b in range(1, groups[level])]
    return jnp.stack(blocks, 1).reshape(shape)


def in_order(values):
    index = lax.axis_index("dp")
    shape = values.shape
    count = shape[0].bit_length() - 1
    values = values.reshape((2,) * count + shape[1:])
    for axis in range(count):
        values = jnp.where((index >> (count - 1 - axis)) & 1, jnp.flip(values, axis), values)
    return values.reshape(shape)


def ring_tables():
    cycle = [0, 2, 4, 6, 7, 5, 3, 1]
    clockwise = [(cycle[i], cycle[(i + 1) % 8]) for i in range(8)]
    return clockwise, [(b, a) for a, b in clockwise]


def ring_place_of(index):
    return jnp.where((index & 1) == 0, index >> 1, 7 - (index >> 1))


def ring_device(place):
    place = lax.rem(place, 8)
    return jnp.where(place < 4, 2 * place, 2 * (7 - place) + 1)


def hop(values, direction):
    clockwise, backward = ring_tables()
    return lax.ppermute(values, "dp", clockwise if direction > 0 else backward)


def ring_device_at(index, distance):
    return ring_device(ring_place_of(index) + distance + 8)


class Gather:
    def __init__(self, shard, lead):
        self.lead = lead
        self.shard = shard
        self.ahead = [shard]
        self.behind = [shard]

    def start(self, sides):
        moving = []
        if "a" in sides:
            moving.append(hop(self.ahead[-1], self.lead))
        if "b" in sides:
            moving.append(hop(self.behind[-1], -self.lead))
        return tuple(moving)

    def finish(self, sides, moved):
        moved = list(moved)
        if "a" in sides:
            self.ahead.append(moved.pop(0))
        if "b" in sides:
            self.behind.append(moved.pop(0))

    def pieces(self):
        rows = self.shard.shape[0]
        distances = [-self.lead * k for k in range(5)] + [self.lead * k for k in range(1, 4)]
        places = [
            partial(lambda distance, index: ring_device_at(index, distance) * rows, distance)
            for distance in distances
        ]
        return self.ahead + self.behind[1:], places


class Scatter:
    def __init__(self, part, lead, first):
        self.part, self.lead = part, lead
        self.rows = part.shape[0] // 8
        self.left = {"a": 4, "b": 3}
        self.added = {"a": False, "b": False}
        self.held = dict(zip("ab", first))

    def signs(self):
        return {"a": self.lead, "b": -self.lead}

    def add(self, values):
        full = {"a": 4, "b": 3}
        adding = [k for k in values if 0 < self.left[k] < full[k] and not self.added[k]]
        if adding:
            signs = self.signs()
            sums = add_blocks(
                self.part,
                [values[k] for k in adding],
                [signs[k] * self.left[k] for k in adding],
            )
            values = {**values, **dict(zip(adding, sums))}
            for k in adding:
                self.added[k] = True
        return values

    def prepare(self, sides):
        values = self.add({k: self.held[k] for k in sides})
        return tuple(values[k] for k in sides)

    def start(self, sides):
        values = self.add({k: self.held[k] for k in sides if k in "ab"})
        signs = self.signs()
        for k in values:
            self.left[k] -= 1
            self.added[k] = False
        values = {k: hop(value, signs[k]) for k, value in values.items()}
        if "+" in sides:
            values = self.add(values)
        return tuple(values.values())

    def finish(self, sides, moved):
        self.held.update(zip(sides, moved))

    def total(self):
        at = ring_device_at(lax.axis_index("dp"), 0)
        block = lax.dynamic_slice_in_dim(self.part, at * self.rows, self.rows, 0)
        return self.held["a"].astype(f32) + self.held["b"].astype(f32) + block.astype(f32)


def gather_plain(shard):
    return lax.all_gather(shard, "dp", axis=0, tiled=True)


def scatter_plain(part):
    return lax.psum_scatter(part.astype(f32), "dp", scatter_dimension=0, tiled=True)


stage = lax.optimization_barrier


def run(kernel, name, outs, args, scratch=None):
    vmem = pl.BlockSpec(memory_space=pltpu.VMEM)
    anywhere = pl.BlockSpec(memory_space=pl.ANY)
    by_copy = scratch is not None
    return pl.pallas_call(
        kernel,
        out_shape=[jax.ShapeDtypeStruct(shape, dtype) for shape, dtype in outs],
        in_specs=[vmem if not by_copy or x.size < 40000 else anywhere for x in args],
        out_specs=[anywhere if by_copy else vmem] * len(outs),
        scratch_shapes=[pltpu.VMEM(shape, dtype) for shape, dtype in scratch]
        + [pltpu.SemaphoreType.DMA((48,))]
        if by_copy
        else [],
        cost_estimate=pl.CostEstimate(flops=0, bytes_accessed=1024, transcendentals=0),
        name=name,
    )(*args)


class Copies:
    def __init__(self, semaphores):
        self.semaphores = semaphores
        self.used = 0

    def start(self, source, target):
        copy = pltpu.make_async_copy(source, target, self.semaphores.at[self.used])
        self.used += 1
        copy.start()
        return copy

    def each(self, sources, targets, count, width):
        first = self.used
        self.used += count * len(sources)

        def copy(k, tile):
            at = pl.ds(pl.multiple_of(tile * width, width), width)
            number = first + k * count + tile
            return pltpu.make_async_copy(
                sources[k].at[:, at], targets[k].at[:, at], self.semaphores.at[number]
            )

        def start(tile):
            for k in range(len(sources)):
                copy(k, tile).start()

        def finish(tile, carry=0):
            for k in range(len(sources)):
                copy(k, tile).wait()
            return carry

        return start, finish

    def place(self, pieces, places, target):
        started = []
        for piece, place in zip(pieces, places):
            if place is None:
                started.append(self.start(piece, target))
            else:
                at = pl.multiple_of(place(lax.axis_index("dp")), 8)
                started.append(self.start(piece, target.at[pl.ds(at, piece.shape[0]), :]))
        return started


    def first_blocks(self, part, lead, outs):
        started = []
        for distance, out in zip((4 * lead, -3 * lead), outs):
            rows = out.shape[0]
            at = pl.multiple_of(ring_device_at(lax.axis_index("dp"), distance) * rows, 8)
            started.append(self.start(part.at[pl.ds(at, rows), :], out))
        return started


def wait(copies):
    for copy in copies:
        copy.wait()


def kernel_add(distances, part, *refs):
    count = len(distances)
    moved, outs, refs = refs[:count], refs[count : 2 * count], refs[2 * count :]
    copies = Copies(refs[-1])
    rows = outs[0].shape[0]
    arriving = []
    for k, distance in enumerate(distances):
        at = pl.multiple_of(ring_device_at(lax.axis_index("dp"), distance) * rows, 8)
        arriving.append(copies.start(moved[k], refs[2 * k]))
        arriving.append(copies.start(part.at[pl.ds(at, rows), :], refs[2 * k + 1]))
    leaving = []
    step = 48 if rows % 48 == 0 else rows
    for k in range(count):
        wait(arriving[2 * k : 2 * k + 2])
        total, block = refs[2 * k], refs[2 * k + 1]

        def add(i, carry):
            at = pl.ds(pl.multiple_of(i * step, step), step)
            total[at, :] = (total[at, :].astype(f32) + block[at, :].astype(f32)).astype(bf16)
            return carry

        lax.fori_loop(0, rows // step, add, 0)
        leaving.append(copies.start(total, outs[k]))
    wait(leaving)


def add_blocks(part, moved, distances):
    shape = moved[0].shape
    return run(
        partial(kernel_add, distances),
        "add_blocks",
        [(shape, bf16)] * len(moved),
        (part, *moved),
        [(shape, bf16)] * (2 * len(moved)),
    )


def dot(a, b):
    return jnp.dot(a, b, preferred_element_type=f32)


def dot_last(a, b):
    return lax.dot_general(a, b, (((1,), (1,)), ((), ())), preferred_element_type=f32)


def dot_first(a, b):
    return lax.dot_general(a, b, (((0,), (0,)), ((), ())), preferred_element_type=f32)


def core_here():
    return lax.axis_index("mp") & 1


def pair_rows(total, pair):
    half = total // 2
    return pl.ds(pl.multiple_of(pair * half, half), half)


def image_rows(rows, image):
    return pl.ds(pl.multiple_of(image * rows, rows), rows)


def tiles(total):
    return total // 384 if total % 384 == 0 else 1


def chosen(index, values):
    shape = (values.shape[0], index.shape[1])
    select = lax.broadcasted_iota(jnp.int32, shape, 0) == index
    return dot_first(select.astype(f32).astype(bf16), values)


def head_values(values, local, depth, head, t):
    return values[:, t * local + head * depth : t * local + (head + 1) * depth]


def stacked_probs(values, local, depth, heads):
    scores = jnp.concatenate(
        [
            dot_last(
                head_values(values, local, depth, head, 0),
                head_values(values, local, depth, head, 1),
            )
            for head in range(heads)
        ],
        0,
    )
    scores = scores * depth ** (-0.5)
    exp_scores = jnp.exp(scores - jnp.max(scores, axis=-1, keepdims=True))
    return exp_scores / jnp.sum(exp_scores, axis=-1, keepdims=True)


def lane_start(columns):
    return columns // 128 * 128


def kernel_mods(cond, weights, out):
    for k in range(out.shape[0]):
        out[k] = dot(cond[...], weights[k].astype(bf16))


def kernel_silu(grads, weights, out):
    total = dot_last(grads[0], weights[0].astype(bf16))
    for k in range(1, grads.shape[0]):
        total = total + dot_last(grads[k], weights[k].astype(bf16))
    out[...] = total


def kernel_norm(tokens, index, own, normed):
    images, rows = index.shape
    core = core_here()

    def norm(image, carry):
        at = image_rows(rows, image)
        values = chosen(index[pl.ds(image, 1), :], tokens[image])
        normed[at, :] = layer_norm(values)[0]

        @pl.when(image // (images // 2) == core)
        def _():
            place = image_rows(rows, image - core * (images // 2))
            own[place, :] = values.astype(bf16)

        return carry

    lax.fori_loop(0, images, norm, 0)


def kernel_project(places, *refs):
    count = len(places)
    pieces, (given, mods) = refs[:count], refs[count : count + 2]
    outs, refs = refs[count + 2 : count + 4], refs[count + 4 :]
    full, normed, hidden, projected, semaphores = refs
    copies = Copies(semaphores)
    images = mods.shape[1]
    total = normed.shape[0]
    rows = total // images
    arriving = [copies.start(given, normed)]
    columns = full.shape[1]
    placed = copies.place([piece.at[:, :columns] for piece in pieces], places, full)
    wait(arriving)

    def norm(image, carry):
        at = image_rows(rows, image)
        scale = mods[1, pl.ds(image, 1), :]
        values = normed[at, :] * (1.0 + scale) + mods[0, pl.ds(image, 1), :]
        hidden[at, :] = values.astype(bf16)
        return carry

    lax.fori_loop(0, images, norm, 0)
    leaving = [copies.start(hidden, outs[0])]
    wait(placed)
    weights = full[:, : projected.shape[1]]

    def project(pair, carry):
        at = pair_rows(total, pair)
        projected[at, :] = dot(hidden[at, :], weights).astype(bf16)
        return carry

    lax.fori_loop(0, 2, project, 0)
    leaving.append(copies.start(projected, outs[1]))
    wait(leaving)


def kernel_attend(places, heads, rows, *refs):
    count = len(places)
    pieces, (given,) = refs[:count], refs[count : count + 1]
    outs, refs = refs[count + 1 : count + 4], refs[count + 4 :]
    full, projected, attended, own, other, semaphores = refs
    copies = Copies(semaphores)
    total = projected.shape[0]
    local = attended.shape[1]
    depth = local // heads
    core = core_here()
    start = lane_start(3 * local)
    arriving = [copies.start(given, projected)]
    placed = copies.place([piece.at[:, start:] for piece in pieces], places, full)
    wait(arriving)

    def attend(image, carry):
        at = image_rows(rows, image)
        values = projected[at, :]
        probs = stacked_probs(values, local, depth, heads).astype(bf16)
        attended[at, :] = jnp.concatenate(
            [
                dot(
                    probs[head * rows : (head + 1) * rows],
                    head_values(values, local, depth, head, 2),
                ).astype(bf16)
                for head in range(heads)
            ],
            1,
        )
        return carry

    lax.fori_loop(0, total // rows, attend, 0)
    leaving = [copies.start(attended, outs[0])]
    wait(placed)
    weights = full[:, 3 * local - start :]
    other[...] = dot_last(attended[pair_rows(total, 1 - core), :], weights).astype(bf16)
    leaving.append(copies.start(other, outs[2]))
    own[...] = dot_last(attended[pair_rows(total, core), :], weights)
    leaving.append(copies.start(own, outs[1]))
    wait(leaving)


def kernel_kept_grad(grads, index, mods, own, mlp_grad):
    core = core_here()
    images, rows = index.shape
    half = images // 2
    for place in range(images):
        pair = core if place < half else 1 - core
        image = pair * half + place % half
        values = chosen(index[pl.ds(image, 1), :], grads[image])
        at = slice(place * rows, (place + 1) * rows)
        if place < half:
            own[at, :] = values.astype(bf16)
        mlp_grad[at, :] = (mods[5, pl.ds(image, 1), :] * values).astype(bf16)


def kernel_second_norm(kept, mods, own, moved, residual, hidden_two):
    core = core_here()
    half = mods.shape[1] // 2
    rows = residual.shape[0] // half
    for image in range(half):
        at = slice(image * rows, (image + 1) * rows)
        where = core * half + image
        gate, shift, scale = [mods[k, pl.ds(where, 1), :] for k in (2, 3, 4)]
        attn_out = own[at, :].astype(f32) + moved[at, :].astype(f32)
        values = kept[at, :].astype(f32) + gate * attn_out
        residual[at, :] = values
        normed, _ = layer_norm(values)
        hidden_two[at, :] = (normed * (1.0 + scale) + shift).astype(bf16)


gelu_rate = math.sqrt(2.0 / math.pi)


def gelu_parts(values):
    tanh = jnp.tanh(gelu_rate * (values + 0.044715 * (values * values * values)))
    return 0.5 * (1.0 + tanh), tanh


def kernel_feed_forward(places, lead, *refs):
    count = len(places)
    pieces, (here, there, mlp) = refs[:count], refs[count : count + 3]
    outs, refs = refs[count + 3 : -7], refs[-7:]
    full, hidden_two, mlp_grad, pre_act, activated, fc2_grad, semaphores = refs
    copies = Copies(semaphores)
    half = here.shape[0]
    arriving = [copies.start(here, hidden_two.at[:half, :])]
    arriving.append(copies.start(there, hidden_two.at[half:, :]))
    arriving += copies.place(pieces, places, full)
    arriving.append(copies.start(mlp, mlp_grad))
    columns = full.shape[1]
    count = tiles(columns)
    width = columns // count
    leave, leave_end = copies.each([pre_act, activated, fc2_grad], outs[:3], count, width)
    wait(arriving)

    def product(tile, carry):
        at = pl.ds(pl.multiple_of(tile * width, width), width)
        values = dot(hidden_two[...], full[:, at])
        pre_act[:, at] = values
        low = (values * gelu_parts(values)[0]).astype(bf16)
        activated[:, at] = low
        fc2_grad[:, at] = dot_first(mlp_grad[...], low).astype(bf16)
        leave(tile)
        return carry

    lax.fori_loop(0, count, product, 0)
    leaving = copies.first_blocks(fc2_grad, lead, outs[3:])
    lax.fori_loop(0, count, leave_end, 0)
    wait(leaving)


def kernel_fc1_grad(lead, here, there, pre, *refs):
    outs, (hidden_two, pre_grad, fc1_grad, semaphores) = refs[:-4], refs[-4:]
    copies = Copies(semaphores)
    half = here.shape[0]
    arriving = [copies.start(here, hidden_two.at[:half, :])]
    arriving.append(copies.start(there, hidden_two.at[half:, :]))
    arriving.append(copies.start(pre, pre_grad))
    wait(arriving)
    columns = fc1_grad.shape[1]
    count = tiles(columns)
    width = columns // count
    leave, leave_end = copies.each([fc1_grad], outs[:1], count, width)

    def product(tile, carry):
        at = pl.ds(pl.multiple_of(tile * width, width), width)
        fc1_grad[:, at] = dot_first(hidden_two[...], pre_grad[:, at]).astype(bf16)
        leave(tile)
        return carry

    lax.fori_loop(0, count, product, 0)
    leaving = copies.first_blocks(fc1_grad, lead, outs[1:])
    lax.fori_loop(0, count, leave_end, 0)
    wait(leaving)


def kernel_feed_back(one_places, two_places, *refs):
    count = len(one_places)
    ones, twos, refs = refs[:count], refs[count : 2 * count], refs[2 * count :]
    (mlp, pre), outs, refs = refs[:2], refs[2:5], refs[5:]
    fc1, fc2, mlp_grad, pre_act, pre_grad, own, other, semaphores = refs
    copies = Copies(semaphores)
    arriving = [copies.start(mlp, mlp_grad)] + copies.place(twos, two_places, fc2)
    columns = fc2.shape[1]
    count = tiles(columns)
    width = columns // count
    values_in = [copies.start(pre, pre_act)]
    later = copies.place(ones, one_places, fc1)
    leave, leave_end = copies.each([pre_grad], outs[:1], count, width)
    wait(arriving + values_in)

    def product(tile, carry):
        at = pl.ds(pl.multiple_of(tile * width, width), width)
        gradient = dot(mlp_grad[...], fc2[:, at])
        values = pre_act[:, at]
        share, tanh = gelu_parts(values)
        slope = share + 0.5 * values * (1.0 - tanh * tanh) * gelu_rate * (
            1.0 + 3.0 * 0.044715 * (values * values)
        )
        pre_grad[:, at] = (gradient * slope).astype(bf16)
        leave(tile)
        return carry

    lax.fori_loop(0, count, product, 0)
    wait(later)
    back_product(copies, pre_grad, fc1, own, other, outs[1:])
    lax.fori_loop(0, count, leave_end, 0)


def back_product(copies, rows, weights, own, other, outs):
    half = own.shape[0]
    depth = weights.shape[0]
    count = tiles(depth)
    width = depth // count
    leave, leave_end = copies.each([own, other], outs, count, width)

    def product(tile, carry):
        at = pl.ds(pl.multiple_of(tile * width, width), width)
        values = dot_last(rows[...], weights[at, :])
        other[:, at] = values[half:].astype(bf16)
        own[:, at] = values[:half]
        leave(tile)
        return carry

    lax.fori_loop(0, count, product, 0)
    lax.fori_loop(0, count, leave_end, 0)


def kernel_feed_out(places, *refs):
    count = len(places)
    pieces, (low,) = refs[:count], refs[count : count + 1]
    outs, (full, activated, own, other, semaphores) = refs[count + 1 : count + 3], refs[count + 3 :]
    copies = Copies(semaphores)
    arriving = [copies.start(low, activated)] + copies.place(pieces, places, full)
    wait(arriving)
    back_product(copies, activated, full, own, other, outs)


def kernel_second_back(
    own, moved, residual, attn_own, attn_moved, grad, mods, residual_grad, attn_grad, sums
):
    core = core_here()
    half = mods.shape[1] // 2
    rows = residual.shape[0] // half
    for image in range(half):
        at = slice(image * rows, (image + 1) * rows)
        where = core * half + image
        gate, scale = [mods[k, pl.ds(where, 1), :] for k in (2, 4)]
        normed, inverse = layer_norm(residual[at, :])
        gradient = own[at, :].astype(f32) + moved[at, :].astype(f32)
        sums[1, pl.ds(image, 1), :] = jnp.sum(gradient, axis=0, keepdims=True)
        sums[2, pl.ds(image, 1), :] = jnp.sum(gradient * normed, axis=0, keepdims=True)
        values = grad[at, :].astype(f32) + norm_back(normed, inverse, gradient * (1.0 + scale))
        residual_grad[at, :] = values
        attn_out = attn_own[at, :].astype(f32) + attn_moved[at, :].astype(f32)
        sums[0, pl.ds(image, 1), :] = jnp.sum(values * attn_out, axis=0, keepdims=True)
        attn_grad[at, :] = (gate * values).astype(bf16)


def kernel_attention_back(places, heads, rows, lead, *refs):
    count = len(places)
    pieces, inputs = refs[:count], refs[count : count + 5]
    outs, refs = refs[count + 5 : -11], refs[-11:]
    here, there, projected_in, attended_in, hidden_in = inputs
    full, out_grad, projected, attended, hidden, back, grads, attn_grad, own, other = refs[:-1]
    copies = Copies(refs[-1])
    core = core_here()
    total = out_grad.shape[0]
    local = attended.shape[1]
    depth = local // heads
    arriving = [
        copies.start(here, out_grad.at[pair_rows(total, core), :]),
        copies.start(there, out_grad.at[pair_rows(total, 1 - core), :]),
    ] + copies.place(pieces, places, full)
    later = [copies.start(projected_in, projected), copies.start(attended_in, attended)]
    last = [copies.start(hidden_in, hidden)]
    wait(arriving)
    back[...] = dot(out_grad[...], full[:, 3 * local :]).astype(bf16)
    wait(later)

    def image_back(image, carry):
        at = image_rows(rows, image)
        values = projected[at, :]
        gradient = back[at, :]
        probs = stacked_probs(values, local, depth, heads)
        prob_grad = jnp.concatenate(
            [
                dot_last(
                    head_values(gradient, local, depth, head, 0),
                    head_values(values, local, depth, head, 2),
                )
                for head in range(heads)
            ],
            0,
        )
        score_grad = probs * (prob_grad - jnp.sum(prob_grad * probs, axis=-1, keepdims=True))
        score_grad = score_grad.astype(bf16)
        probs = probs.astype(bf16)
        parts = []
        for t in range(3):
            for head in range(heads):
                own_rows = slice(head * rows, (head + 1) * rows)
                if t == 0:
                    key = head_values(values, local, depth, head, 1)
                    part = dot(score_grad[own_rows], key) * depth ** (-0.5)
                elif t == 1:
                    query = head_values(values, local, depth, head, 0)
                    part = dot_first(score_grad[own_rows], query) * depth ** (-0.5)
                else:
                    part = dot_first(
                        probs[own_rows], head_values(gradient, local, depth, head, 0)
                    )
                parts.append(part.astype(bf16))
        grads[at, :] = jnp.concatenate(parts, 1)
        return carry

    lax.fori_loop(0, total // rows, image_back, 0)
    weights = full[:, : 3 * local]
    other[...] = dot_last(grads[pair_rows(total, 1 - core), :], weights).astype(bf16)
    leaving = [copies.start(other, outs[2])]
    own[...] = dot_last(grads[pair_rows(total, core), :], weights)
    leaving.append(copies.start(own, outs[1]))
    wait(last)
    attn_grad[:, 3 * local :] = dot_first(out_grad[...], attended[...]).astype(bf16)
    attn_grad[:, : 3 * local] = dot_first(hidden[...], grads[...]).astype(bf16)
    leaving.append(copies.start(attn_grad, outs[0]))
    leaving += copies.first_blocks(attn_grad, lead, outs[3:])
    wait(leaving)


def kernel_output(own, moved, residual, grad, mods, kept_out, sums):
    core = core_here()
    half = mods.shape[1] // 2
    rows = residual.shape[0] // half
    for image in range(half):
        at = slice(image * rows, (image + 1) * rows)
        mlp_out = own[at, :].astype(f32) + moved[at, :].astype(f32)
        gate = mods[5, pl.ds(core * half + image, 1), :]
        kept_out[at, :] = (residual[at, :] + gate * mlp_out).astype(bf16)
        sums[pl.ds(image, 1), :] = jnp.sum(
            grad[at, :].astype(f32) * mlp_out, axis=0, keepdims=True
        )


def kernel_first_back(
    own, moved, residual_grad, kept, mods, late, last, kept_grad, mine, partner
):
    me = lax.axis_index("mp")
    core = me & 1
    half = mods.shape[1] // 2
    rows = residual_grad.shape[0] // half
    local = mine.shape[2]
    lines = [[], []]
    for image in range(half):
        at = slice(image * rows, (image + 1) * rows)
        normed, inverse = layer_norm(kept[at, :].astype(f32))
        gradient = own[at, :].astype(f32) + moved[at, :].astype(f32)
        lines[0].append(jnp.sum(gradient, axis=0, keepdims=True))
        lines[1].append(jnp.sum(gradient * normed, axis=0, keepdims=True))
        scale = mods[1, pl.ds(core * half + image, 1), :]
        values = residual_grad[at, :] + norm_back(normed, inverse, gradient * (1.0 + scale))
        kept_grad[at, :] = values.astype(bf16)
    planes = [jnp.concatenate(line, 0) for line in lines]
    planes += [late[0], late[1], late[2], last[...]]
    for k, plane in enumerate(planes):
        blocks = [plane[:, j * local : (j + 1) * local] for j in range(4)]
        for out, device in ((mine, me), (partner, me ^ 1)):
            picked = blocks[0]
            for j in range(1, 4):
                picked = jnp.where(device == j, blocks[j], picked)
            out[k] = picked.astype(bf16)


def new_state(weight, moment, average, gradient, rate, steps):
    decay = (1.0 + steps) / (10.0 + steps)
    new_moment = momentum_rate * moment + gradient
    master = weight - rate * (gradient + momentum_rate * new_moment)
    return master, new_moment, decay * average + (1.0 - decay) * master


def attention_step(rate, steps, gradient, *refs):
    counts = steps[0].astype(f32)
    qkv, proj, qkv_out, proj_out = refs[:3], refs[3:6], refs[6:9], refs[9:]
    local = proj[0].shape[1]
    for t in range(3):
        values = new_state(
            *[ref[t] for ref in qkv], gradient[:, t * local : (t + 1) * local], rate, counts
        )
        for ref, value in zip(qkv_out, values):
            ref[t] = value
    values = new_state(*[ref[...] for ref in proj], gradient[:, 3 * local :], rate, counts)
    for ref, value in zip(proj_out, values):
        ref[...] = value


def step_attention(qkv, proj, gradient, rate, steps):
    whole = pl.BlockSpec(memory_space=pltpu.VMEM)
    size = qkv[0].size + proj[0].size
    return pl.pallas_call(
        partial(attention_step, rate),
        out_shape=[jax.ShapeDtypeStruct(x.shape, f32) for x in qkv + proj],
        in_specs=[pl.BlockSpec(memory_space=pltpu.SMEM)] + [whole] * 7,
        out_specs=[whole] * 6,
        cost_estimate=pl.CostEstimate(flops=0, bytes_accessed=1024, transcendentals=0),
        name="step_attention",
    )(steps, gradient, *qkv, *proj)


def ada_step(rate, steps, cond, mods, weight, moment, average, master, new_moment, ema):
    counts = steps[0].astype(f32)
    gradient = lax.dot_general(
        cond[...], mods[0], (((0,), (0,)), ((), ())), preferred_element_type=f32
    )
    values = new_state(weight[0], moment[0], average[0], gradient, rate, counts)
    master[0], new_moment[0], ema[0] = values


def step_ada(weight, moment, average, cond, mods, rate, steps):
    count, rows, columns = weight.shape
    spec = pl.BlockSpec((1, rows, columns), lambda k: (k, 0, 0))
    return pl.pallas_call(
        partial(ada_step, rate),
        grid=(count,),
        out_shape=[jax.ShapeDtypeStruct(weight.shape, f32)] * 3,
        in_specs=[
            pl.BlockSpec(memory_space=pltpu.SMEM),
            pl.BlockSpec(cond.shape, lambda k: (0, 0)),
            pl.BlockSpec((1,) + mods.shape[1:], lambda k: (k, 0, 0)),
        ]
        + [spec] * 3,
        out_specs=[spec] * 3,
        cost_estimate=pl.CostEstimate(flops=0, bytes_accessed=1024, transcendentals=0),
        name="step_ada",
    )(steps, cond, mods, weight, moment, average)


def per_device(
    tokens,
    condition,
    cotangent,
    kept_index,
    skip_index,
    step_count,
    ada_weight,
    qkv_weight,
    proj_weight,
    fc1_weight,
    fc2_weight,
    ada_moment,
    qkv_moment,
    proj_moment,
    fc1_moment,
    fc2_moment,
    ada_average,
    qkv_average,
    proj_average,
    fc1_average,
    fc2_average,
):
    images, seq, width = tokens.shape
    kept_count = kept_index.shape[1]
    own_d = ada_weight.shape[0]
    mods = ada_weight.shape[1]
    local = ada_weight.shape[2]
    units = fc1_weight.shape[1]
    local_heads = local // HEAD_DIM
    total = images * kept_count
    half = total // 2
    core = lax.axis_index("mp") % 2
    chip = lax.axis_index("mp") // 2
    dp_size = lax.axis_size("dp")
    index = lax.axis_index("dp")
    ring = dp_size == 8

    def tick(extras, *hops):
        hops = [(one, sides) for one, sides in hops if one is not None]
        moving = tuple(one.start(sides) for one, sides in hops)
        held, moved = stage((tuple(extras()), moving))
        for (one, sides), values in zip(hops, moved):
            one.finish(sides, values)
        return held

    attn_low = jnp.concatenate(
        [qkv_weight[0], qkv_weight[1], qkv_weight[2], proj_weight.T], 1
    ).astype(bf16)
    fc1_low = fc1_weight.astype(bf16)
    fc2_low = fc2_weight.T.astype(bf16)
    if ring:
        attn_ring, fc1_ring, fc2_ring = Gather(attn_low, 1), Gather(fc1_low, 1), Gather(fc2_low, -1)
    else:
        attn_ring = fc1_ring = fc2_ring = None
        attn_pieces, attn_places = [gather_plain(attn_low)], [None]
        fc1_pieces, fc1_places = [gather_plain(fc1_low)], [None]
        fc2_pieces, fc2_places = [gather_plain(fc2_low)], [None]
    block = [((width // 8, units), bf16)] * 2 if ring else []
    attn_block = [((width // 8, 4 * local), bf16)] * 2 if ring else []

    cond_float = condition.astype(f32)
    silu_cond = jax.nn.silu(cond_float).astype(bf16)
    small = silu_cond.reshape(images, dp_size, own_d)
    levels = len(dp_groups())
    def first_norm():
        return spread_round(small, 0, 0), *run(
            kernel_norm,
            "first_norm",
            [((half, width), bf16), ((total, width), f32)],
            (tokens, kept_index),
        )

    small, kept_own, normed = tick(first_norm, (attn_ring, "ab"))
    ada_state = [jnp.moveaxis(x, 1, 0) for x in (ada_weight, ada_moment, ada_average)]

    def rest_of_cond():
        values = small
        for level in range(1, levels):
            values = spread_round(values, 0, level)
        return (values,)

    (small,) = tick(rest_of_cond, (attn_ring, "ab"))

    def sum_of_mods():
        own = lax.dynamic_index_in_dim(small, index, 1, keepdims=False)
        (values,) = run(
            kernel_mods, "mods", [((mods, dp_size * images, local), f32)], (own, ada_state[0])
        )
        for level in reversed(range(1, levels)):
            values = sum_round(values, 1, level)
        return own, values

    cond_own, small = tick(sum_of_mods, (attn_ring, "ab"))
    (mod_local,) = tick(lambda: (sum_round(small, 1, 0),), (attn_ring, "a"))
    if ring:
        attn_pieces, attn_places = attn_ring.pieces()

    def all_mods():
        at_core = swap_core(mod_local)
        at_x = swap_x(mod_local)
        at_both = lax.ppermute(mod_local, "mp", [(j, j ^ 3) for j in range(4)])
        pairs = [join_pair(mod_local, at_core, core, 2), join_pair(at_x, at_both, core, 2)]
        return (
            jnp.where(chip == 0, jnp.concatenate(pairs, 2), jnp.concatenate(pairs[::-1], 2)),
        )

    (modulation,) = tick(all_mods, (fc1_ring, "ab"))


    def project():
        outs = [((total, width), bf16), ((total, 3 * local), bf16)]
        lanes = -(-3 * local // 128) * 128
        return run(
            partial(kernel_project, attn_places),
            "project",
            outs,
            (*attn_pieces, normed, modulation),
            [((width, lanes), bf16), ((total, width), f32)] + outs,
        )

    hidden, projected = tick(project, (fc2_ring, "ab"))

    def add_low(own, other):
        return (own + other.astype(f32)).astype(bf16)

    def attend():
        outs = [((total, local), bf16), ((half, width), f32), ((half, width), bf16)]
        lanes = 4 * local - lane_start(3 * local)
        return run(
            partial(kernel_attend, attn_places, local_heads, kept_count),
            "attend",
            outs,
            (*attn_pieces, projected),
            [((width, lanes), bf16), ((total, 3 * local), bf16)] + outs,
        )

    attended, own_part, other_part = tick(attend, (fc1_ring, "ab"))

    def attention_sums():
        own = add_low(own_part, swap_core(other_part))
        return own, swap_x(own), *kept_grads()


    def kept_grads():
        return run(
            kernel_kept_grad,
            "kept_grad",
            [((half, width), bf16), ((total, width), bf16)],
            (cotangent, kept_index, modulation),
        )

    attn_own, attn_moved, grad_own, mlp_grad = tick(
        attention_sums, (fc1_ring, "ab"), (fc2_ring, "ab")
    )

    def second_norm():
        values, low = run(
            kernel_second_norm,
            "second_norm",
            [((half, width), f32), ((half, width), bf16)],
            (kept_own, modulation, attn_own, attn_moved),
        )
        return values, low, swap_core(low)

    residual, hidden_here, hidden_there = tick(second_norm, (fc1_ring, "a"), (fc2_ring, "a"))
    if ring:
        fc1_pieces, fc1_places = fc1_ring.pieces()

    def feed_forward():
        outs = [((total, units), f32), ((total, units), bf16), ((width, units), bf16)]
        return run(
            partial(kernel_feed_forward, fc1_places, -1),
            "feed_forward",
            outs + block,
            (*fc1_pieces, hidden_here, hidden_there, mlp_grad),
            [((width, units), bf16), ((total, width), bf16), ((total, width), bf16)] + outs,
        )

    pre_act, activated, fc2_grad, *first = tick(feed_forward, (fc2_ring, "ba"))
    if ring:
        fc2_pieces, fc2_places = fc2_ring.pieces()
        fc2_sums = Scatter(fc2_grad, -1, first)
    else:
        fc2_sums = fc1_sums = attn_sums = None

    def feed_back():
        outs = [((total, units), bf16), ((half, width), f32), ((half, width), bf16)]
        return run(
            partial(kernel_feed_back, fc1_places, fc2_places),
            "feed_back",
            outs,
            (*fc1_pieces, *fc2_pieces, mlp_grad, pre_act),
            [
                ((width, units), bf16),
                ((width, units), bf16),
                ((total, width), bf16),
                ((total, units), f32),
            ]
            + outs,
        )

    pre_grad, own_part, other_part = tick(feed_back, (fc2_sums, "ab"))
    moving = []

    def products():
        own_low = add_low(own_part, swap_core(other_part))
        outs = [((width, units), bf16)]
        grad, *first = run(
            partial(kernel_fc1_grad, -1),
            "fc1_grad",
            outs + block,
            (hidden_here, hidden_there, pre_grad),
            [((total, width), bf16), ((total, units), bf16)] + outs,
        )
        if ring:
            moving.append(Scatter(grad, -1, first))
            first = moving[0].start("ab")
        outs = [((half, width), f32), ((half, width), bf16)]
        sums = run(
            partial(kernel_feed_out, fc2_places),
            "feed_out",
            outs,
            (*fc2_pieces, activated),
            [((width, units), bf16), ((total, units), bf16)] + outs,
        )
        return own_low, swap_x(own_low), grad, *sums, *first

    hidden_own, hidden_moved, fc1_grad, own_mlp, other_mlp, *first = tick(
        products, (fc2_sums, "ab+")
    )
    if ring:
        (fc1_sums,) = moving
        fc1_sums.part = fc1_grad
        fc1_sums.finish("ab", first)

    def second_back():
        sums = run(
            kernel_second_back,
            "second_back",
            [((half, width), f32), ((half, width), bf16), ((3, images // 2, width), f32)],
            (
                hidden_own,
                hidden_moved,
                residual,
                attn_own,
                attn_moved,
                grad_own,
                modulation,
            ),
        )
        return *sums, *(fc1_sums.prepare("ab") if ring else ())

    residual_grad, out_here, late_mods, *sums = tick(second_back, (fc2_sums, "ab"))
    if ring:
        fc1_sums.finish("ab", sums)
    out_here, out_there, mlp_own = tick(
        lambda: (out_here, swap_core(out_here), add_low(own_mlp, swap_core(other_mlp)))
    )

    def attention_back():
        outs = [((width, 4 * local), bf16), ((half, width), f32), ((half, width), bf16)]
        back = run(
            partial(kernel_attention_back, attn_places, local_heads, kept_count, 1),
            "attention_back",
            outs + attn_block,
            (*attn_pieces, out_here, out_there, projected, attended, hidden),
            [
                ((width, 4 * local), bf16),
                ((total, width), bf16),
                ((total, 3 * local), bf16),
                ((total, local), bf16),
                ((total, width), bf16),
                ((total, local), bf16),
                ((total, 3 * local), bf16),
            ]
            + outs,
        )
        return swap_x(mlp_own), *back

    mlp_moved, attn_grad, own_part, other_part, *first = tick(attention_back, (fc1_sums, "ab"))
    if ring:
        attn_sums = Scatter(attn_grad, 1, first)

    def output():
        return run(
            kernel_output,
            "output",
            [((half, width), bf16), ((images // 2, width), f32)],
            (mlp_own, mlp_moved, residual, grad_own, modulation),
        )

    def attention_back_sums():
        own = add_low(own_part, swap_core(other_part))
        return own, swap_x(own), *output()

    back_own, back_moved, kept_out, last_mods = tick(
        attention_back_sums, (attn_sums, "ab+"), (fc1_sums, "ab")
    )

    def first_back():
        kept, mine, partner = run(
            kernel_first_back,
            "first_back",
            [
                ((half, width), bf16),
                ((mods, images // 2, local), bf16),
                ((mods, images // 2, local), bf16),
            ],
            (
                back_own,
                back_moved,
                residual_grad,
                kept_own,
                modulation,
                late_mods,
                last_mods,
            ),
        )
        return kept, join_pair(mine, swap_core(partner), core, 1)

    kept_grad, small = tick(first_back, (attn_sums, "ab"))

    def spreads():
        values = spread_round(small, 1, 0)
        return values, spread_pair(kept_grad, core), spread_pair(kept_out, core)

    small, kept_grad, kept_out = tick(spreads, (attn_sums, "ab"))
    kept_grad, kept_out = [x.reshape(images, kept_count, width) for x in (kept_grad, kept_out)]

    rate = 0.02 / math.sqrt(images * dp_size * kept_count)
    steps = step_count[0].astype(f32)
    positions = lax.broadcasted_iota(jnp.int32, (images, seq, kept_count), 1)
    select = (kept_index[:, None, :] == positions).astype(bf16)
    is_kept = jnp.any(kept_index[:, None, :] == positions, axis=2)[:, :, None]

    def outputs():
        values = small
        for level in range(1, levels):
            values = spread_round(values, 1, level)
        placed = jnp.einsum("bsi,bid->bsd", select, kept_grad, preferred_element_type=f32)
        grads = jnp.where(is_kept, placed, cotangent.astype(f32))
        placed = jnp.einsum("bsi,bid->bsd", select, kept_out, preferred_element_type=f32)
        out = jnp.where(is_kept, placed.astype(bf16), tokens)
        last = (fc2_sums.held["a"], fc2_sums.held["b"]) if ring else ()
        return values, grads, out, *last

    mod_grad_all, tokens_grad, block_out, *last = tick(
        outputs, (attn_sums, "a"), (fc1_sums, "a")
    )
    if ring:
        fc2_sums.finish("ab", last)
    (silu_part,) = run(
        kernel_silu, "silu", [((dp_size * images, own_d), f32)], (mod_grad_all, ada_state[0])
    )
    silu_part = silu_part + swap_core(silu_part)
    silu_part = silu_part + swap_x(silu_part)
    ada_new = step_ada(*ada_state, cond_own, mod_grad_all, rate, step_count)
    ada_master, ada_momentum, ada_ema = [jnp.moveaxis(x, 0, 1) for x in ada_new]
    attn_shard = attn_sums.total() if ring else scatter_plain(attn_grad)
    fc1_shard = fc1_sums.total() if ring else scatter_plain(fc1_grad)
    if ring:
        fc2_sums.finish("a", fc2_sums.start("a"))
        fc2_shard = fc2_sums.total()
    else:
        fc2_shard = scatter_plain(fc2_grad)
    fc2_master, fc2_momentum, fc2_ema = new_state(
        fc2_weight.T, fc2_moment.T, fc2_average.T, fc2_shard, rate, steps
    )
    silu_blocks = silu_part.reshape(dp_size, images, own_d)
    attn_new = step_attention(
        (qkv_weight, qkv_moment, qkv_average),
        (proj_weight.T, proj_moment.T, proj_average.T),
        attn_shard,
        rate,
        step_count,
    )
    for level in reversed(range(levels)):
        silu_blocks = turn_round(silu_blocks, level)
    silu_blocks = in_order(silu_blocks)
    qkv_master, qkv_momentum, qkv_ema, proj_master, proj_momentum, proj_ema = attn_new
    fc1_master, fc1_momentum, fc1_ema = new_state(
        fc1_weight, fc1_moment, fc1_average, fc1_shard, rate, steps
    )
    silu_grad = jnp.moveaxis(silu_blocks, 0, 1).reshape(images, width)
    silu_value, silu_pull = jax.vjp(jax.nn.silu, cond_float)
    condition_grad = silu_pull(silu_grad)[0]
    return (
        block_out,
        tokens_grad,
        condition_grad,
        ada_master,
        qkv_master,
        proj_master.T,
        fc1_master,
        fc2_master.T,
        ada_momentum,
        qkv_momentum,
        proj_momentum.T,
        fc1_momentum,
        fc2_momentum.T,
        ada_ema,
        qkv_ema,
        proj_ema.T,
        fc1_ema,
        fc2_ema.T,
    )


def solution(mesh):
    weights = (
        P("dp", None, "mp"),
        P(None, "dp", "mp"),
        P("mp", "dp"),
        P("dp", "mp"),
        P("mp", "dp"),
    )
    rows = P("dp", None, None)
    pairs = P("dp", None)
    return jax.shard_map(
        per_device,
        mesh=mesh,
        in_specs=(rows, pairs, rows, pairs, pairs, P()) + weights * 3,
        out_specs=(rows, rows, pairs) + weights * 3,
        check_vma=False,
    )
```

```python
from functools import partial
import math

import jax
import jax.numpy as jnp
from jax import lax
from jax.experimental import pallas as pl
from jax.experimental.pallas import tpu as pltpu
from jax.sharding import PartitionSpec as P

HEAD_DIM = 72

epsilon = 1e-06
momentum_rate = 0.9

f32 = jnp.float32
bf16 = jnp.bfloat16


def layer_norm(values):
    centered = values - jnp.mean(values, axis=-1, keepdims=True)
    inverse = lax.rsqrt(jnp.mean(centered * centered, axis=-1, keepdims=True) + epsilon)
    return (centered * inverse, inverse)


def norm_back(normed, inverse, gradient):
    return inverse * (
        gradient
        - jnp.mean(gradient, axis=-1, keepdims=True)
        - normed * jnp.mean(gradient * normed, axis=-1, keepdims=True)
    )


def swap_core(values):
    return lax.ppermute(values, "mp", [(j, j ^ 1) for j in range(4)])


def swap_x(values):
    return lax.ppermute(values, "mp", [(j, j ^ 2) for j in range(4)])


def join_pair(own, other, core, axis=0):
    return jnp.where(
        core == 0,
        jnp.concatenate([own, other], axis),
        jnp.concatenate([other, own], axis),
    )


def spread_pair(own, core):
    return join_pair(own, swap_core(own), core)


def swap_dp(values, bit):
    size = lax.axis_size("dp")
    return lax.ppermute(values, "dp", [(i, i ^ bit) for i in range(size)])


def dp_groups():
    size = lax.axis_size("dp")
    return [4] + [2] * (size.bit_length() - 3)


def spread_round(values, axis, level):
    groups = dp_groups()
    step = math.prod(groups[:level])
    others = [swap_dp(values, step * b) for b in range(1, groups[level])]
    return jnp.concatenate([values] + others, axis)


def sum_round(values, axis, level):
    groups = dp_groups()
    step = math.prod(groups[:level])
    blocks = jnp.split(values, groups[level], axis)
    total = blocks[0]
    for b in range(1, groups[level]):
        total = total + swap_dp(blocks[b], step * b)
    return total


def turn_round(values, level):
    groups = dp_groups()
    step = math.prod(groups[:level])
    shape = values.shape
    values = values.reshape((-1, groups[level], step) + shape[1:])
    blocks = [values[:, b] for b in range(groups[level])]
    blocks = [blocks[0]] + [swap_dp(blocks[b], step * b) for b in range(1, groups[level])]
    return jnp.stack(blocks, 1).reshape(shape)


def in_order(values):
    index = lax.axis_index("dp")
    shape = values.shape
    count = shape[0].bit_length() - 1
    values = values.reshape((2,) * count + shape[1:])
    for axis in range(count):
        values = jnp.where((index >> (count - 1 - axis)) & 1, jnp.flip(values, axis), values)
    return values.reshape(shape)


def ring_tables():
    cycle = [0, 2, 4, 6, 7, 5, 3, 1]
    clockwise = [(cycle[i], cycle[(i + 1) % 8]) for i in range(8)]
    return clockwise, [(b, a) for a, b in clockwise]


def ring_place_of(index):
    return jnp.where((index & 1) == 0, index >> 1, 7 - (index >> 1))


def ring_device(place):
    place = lax.rem(place, 8)
    return jnp.where(place < 4, 2 * place, 2 * (7 - place) + 1)


def hop(values, direction):
    clockwise, backward = ring_tables()
    return lax.ppermute(values, "dp", clockwise if direction > 0 else backward)


def ring_device_at(index, distance):
    return ring_device(ring_place_of(index) + distance + 8)


class Gather:
    def __init__(self, shard, lead):
        self.lead = lead
        self.shard = shard
        self.ahead = [shard]
        self.behind = [shard]

    def start(self, sides):
        moving = []
        if "a" in sides:
            moving.append(hop(self.ahead[-1], self.lead))
        if "b" in sides:
            moving.append(hop(self.behind[-1], -self.lead))
        return tuple(moving)

    def finish(self, sides, moved):
        moved = list(moved)
        if "a" in sides:
            self.ahead.append(moved.pop(0))
        if "b" in sides:
            self.behind.append(moved.pop(0))

    def pieces(self):
        rows = self.shard.shape[0]
        distances = [-self.lead * k for k in range(5)] + [self.lead * k for k in range(1, 4)]
        places = [
            partial(lambda distance, index: ring_device_at(index, distance) * rows, distance)
            for distance in distances
        ]
        return self.ahead + self.behind[1:], places


class Scatter:
    def __init__(self, part, lead, first):
        self.part, self.lead = part, lead
        self.rows = part.shape[0] // 8
        self.left = {"a": 4, "b": 3}
        self.added = {"a": False, "b": False}
        self.held = dict(zip("ab", first))

    def signs(self):
        return {"a": self.lead, "b": -self.lead}

    def add(self, values):
        full = {"a": 4, "b": 3}
        adding = [k for k in values if 0 < self.left[k] < full[k] and not self.added[k]]
        if adding:
            signs = self.signs()
            sums = add_blocks(
                self.part,
                [values[k] for k in adding],
                [signs[k] * self.left[k] for k in adding],
            )
            values = {**values, **dict(zip(adding, sums))}
            for k in adding:
                self.added[k] = True
        return values

    def prepare(self, sides):
        values = self.add({k: self.held[k] for k in sides})
        return tuple(values[k] for k in sides)

    def start(self, sides):
        values = self.add({k: self.held[k] for k in sides if k in "ab"})
        signs = self.signs()
        for k in values:
            self.left[k] -= 1
            self.added[k] = False
        values = {k: hop(value, signs[k]) for k, value in values.items()}
        if "+" in sides:
            values = self.add(values)
        return tuple(values.values())

    def finish(self, sides, moved):
        self.held.update(zip(sides, moved))

    def given(self):
        return self.held["a"], self.held["b"], self.part


def gather_plain(shard):
    return lax.all_gather(shard, "dp", axis=0, tiled=True)


def scatter_plain(part):
    return lax.psum_scatter(part.astype(f32), "dp", scatter_dimension=0, tiled=True)


stage = lax.optimization_barrier


def run(kernel, name, outs, args, scratch=None):
    vmem = pl.BlockSpec(memory_space=pltpu.VMEM)
    anywhere = pl.BlockSpec(memory_space=pl.ANY)
    by_copy = scratch is not None
    return pl.pallas_call(
        kernel,
        out_shape=[jax.ShapeDtypeStruct(shape, dtype) for shape, dtype in outs],
        in_specs=[vmem if not by_copy or x.size < 40000 else anywhere for x in args],
        out_specs=[anywhere if by_copy else vmem] * len(outs),
        scratch_shapes=[pltpu.VMEM(shape, dtype) for shape, dtype in scratch]
        + [pltpu.SemaphoreType.DMA((48,))]
        if by_copy
        else [],
        compiler_params=pltpu.CompilerParams(vmem_limit_bytes=20 << 20),
        cost_estimate=pl.CostEstimate(flops=0, bytes_accessed=1024, transcendentals=0),
        name=name,
    )(*args)


class Copies:
    def __init__(self, semaphores):
        self.semaphores = semaphores
        self.used = 0

    def start(self, source, target):
        copy = pltpu.make_async_copy(source, target, self.semaphores.at[self.used])
        self.used += 1
        copy.start()
        return copy

    def each(self, sources, targets, count, width):
        first = self.used
        self.used += count * len(sources)

        def copy(k, tile):
            at = pl.ds(pl.multiple_of(tile * width, width), width)
            number = first + k * count + tile
            return pltpu.make_async_copy(
                sources[k].at[:, at], targets[k].at[:, at], self.semaphores.at[number]
            )

        def start(tile):
            for k in range(len(sources)):
                copy(k, tile).start()

        def finish(tile, carry=0):
            for k in range(len(sources)):
                copy(k, tile).wait()
            return carry

        return start, finish

    def place(self, pieces, places, target):
        started = []
        for piece, place in zip(pieces, places):
            if place is None:
                started.append(self.start(piece, target))
            else:
                at = pl.multiple_of(place(lax.axis_index("dp")), 8)
                started.append(self.start(piece, target.at[pl.ds(at, piece.shape[0]), :]))
        return started


    def first_blocks(self, part, lead, outs):
        started = []
        for distance, out in zip((4 * lead, -3 * lead), outs):
            rows = out.shape[0]
            at = pl.multiple_of(ring_device_at(lax.axis_index("dp"), distance) * rows, 8)
            started.append(self.start(part.at[pl.ds(at, rows), :], out))
        return started


def wait(copies):
    for copy in copies:
        copy.wait()


def kernel_add(distances, part, *refs):
    count = len(distances)
    moved, outs, blocks, semaphores = refs[:count], refs[count : 2 * count], refs[2 * count], refs[-1]
    copies = Copies(semaphores)
    rows = outs[0].shape[0]
    arriving = []
    for k, distance in enumerate(distances):
        at = pl.multiple_of(ring_device_at(lax.axis_index("dp"), distance) * rows, 8)
        arriving.append(copies.start(part.at[pl.ds(at, rows), :], blocks.at[k]))
    step = 48 if rows % 48 == 0 else rows
    for k in range(count):
        arriving[k].wait()
        total, block, out = moved[k], blocks.at[k], outs[k]

        def add(i, carry):
            at = pl.ds(pl.multiple_of(i * step, step), step)
            out[at, :] = (total[at, :].astype(f32) + block[at, :].astype(f32)).astype(bf16)
            return carry

        lax.fori_loop(0, rows // step, add, 0)


def add_blocks(part, moved, distances):
    shape = moved[0].shape
    count = len(moved)
    vmem = pl.BlockSpec(memory_space=pltpu.VMEM)
    return pl.pallas_call(
        partial(kernel_add, distances),
        out_shape=[jax.ShapeDtypeStruct(shape, bf16)] * count,
        in_specs=[pl.BlockSpec(memory_space=pl.ANY)] + [vmem] * count,
        out_specs=[vmem] * count,
        scratch_shapes=[pltpu.VMEM((count,) + shape, bf16), pltpu.SemaphoreType.DMA((count,))],
        compiler_params=pltpu.CompilerParams(vmem_limit_bytes=8 << 20),
        cost_estimate=pl.CostEstimate(flops=0, bytes_accessed=1024, transcendentals=0),
        name="add_blocks",
    )(part, *moved)


def dot(a, b):
    return jnp.dot(a, b, preferred_element_type=f32)


def dot_last(a, b):
    return lax.dot_general(a, b, (((1,), (1,)), ((), ())), preferred_element_type=f32)


def dot_first(a, b):
    return lax.dot_general(a, b, (((0,), (0,)), ((), ())), preferred_element_type=f32)


def core_here():
    return lax.axis_index("mp") & 1


def pair_rows(total, pair):
    half = total // 2
    return pl.ds(pl.multiple_of(pair * half, half), half)


def image_rows(rows, image):
    return pl.ds(pl.multiple_of(image * rows, rows), rows)


def tiles(total):
    return total // 384 if total % 384 == 0 else 1


def chosen(index, values):
    shape = (values.shape[0], index.shape[1])
    select = lax.broadcasted_iota(jnp.int32, shape, 0) == index
    return dot_first(select.astype(f32).astype(bf16), values)


def head_values(values, local, depth, head, t):
    return values[:, t * local + head * depth : t * local + (head + 1) * depth]


def stacked_probs(values, local, depth, heads):
    scores = jnp.concatenate(
        [
            dot_last(
                head_values(values, local, depth, head, 0),
                head_values(values, local, depth, head, 1),
            )
            for head in range(heads)
        ],
        0,
    )
    scores = scores * depth ** (-0.5)
    exp_scores = jnp.exp(scores - jnp.max(scores, axis=-1, keepdims=True))
    return exp_scores / jnp.sum(exp_scores, axis=-1, keepdims=True)


def lane_start(columns):
    return columns // 128 * 128


def kernel_mods(cond, weights, out):
    for k in range(out.shape[0]):
        out[k] = dot(cond[...], weights[k].astype(bf16))


def kernel_silu(grads, weights, out):
    total = dot_last(grads[0], weights[0].astype(bf16))
    for k in range(1, grads.shape[0]):
        total = total + dot_last(grads[k], weights[k].astype(bf16))
    out[...] = total


def kernel_norm(tokens, index, own, normed):
    images, rows = index.shape
    core = core_here()

    def norm(image, carry):
        at = image_rows(rows, image)
        values = chosen(index[pl.ds(image, 1), :], tokens[image])
        normed[at, :] = layer_norm(values)[0]

        @pl.when(image // (images // 2) == core)
        def _():
            place = image_rows(rows, image - core * (images // 2))
            own[place, :] = values.astype(bf16)

        return carry

    lax.fori_loop(0, images, norm, 0)


def kernel_project(places, *refs):
    count = len(places)
    pieces, (given, mods) = refs[:count], refs[count : count + 2]
    outs, refs = refs[count + 2 : count + 4], refs[count + 4 :]
    full, normed, hidden, projected, semaphores = refs
    copies = Copies(semaphores)
    images = mods.shape[1]
    total = normed.shape[0]
    rows = total // images
    arriving = [copies.start(given, normed)]
    columns = full.shape[1]
    placed = copies.place([piece.at[:, :columns] for piece in pieces], places, full)
    wait(arriving)

    def norm(image, carry):
        at = image_rows(rows, image)
        scale = mods[1, pl.ds(image, 1), :]
        values = normed[at, :] * (1.0 + scale) + mods[0, pl.ds(image, 1), :]
        hidden[at, :] = values.astype(bf16)
        return carry

    lax.fori_loop(0, images, norm, 0)
    leaving = [copies.start(hidden, outs[0])]
    wait(placed)
    weights = full[:, : projected.shape[1]]

    def project(pair, carry):
        at = pair_rows(total, pair)
        projected[at, :] = dot(hidden[at, :], weights).astype(bf16)
        return carry

    lax.fori_loop(0, 2, project, 0)
    leaving.append(copies.start(projected, outs[1]))
    wait(leaving)


def kernel_attend(places, heads, rows, *refs):
    count = len(places)
    pieces, (given,) = refs[:count], refs[count : count + 1]
    outs, refs = refs[count + 1 : count + 4], refs[count + 4 :]
    full, projected, attended, own, other, semaphores = refs
    copies = Copies(semaphores)
    total = projected.shape[0]
    local = attended.shape[1]
    depth = local // heads
    core = core_here()
    start = lane_start(3 * local)
    arriving = [copies.start(given, projected)]
    placed = copies.place([piece.at[:, start:] for piece in pieces], places, full)
    wait(arriving)

    def attend(image, carry):
        at = image_rows(rows, image)
        values = projected[at, :]
        probs = stacked_probs(values, local, depth, heads).astype(bf16)
        attended[at, :] = jnp.concatenate(
            [
                dot(
                    probs[head * rows : (head + 1) * rows],
                    head_values(values, local, depth, head, 2),
                ).astype(bf16)
                for head in range(heads)
            ],
            1,
        )
        return carry

    lax.fori_loop(0, total // rows, attend, 0)
    leaving = [copies.start(attended, outs[0])]
    wait(placed)
    weights = full[:, 3 * local - start :]
    other[...] = dot_last(attended[pair_rows(total, 1 - core), :], weights).astype(bf16)
    leaving.append(copies.start(other, outs[2]))
    own[...] = dot_last(attended[pair_rows(total, core), :], weights)
    leaving.append(copies.start(own, outs[1]))
    wait(leaving)


def kernel_kept_grad(grads, index, mods, own, mlp_grad):
    core = core_here()
    images, rows = index.shape
    half = images // 2
    for place in range(images):
        pair = core if place < half else 1 - core
        image = pair * half + place % half
        values = chosen(index[pl.ds(image, 1), :], grads[image])
        at = slice(place * rows, (place + 1) * rows)
        if place < half:
            own[at, :] = values.astype(bf16)
        mlp_grad[at, :] = (mods[5, pl.ds(image, 1), :] * values).astype(bf16)


def kernel_second_norm(kept, mods, own, moved, residual, hidden_two):
    core = core_here()
    half = mods.shape[1] // 2
    rows = residual.shape[0] // half
    for image in range(half):
        at = slice(image * rows, (image + 1) * rows)
        where = core * half + image
        gate, shift, scale = [mods[k, pl.ds(where, 1), :] for k in (2, 3, 4)]
        attn_out = own[at, :].astype(f32) + moved[at, :].astype(f32)
        values = kept[at, :].astype(f32) + gate * attn_out
        residual[at, :] = values
        normed, _ = layer_norm(values)
        hidden_two[at, :] = (normed * (1.0 + scale) + shift).astype(bf16)


gelu_rate = math.sqrt(2.0 / math.pi)


def gelu_parts(values):
    tanh = jnp.tanh(gelu_rate * (values + 0.044715 * (values * values * values)))
    return 0.5 * (1.0 + tanh), tanh


def kernel_feed_forward(places, lead, *refs):
    count = len(places)
    pieces, (here, there, mlp) = refs[:count], refs[count : count + 3]
    outs, refs = refs[count + 3 : -7], refs[-7:]
    full, hidden_two, mlp_grad, pre_act, activated, fc2_grad, semaphores = refs
    copies = Copies(semaphores)
    half = here.shape[0]
    arriving = [copies.start(here, hidden_two.at[:half, :])]
    arriving.append(copies.start(there, hidden_two.at[half:, :]))
    arriving += copies.place(pieces, places, full)
    arriving.append(copies.start(mlp, mlp_grad))
    columns = full.shape[1]
    count = tiles(columns)
    width = columns // count
    leave, leave_end = copies.each([pre_act, activated, fc2_grad], outs[:3], count, width)
    wait(arriving)

    def product(tile, carry):
        at = pl.ds(pl.multiple_of(tile * width, width), width)
        values = dot(hidden_two[...], full[:, at])
        pre_act[:, at] = values
        low = (values * gelu_parts(values)[0]).astype(bf16)
        activated[:, at] = low
        fc2_grad[:, at] = dot_first(mlp_grad[...], low).astype(bf16)
        leave(tile)
        return carry

    lax.fori_loop(0, count, product, 0)
    leaving = copies.first_blocks(fc2_grad, lead, outs[3:])
    lax.fori_loop(0, count, leave_end, 0)
    wait(leaving)


def kernel_fc1_grad(lead, here, there, pre, *refs):
    outs, (hidden_two, pre_grad, fc1_grad, semaphores) = refs[:-4], refs[-4:]
    copies = Copies(semaphores)
    half = here.shape[0]
    arriving = [copies.start(here, hidden_two.at[:half, :])]
    arriving.append(copies.start(there, hidden_two.at[half:, :]))
    arriving.append(copies.start(pre, pre_grad))
    wait(arriving)
    columns = fc1_grad.shape[1]
    count = tiles(columns)
    width = columns // count
    leave, leave_end = copies.each([fc1_grad], outs[:1], count, width)

    def product(tile, carry):
        at = pl.ds(pl.multiple_of(tile * width, width), width)
        fc1_grad[:, at] = dot_first(hidden_two[...], pre_grad[:, at]).astype(bf16)
        leave(tile)
        return carry

    lax.fori_loop(0, count, product, 0)
    leaving = copies.first_blocks(fc1_grad, lead, outs[1:])
    lax.fori_loop(0, count, leave_end, 0)
    wait(leaving)


def kernel_feed_back(one_places, two_places, *refs):
    count = len(one_places)
    ones, twos, refs = refs[:count], refs[count : 2 * count], refs[2 * count :]
    (mlp, pre), outs, refs = refs[:2], refs[2:5], refs[5:]
    fc1, fc2, mlp_grad, pre_act, pre_grad, own, other, semaphores = refs
    copies = Copies(semaphores)
    arriving = [copies.start(mlp, mlp_grad)] + copies.place(twos, two_places, fc2)
    columns = fc2.shape[1]
    count = tiles(columns)
    width = columns // count
    values_in = [copies.start(pre, pre_act)]
    later = copies.place(ones, one_places, fc1)
    leave, leave_end = copies.each([pre_grad], outs[:1], count, width)
    wait(arriving + values_in)

    def product(tile, carry):
        at = pl.ds(pl.multiple_of(tile * width, width), width)
        gradient = dot(mlp_grad[...], fc2[:, at])
        values = pre_act[:, at]
        share, tanh = gelu_parts(values)
        slope = share + 0.5 * values * (1.0 - tanh * tanh) * gelu_rate * (
            1.0 + 3.0 * 0.044715 * (values * values)
        )
        pre_grad[:, at] = (gradient * slope).astype(bf16)
        leave(tile)
        return carry

    lax.fori_loop(0, count, product, 0)
    wait(later)
    back_product(copies, pre_grad, fc1, own, other, outs[1:])
    lax.fori_loop(0, count, leave_end, 0)


def back_product(copies, rows, weights, own, other, outs):
    half = own.shape[0]
    depth = weights.shape[0]
    count = tiles(depth)
    width = depth // count
    leave, leave_end = copies.each([own, other], outs, count, width)

    def product(tile, carry):
        at = pl.ds(pl.multiple_of(tile * width, width), width)
        values = dot_last(rows[...], weights[at, :])
        other[:, at] = values[half:].astype(bf16)
        own[:, at] = values[:half]
        leave(tile)
        return carry

    lax.fori_loop(0, count, product, 0)
    lax.fori_loop(0, count, leave_end, 0)


def kernel_feed_out(places, *refs):
    count = len(places)
    pieces, (low,) = refs[:count], refs[count : count + 1]
    outs, (full, activated, own, other, semaphores) = refs[count + 1 : count + 3], refs[count + 3 :]
    copies = Copies(semaphores)
    arriving = [copies.start(low, activated)] + copies.place(pieces, places, full)
    wait(arriving)
    back_product(copies, activated, full, own, other, outs)


def kernel_second_back(
    own, moved, residual, attn_own, attn_moved, grad, mods, residual_grad, attn_grad, sums
):
    core = core_here()
    half = mods.shape[1] // 2
    rows = residual.shape[0] // half
    for image in range(half):
        at = slice(image * rows, (image + 1) * rows)
        where = core * half + image
        gate, scale = [mods[k, pl.ds(where, 1), :] for k in (2, 4)]
        normed, inverse = layer_norm(residual[at, :])
        gradient = own[at, :].astype(f32) + moved[at, :].astype(f32)
        sums[1, pl.ds(image, 1), :] = jnp.sum(gradient, axis=0, keepdims=True)
        sums[2, pl.ds(image, 1), :] = jnp.sum(gradient * normed, axis=0, keepdims=True)
        values = grad[at, :].astype(f32) + norm_back(normed, inverse, gradient * (1.0 + scale))
        residual_grad[at, :] = values
        attn_out = attn_own[at, :].astype(f32) + attn_moved[at, :].astype(f32)
        sums[0, pl.ds(image, 1), :] = jnp.sum(values * attn_out, axis=0, keepdims=True)
        attn_grad[at, :] = (gate * values).astype(bf16)


def kernel_attention_back(places, heads, rows, lead, *refs):
    count = len(places)
    pieces, inputs = refs[:count], refs[count : count + 5]
    outs, refs = refs[count + 5 : -11], refs[-11:]
    here, there, projected_in, attended_in, hidden_in = inputs
    full, out_grad, projected, attended, hidden, back, grads, attn_grad, own, other = refs[:-1]
    copies = Copies(refs[-1])
    core = core_here()
    total = out_grad.shape[0]
    local = attended.shape[1]
    depth = local // heads
    arriving = [
        copies.start(here, out_grad.at[pair_rows(total, core), :]),
        copies.start(there, out_grad.at[pair_rows(total, 1 - core), :]),
    ] + copies.place(pieces, places, full)
    later = [copies.start(projected_in, projected), copies.start(attended_in, attended)]
    last = [copies.start(hidden_in, hidden)]
    wait(arriving)
    back[...] = dot(out_grad[...], full[:, 3 * local :]).astype(bf16)
    wait(later)

    def image_back(image, carry):
        at = image_rows(rows, image)
        values = projected[at, :]
        gradient = back[at, :]
        probs = stacked_probs(values, local, depth, heads)
        prob_grad = jnp.concatenate(
            [
                dot_last(
                    head_values(gradient, local, depth, head, 0),
                    head_values(values, local, depth, head, 2),
                )
                for head in range(heads)
            ],
            0,
        )
        score_grad = probs * (prob_grad - jnp.sum(prob_grad * probs, axis=-1, keepdims=True))
        score_grad = score_grad.astype(bf16)
        probs = probs.astype(bf16)
        parts = []
        for t in range(3):
            for head in range(heads):
                own_rows = slice(head * rows, (head + 1) * rows)
                if t == 0:
                    key = head_values(values, local, depth, head, 1)
                    part = dot(score_grad[own_rows], key) * depth ** (-0.5)
                elif t == 1:
                    query = head_values(values, local, depth, head, 0)
                    part = dot_first(score_grad[own_rows], query) * depth ** (-0.5)
                else:
                    part = dot_first(
                        probs[own_rows], head_values(gradient, local, depth, head, 0)
                    )
                parts.append(part.astype(bf16))
        grads[at, :] = jnp.concatenate(parts, 1)
        return carry

    lax.fori_loop(0, total // rows, image_back, 0)
    weights = full[:, : 3 * local]
    other[...] = dot_last(grads[pair_rows(total, 1 - core), :], weights).astype(bf16)
    leaving = [copies.start(other, outs[2])]
    own[...] = dot_last(grads[pair_rows(total, core), :], weights)
    leaving.append(copies.start(own, outs[1]))
    wait(last)
    attn_grad[:, 3 * local :] = dot_first(out_grad[...], attended[...]).astype(bf16)
    attn_grad[:, : 3 * local] = dot_first(hidden[...], grads[...]).astype(bf16)
    leaving.append(copies.start(attn_grad, outs[0]))
    leaving += copies.first_blocks(attn_grad, lead, outs[3:])
    wait(leaving)


def kernel_place(here, there, base, index, out):
    image = pl.program_id(0)
    rows = index.shape[2]
    half = here.shape[0] // rows
    pair = image // half
    at = image_rows(rows, image - pair * half)
    same = pair == core_here()
    values = jnp.where(same, here[at, :], there[at, :])
    select = lax.broadcasted_iota(jnp.int32, (base.shape[1], rows), 0) == index[0]
    select = select.astype(f32)
    kept = jnp.sum(select, axis=1, keepdims=True) > 0.5
    placed = dot(select.astype(bf16), values)
    out[0] = jnp.where(kept, placed, base[0].astype(f32)).astype(out.dtype)


def place_kept(here, there, base, index, dtype):
    images, seq, width = base.shape
    count = index.shape[1]
    whole = pl.BlockSpec(here.shape, lambda i: (0, 0))
    spec = pl.BlockSpec((1, seq, width), lambda i: (i, 0, 0))
    return pl.pallas_call(
        kernel_place,
        grid=(images,),
        out_shape=jax.ShapeDtypeStruct(base.shape, dtype),
        in_specs=[whole, whole, spec, pl.BlockSpec((1, 1, count), lambda i: (i, 0, 0))],
        out_specs=spec,
        cost_estimate=pl.CostEstimate(flops=0, bytes_accessed=1024, transcendentals=0),
        name="place_kept",
    )(here, there, base, index.reshape(images, 1, count))


def kernel_output(own, moved, residual, grad, mods, kept_out, sums):
    core = core_here()
    half = mods.shape[1] // 2
    rows = residual.shape[0] // half
    for image in range(half):
        at = slice(image * rows, (image + 1) * rows)
        mlp_out = own[at, :].astype(f32) + moved[at, :].astype(f32)
        gate = mods[5, pl.ds(core * half + image, 1), :]
        kept_out[at, :] = (residual[at, :] + gate * mlp_out).astype(bf16)
        sums[pl.ds(image, 1), :] = jnp.sum(
            grad[at, :].astype(f32) * mlp_out, axis=0, keepdims=True
        )


def kernel_first_back(
    own, moved, residual_grad, kept, mods, late, last, kept_grad, mine, partner
):
    me = lax.axis_index("mp")
    core = me & 1
    half = mods.shape[1] // 2
    rows = residual_grad.shape[0] // half
    local = mine.shape[2]
    lines = [[], []]
    for image in range(half):
        at = slice(image * rows, (image + 1) * rows)
        normed, inverse = layer_norm(kept[at, :].astype(f32))
        gradient = own[at, :].astype(f32) + moved[at, :].astype(f32)
        lines[0].append(jnp.sum(gradient, axis=0, keepdims=True))
        lines[1].append(jnp.sum(gradient * normed, axis=0, keepdims=True))
        scale = mods[1, pl.ds(core * half + image, 1), :]
        values = residual_grad[at, :] + norm_back(normed, inverse, gradient * (1.0 + scale))
        kept_grad[at, :] = values.astype(bf16)
    planes = [jnp.concatenate(line, 0) for line in lines]
    planes += [late[0], late[1], late[2], last[...]]
    for k, plane in enumerate(planes):
        blocks = [plane[:, j * local : (j + 1) * local] for j in range(4)]
        for out, device in ((mine, me), (partner, me ^ 1)):
            picked = blocks[0]
            for j in range(1, 4):
                picked = jnp.where(device == j, blocks[j], picked)
            out[k] = picked.astype(bf16)


def new_state(weight, moment, average, gradient, rate, steps):
    decay = (1.0 + steps) / (10.0 + steps)
    new_moment = momentum_rate * moment + gradient
    master = weight - rate * (gradient + momentum_rate * new_moment)
    return master, new_moment, decay * average + (1.0 - decay) * master


def summed(given):
    total = given[0][...].astype(f32)
    for ref in given[1:]:
        total = total + ref[...].astype(f32)
    return total


def one_step(rate, count, index, steps, *refs):
    given, refs = refs[:count], refs[count:]
    values = new_state(*[ref[...] for ref in refs[:3]], summed(given), rate, steps[0].astype(f32))
    for ref, value in zip(refs[3:], values):
        ref[...] = value


def attention_step(rate, count, index, steps, *refs):
    given, refs = refs[:count], refs[count:]
    gradient = summed(given)
    counts = steps[0].astype(f32)
    qkv, proj, qkv_out, proj_out = refs[:3], refs[3:6], refs[6:9], refs[9:]
    local = proj[0].shape[1]
    for t in range(3):
        values = new_state(
            *[ref[t] for ref in qkv], gradient[:, t * local : (t + 1) * local], rate, counts
        )
        for ref, value in zip(qkv_out, values):
            ref[t] = value
    values = new_state(*[ref[...] for ref in proj], gradient[:, 3 * local :], rate, counts)
    for ref, value in zip(proj_out, values):
        ref[...] = value


def step_weights(kernel, name, state, given, rate, steps):
    rows = given[0].shape[0]
    block = 48 if rows % 48 == 0 else rows
    count = rows // block

    def spec(x):
        if x.ndim == 3:
            return pl.BlockSpec((x.shape[0], block, x.shape[2]), lambda i, index: (0, i, 0))
        return pl.BlockSpec((block, x.shape[1]), lambda i, index: (i, 0))

    own = pl.BlockSpec((block, given[0].shape[1]), lambda i, index: (index[0] * count + i, 0))
    specs = [spec(x) for x in given[:2]] + [own] * (len(given) - 2)
    return pl.pallas_call(
        partial(kernel, rate, len(given)),
        grid_spec=pltpu.PrefetchScalarGridSpec(
            num_scalar_prefetch=1,
            grid=(count,),
            in_specs=[pl.BlockSpec(memory_space=pltpu.SMEM)] + specs + [spec(x) for x in state],
            out_specs=[spec(x) for x in state],
        ),
        out_shape=[jax.ShapeDtypeStruct(x.shape, f32) for x in state],
        cost_estimate=pl.CostEstimate(flops=0, bytes_accessed=1024, transcendentals=0),
        name=name,
    )(lax.axis_index("dp").astype(jnp.int32).reshape(1), steps, *given, *state)


def ada_step(rate, steps, cond, mods, weight, moment, average, master, new_moment, ema):
    counts = steps[0].astype(f32)
    for k in range(weight.shape[0]):
        gradient = dot_first(cond[...], mods[k])
        values = new_state(weight[k], moment[k], average[k], gradient, rate, counts)
        master[k], new_moment[k], ema[k] = values


def step_ada(weight, moment, average, cond, mods, rate, steps):
    count, rows, columns = weight.shape
    spec = pl.BlockSpec((2, rows, columns), lambda k: (k, 0, 0))
    return pl.pallas_call(
        partial(ada_step, rate),
        grid=(count // 2,),
        out_shape=[jax.ShapeDtypeStruct(weight.shape, f32)] * 3,
        in_specs=[
            pl.BlockSpec(memory_space=pltpu.SMEM),
            pl.BlockSpec(cond.shape, lambda k: (0, 0)),
            pl.BlockSpec((2,) + mods.shape[1:], lambda k: (k, 0, 0)),
        ]
        + [spec] * 3,
        out_specs=[spec] * 3,
        cost_estimate=pl.CostEstimate(flops=0, bytes_accessed=1024, transcendentals=0),
        name="step_ada",
    )(steps, cond, mods, weight, moment, average)


def per_device(
    tokens,
    condition,
    cotangent,
    kept_index,
    skip_index,
    step_count,
    ada_weight,
    qkv_weight,
    proj_weight,
    fc1_weight,
    fc2_weight,
    ada_moment,
    qkv_moment,
    proj_moment,
    fc1_moment,
    fc2_moment,
    ada_average,
    qkv_average,
    proj_average,
    fc1_average,
    fc2_average,
):
    images, seq, width = tokens.shape
    kept_count = kept_index.shape[1]
    own_d = ada_weight.shape[0]
    mods = ada_weight.shape[1]
    local = ada_weight.shape[2]
    units = fc1_weight.shape[1]
    local_heads = local // HEAD_DIM
    total = images * kept_count
    half = total // 2
    core = lax.axis_index("mp") % 2
    chip = lax.axis_index("mp") // 2
    dp_size = lax.axis_size("dp")
    index = lax.axis_index("dp")
    ring = dp_size == 8

    live = []

    def tick(extras, *hops):
        hops = [(one, sides) for one, sides in hops if one is not None]
        busy = [one for one, _ in hops]
        idle = [one for one in live if one not in busy]
        moving = tuple(one.start(sides) for one, sides in hops)
        work = tuple(extras())
        resting = tuple((one.held["a"], one.held["b"]) for one in idle)
        held, moved, resting = stage((work, moving, resting))
        for (one, sides), values in zip(hops, moved):
            one.finish(sides, values)
        for one, values in zip(idle, resting):
            one.finish("ab", values)
        return held

    rate = 0.02 / math.sqrt(images * dp_size * kept_count)

    attn_low = jnp.concatenate(
        [qkv_weight[0], qkv_weight[1], qkv_weight[2], proj_weight.T], 1
    ).astype(bf16)
    fc1_low = fc1_weight.astype(bf16)
    fc2_low = fc2_weight.T.astype(bf16)
    if ring:
        attn_ring, fc1_ring, fc2_ring = Gather(attn_low, 1), Gather(fc1_low, 1), Gather(fc2_low, -1)
    else:
        attn_ring = fc1_ring = fc2_ring = None
        attn_pieces, attn_places = [gather_plain(attn_low)], [None]
        fc1_pieces, fc1_places = [gather_plain(fc1_low)], [None]
        fc2_pieces, fc2_places = [gather_plain(fc2_low)], [None]
    block = [((width // 8, units), bf16)] * 2 if ring else []
    attn_block = [((width // 8, 4 * local), bf16)] * 2 if ring else []

    cond_float = condition.astype(f32)
    silu_cond = jax.nn.silu(cond_float).astype(bf16)
    small = silu_cond.reshape(images, dp_size, own_d)
    levels = len(dp_groups())
    def first_norm():
        return spread_round(small, 0, 0), *run(
            kernel_norm,
            "first_norm",
            [((half, width), bf16), ((total, width), f32)],
            (tokens, kept_index),
        )

    small, kept_own, normed = tick(first_norm, (attn_ring, "ab"))
    ada_state = [jnp.moveaxis(x, 1, 0) for x in (ada_weight, ada_moment, ada_average)]

    def rest_of_cond():
        values = small
        for level in range(1, levels):
            values = spread_round(values, 0, level)
        return (values,)

    (small,) = tick(rest_of_cond, (attn_ring, "ab"))

    def sum_of_mods():
        own = lax.dynamic_index_in_dim(small, index, 1, keepdims=False)
        (values,) = run(
            kernel_mods, "mods", [((mods, dp_size * images, local), f32)], (own, ada_state[0])
        )
        for level in reversed(range(1, levels)):
            values = sum_round(values, 1, level)
        return own, values

    cond_own, small = tick(sum_of_mods, (attn_ring, "ab"))
    (mod_local,) = tick(lambda: (sum_round(small, 1, 0),), (attn_ring, "a"))
    if ring:
        attn_pieces, attn_places = attn_ring.pieces()

    def all_mods():
        at_core = swap_core(mod_local)
        at_x = swap_x(mod_local)
        at_both = lax.ppermute(mod_local, "mp", [(j, j ^ 3) for j in range(4)])
        pairs = [join_pair(mod_local, at_core, core, 2), join_pair(at_x, at_both, core, 2)]
        return (
            jnp.where(chip == 0, jnp.concatenate(pairs, 2), jnp.concatenate(pairs[::-1], 2)),
        )

    (modulation,) = tick(all_mods, (fc1_ring, "ab"))


    def project():
        outs = [((total, width), bf16), ((total, 3 * local), bf16)]
        lanes = -(-3 * local // 128) * 128
        return run(
            partial(kernel_project, attn_places),
            "project",
            outs,
            (*attn_pieces, normed, modulation),
            [((width, lanes), bf16), ((total, width), f32)] + outs,
        )

    hidden, projected = tick(project, (fc2_ring, "ab"))

    def add_low(own, other):
        return (own + other.astype(f32)).astype(bf16)

    def attend():
        outs = [((total, local), bf16), ((half, width), f32), ((half, width), bf16)]
        lanes = 4 * local - lane_start(3 * local)
        return run(
            partial(kernel_attend, attn_places, local_heads, kept_count),
            "attend",
            outs,
            (*attn_pieces, projected),
            [((width, lanes), bf16), ((total, 3 * local), bf16)] + outs,
        )

    attended, own_part, other_part = tick(attend, (fc1_ring, "ab"))

    def attention_sums():
        own = add_low(own_part, swap_core(other_part))
        return own, swap_x(own), *kept_grads()


    def kept_grads():
        return run(
            kernel_kept_grad,
            "kept_grad",
            [((half, width), bf16), ((total, width), bf16)],
            (cotangent, kept_index, modulation),
        )

    attn_own, attn_moved, grad_own, mlp_grad = tick(
        attention_sums, (fc1_ring, "ab"), (fc2_ring, "ab")
    )

    def second_norm():
        values, low = run(
            kernel_second_norm,
            "second_norm",
            [((half, width), f32), ((half, width), bf16)],
            (kept_own, modulation, attn_own, attn_moved),
        )
        return values, low

    residual, hidden_here = tick(second_norm, (fc1_ring, "a"), (fc2_ring, "a"))
    hidden_here, hidden_there = tick(lambda: (hidden_here, swap_core(hidden_here)))
    if ring:
        fc1_pieces, fc1_places = fc1_ring.pieces()

    def feed_forward():
        outs = [((total, units), f32), ((total, units), bf16), ((width, units), bf16)]
        return run(
            partial(kernel_feed_forward, fc1_places, -1),
            "feed_forward",
            outs + block,
            (*fc1_pieces, hidden_here, hidden_there, mlp_grad),
            [((width, units), bf16), ((total, width), bf16), ((total, width), bf16)] + outs,
        )

    pre_act, activated, fc2_grad, *first = tick(feed_forward, (fc2_ring, "ba"))
    if ring:
        fc2_pieces, fc2_places = fc2_ring.pieces()
        fc2_sums = Scatter(fc2_grad, -1, first)
        live.append(fc2_sums)
    else:
        fc2_sums = fc1_sums = attn_sums = None

    def feed_back():
        outs = [((total, units), bf16), ((half, width), f32), ((half, width), bf16)]
        return run(
            partial(kernel_feed_back, fc1_places, fc2_places),
            "feed_back",
            outs,
            (*fc1_pieces, *fc2_pieces, mlp_grad, pre_act),
            [
                ((width, units), bf16),
                ((width, units), bf16),
                ((total, width), bf16),
                ((total, units), f32),
            ]
            + outs,
        )

    pre_grad, own_part, other_part = tick(feed_back, (fc2_sums, "ab"))
    moving = []

    def products():
        own_low = add_low(own_part, swap_core(other_part))
        outs = [((width, units), bf16)]
        grad, *first = run(
            partial(kernel_fc1_grad, -1),
            "fc1_grad",
            outs + block,
            (hidden_here, hidden_there, pre_grad),
            [((total, width), bf16), ((total, units), bf16)] + outs,
        )
        if ring:
            moving.append(Scatter(grad, -1, first))
            first = moving[0].start("ab")
        return own_low, swap_x(own_low), grad, activated, *first

    hidden_own, hidden_moved, fc1_grad, activated, *first = tick(
        products, (fc2_sums, "ab+")
    )
    if ring:
        (fc1_sums,) = moving
        fc1_sums.part = fc1_grad
        fc1_sums.finish("ab", first)
        live.append(fc1_sums)

    def second_back():
        values, low, lines = run(
            kernel_second_back,
            "second_back",
            [((half, width), f32), ((half, width), bf16), ((3, images // 2, width), f32)],
            (
                hidden_own,
                hidden_moved,
                residual,
                attn_own,
                attn_moved,
                grad_own,
                modulation,
            ),
        )
        outs = [((half, width), f32), ((half, width), bf16)]
        mlp = run(
            partial(kernel_feed_out, fc2_places),
            "feed_out",
            outs,
            (*fc2_pieces, activated),
            [((width, units), bf16), ((total, units), bf16)] + outs,
        )
        sums = ()
        if ring:
            held = stage((fc1_sums.held["a"], fc1_sums.held["b"], low))
            fc1_sums.finish("ab", held[:2])
            sums = fc1_sums.prepare("ab")
        return values, low, lines, *mlp, *sums

    residual_grad, out_here, late_mods, own_mlp, other_mlp, *sums = tick(
        second_back, (fc2_sums, "ab")
    )
    if ring:
        fc1_sums.finish("ab", sums)

    def between():
        sums = fc2_sums.prepare("a") if ring else ()
        low = add_low(own_mlp, swap_core(other_mlp))
        return out_here, swap_core(out_here), low, *sums

    out_here, out_there, mlp_own, *sums = tick(between)
    if ring:
        fc2_sums.finish("a", sums)

    def attention_back():
        outs = [((width, 4 * local), bf16), ((half, width), f32), ((half, width), bf16)]
        back = run(
            partial(kernel_attention_back, attn_places, local_heads, kept_count, 1),
            "attention_back",
            outs + attn_block,
            (*attn_pieces, out_here, out_there, projected, attended, hidden),
            [
                ((width, 4 * local), bf16),
                ((total, width), bf16),
                ((total, 3 * local), bf16),
                ((total, local), bf16),
                ((total, width), bf16),
                ((total, local), bf16),
                ((total, 3 * local), bf16),
            ]
            + outs,
        )
        return swap_x(mlp_own), *back

    mlp_moved, attn_grad, own_part, other_part, *first = tick(
        attention_back, (fc1_sums, "ab"), (fc2_sums, "a")
    )
    if ring:
        attn_sums = Scatter(attn_grad, 1, first)
        live.append(attn_sums)

    def output():
        return run(
            kernel_output,
            "output",
            [((half, width), bf16), ((images // 2, width), f32)],
            (mlp_own, mlp_moved, residual, grad_own, modulation),
        )

    back_own, mlp_moved = tick(
        lambda: (add_low(own_part, swap_core(other_part)), mlp_moved)
    )

    def attention_back_sums():
        given = fc2_sums.given() if ring else (scatter_plain(fc2_grad),)
        state = (fc2_weight.T, fc2_moment.T, fc2_average.T)
        new = step_weights(one_step, "step_fc2", state, given, rate, step_count)
        return swap_x(back_own), *output(), *new

    if ring:
        live.remove(fc2_sums)
    back_moved, kept_out, last_mods, fc2_master, fc2_momentum, fc2_ema = tick(
        attention_back_sums, (attn_sums, "ab+"), (fc1_sums, "ab")
    )

    def first_back():
        kept, mine, partner = run(
            kernel_first_back,
            "first_back",
            [
                ((half, width), bf16),
                ((mods, images // 2, local), bf16),
                ((mods, images // 2, local), bf16),
            ],
            (
                back_own,
                back_moved,
                residual_grad,
                kept_own,
                modulation,
                late_mods,
                last_mods,
            ),
        )
        return kept, join_pair(mine, swap_core(partner), core, 1), swap_core(kept_out)

    kept_grad, small, kept_there = tick(first_back, (attn_sums, "ab"))

    def first_spread():
        sums = fc1_sums.prepare("a") if ring else ()
        return spread_round(small, 1, 0), kept_there, kept_grad, *sums

    small, kept_there, kept_grad, *sums = tick(first_spread, (attn_sums, "ab"))
    if ring:
        fc1_sums.finish("a", sums)

    def last_spread():
        values = small
        for level in range(1, levels):
            values = spread_round(values, 1, level)
        out = place_kept(kept_out, kept_there, tokens, kept_index, bf16)
        return values, kept_grad, swap_core(kept_grad), out

    mod_grad_all, kept_grad, grad_there, block_out = tick(
        last_spread, (attn_sums, "a"), (fc1_sums, "a")
    )

    def silu_first():
        (part,) = run(
            kernel_silu, "silu", [((dp_size * images, own_d), f32)], (mod_grad_all, ada_state[0])
        )
        return part + swap_core(part), mod_grad_all, kept_grad

    silu_part, mod_grad_all, kept_grad = tick(silu_first)

    def silu_second():
        given = fc1_sums.given() if ring else (scatter_plain(fc1_grad),)
        state = (fc1_weight, fc1_moment, fc1_average)
        new = step_weights(one_step, "step_fc1", state, given, rate, step_count)
        new += step_ada(*ada_state, cond_own, mod_grad_all, rate, step_count)
        return silu_part + swap_x(silu_part), *new

    silu_part, fc1_master, fc1_momentum, fc1_ema, *ada_new = tick(silu_second)
    silu_blocks = silu_part.reshape(dp_size, images, own_d)

    def silu_third():
        blocks = silu_blocks
        for level in reversed(range(1, levels)):
            blocks = turn_round(blocks, level)
        given = attn_sums.given() if ring else (scatter_plain(attn_grad),)
        state = (qkv_weight, qkv_moment, qkv_average)
        state += (proj_weight.T, proj_moment.T, proj_average.T)
        new = step_weights(attention_step, "step_attention", state, given, rate, step_count)
        return blocks, kept_grad, *new

    silu_blocks, kept_grad, *attn_new = tick(silu_third)
    qkv_master, qkv_momentum, qkv_ema, proj_master, proj_momentum, proj_ema = attn_new
    tokens_grad = place_kept(kept_grad, grad_there, cotangent, kept_index, f32)
    silu_blocks = in_order(turn_round(silu_blocks, 0))
    ada_master, ada_momentum, ada_ema = [jnp.moveaxis(x, 0, 1) for x in ada_new]
    silu_grad = jnp.moveaxis(silu_blocks, 0, 1).reshape(images, width)
    silu_value, silu_pull = jax.vjp(jax.nn.silu, cond_float)
    condition_grad = silu_pull(silu_grad)[0]
    return (
        block_out,
        tokens_grad,
        condition_grad,
        ada_master,
        qkv_master,
        proj_master.T,
        fc1_master,
        fc2_master.T,
        ada_momentum,
        qkv_momentum,
        proj_momentum.T,
        fc1_momentum,
        fc2_momentum.T,
        ada_ema,
        qkv_ema,
        proj_ema.T,
        fc1_ema,
        fc2_ema.T,
    )


def solution(mesh):
    weights = (
        P("dp", None, "mp"),
        P(None, "dp", "mp"),
        P("mp", "dp"),
        P("dp", "mp"),
        P("mp", "dp"),
    )
    rows = P("dp", None, None)
    pairs = P("dp", None)
    return jax.shard_map(
        per_device,
        mesh=mesh,
        in_specs=(rows, pairs, rows, pairs, pairs, P()) + weights * 3,
        out_specs=(rows, rows, pairs) + weights * 3,
        check_vma=False,
    )
```

```python
from functools import partial
import math

import jax
import jax.numpy as jnp
from jax import lax
from jax.experimental import pallas as pl
from jax.experimental.pallas import tpu as pltpu
from jax.sharding import PartitionSpec as P

HEAD_DIM = 72

epsilon = 1e-06
momentum_rate = 0.9

f32 = jnp.float32
bf16 = jnp.bfloat16


def layer_norm(values):
    centered = values - jnp.mean(values, axis=-1, keepdims=True)
    inverse = lax.rsqrt(jnp.mean(centered * centered, axis=-1, keepdims=True) + epsilon)
    return (centered * inverse, inverse)


def norm_back(normed, inverse, gradient):
    return inverse * (
        gradient
        - jnp.mean(gradient, axis=-1, keepdims=True)
        - normed * jnp.mean(gradient * normed, axis=-1, keepdims=True)
    )


def swap_core(values):
    return lax.ppermute(values, "mp", [(j, j ^ 1) for j in range(4)])


def swap_x(values):
    return lax.ppermute(values, "mp", [(j, j ^ 2) for j in range(4)])


def join_pair(own, other, core, axis=0):
    return jnp.where(
        core == 0,
        jnp.concatenate([own, other], axis),
        jnp.concatenate([other, own], axis),
    )


def spread_pair(own, core):
    return join_pair(own, swap_core(own), core)


def swap_dp(values, bit):
    size = lax.axis_size("dp")
    return lax.ppermute(values, "dp", [(i, i ^ bit) for i in range(size)])


def dp_groups():
    size = lax.axis_size("dp")
    return [4] + [2] * (size.bit_length() - 3)


def spread_round(values, axis, level):
    groups = dp_groups()
    step = math.prod(groups[:level])
    others = [swap_dp(values, step * b) for b in range(1, groups[level])]
    return jnp.concatenate([values] + others, axis)


def sum_round(values, axis, level):
    groups = dp_groups()
    step = math.prod(groups[:level])
    blocks = jnp.split(values, groups[level], axis)
    total = blocks[0]
    for b in range(1, groups[level]):
        total = total + swap_dp(blocks[b], step * b)
    return total


def turn_round(values, level):
    groups = dp_groups()
    step = math.prod(groups[:level])
    shape = values.shape
    values = values.reshape((-1, groups[level], step) + shape[1:])
    blocks = [values[:, b] for b in range(groups[level])]
    blocks = [blocks[0]] + [swap_dp(blocks[b], step * b) for b in range(1, groups[level])]
    return jnp.stack(blocks, 1).reshape(shape)


def in_order(values):
    index = lax.axis_index("dp")
    shape = values.shape
    count = shape[0].bit_length() - 1
    values = values.reshape((2,) * count + shape[1:])
    for axis in range(count):
        values = jnp.where((index >> (count - 1 - axis)) & 1, jnp.flip(values, axis), values)
    return values.reshape(shape)


def ring_tables():
    cycle = [0, 2, 4, 6, 7, 5, 3, 1]
    clockwise = [(cycle[i], cycle[(i + 1) % 8]) for i in range(8)]
    return clockwise, [(b, a) for a, b in clockwise]


def ring_place_of(index):
    return jnp.where((index & 1) == 0, index >> 1, 7 - (index >> 1))


def ring_device(place):
    place = lax.rem(place, 8)
    return jnp.where(place < 4, 2 * place, 2 * (7 - place) + 1)


def hop(values, direction):
    clockwise, backward = ring_tables()
    return lax.ppermute(values, "dp", clockwise if direction > 0 else backward)


def ring_device_at(index, distance):
    return ring_device(ring_place_of(index) + distance + 8)


class Gather:
    def __init__(self, shard, lead):
        self.lead = lead
        self.shard = shard
        self.ahead = [shard]
        self.behind = [shard]

    def start(self, sides):
        moving = []
        if "a" in sides:
            moving.append(hop(self.ahead[-1], self.lead))
        if "b" in sides:
            moving.append(hop(self.behind[-1], -self.lead))
        return tuple(moving)

    def finish(self, sides, moved):
        moved = list(moved)
        if "a" in sides:
            self.ahead.append(moved.pop(0))
        if "b" in sides:
            self.behind.append(moved.pop(0))

    def pieces(self):
        rows = self.shard.shape[0]
        distances = [-self.lead * k for k in range(5)] + [self.lead * k for k in range(1, 4)]
        places = [
            partial(lambda distance, index: ring_device_at(index, distance) * rows, distance)
            for distance in distances
        ]
        return self.ahead + self.behind[1:], places


class Scatter:
    def __init__(self, part, lead, first):
        self.part, self.lead = part, lead
        self.rows = part.shape[0] // 8
        self.left = {"a": 4, "b": 3}
        self.added = {"a": False, "b": False}
        self.held = dict(zip("ab", first))

    def signs(self):
        return {"a": self.lead, "b": -self.lead}

    def add(self, values):
        full = {"a": 4, "b": 3}
        adding = [k for k in values if 0 < self.left[k] < full[k] and not self.added[k]]
        if adding:
            signs = self.signs()
            sums = add_blocks(
                self.part,
                [values[k] for k in adding],
                [signs[k] * self.left[k] for k in adding],
            )
            values = {**values, **dict(zip(adding, sums))}
            for k in adding:
                self.added[k] = True
        return values

    def prepare(self, sides):
        values = self.add({k: self.held[k] for k in sides})
        return tuple(values[k] for k in sides)

    def start(self, sides):
        values = self.add({k: self.held[k] for k in sides if k in "ab"})
        signs = self.signs()
        for k in values:
            self.left[k] -= 1
            self.added[k] = False
        values = {k: hop(value, signs[k]) for k, value in values.items()}
        if "+" in sides:
            values = self.add(values)
        return tuple(values.values())

    def finish(self, sides, moved):
        self.held.update(zip(sides, moved))

    def given(self):
        return self.held["a"], self.held["b"], self.part


def gather_plain(shard):
    return lax.all_gather(shard, "dp", axis=0, tiled=True)


def scatter_plain(part):
    return lax.psum_scatter(part.astype(f32), "dp", scatter_dimension=0, tiled=True)


stage = lax.optimization_barrier


def run(kernel, name, outs, args, scratch=None):
    vmem = pl.BlockSpec(memory_space=pltpu.VMEM)
    anywhere = pl.BlockSpec(memory_space=pl.ANY)
    by_copy = scratch is not None
    return pl.pallas_call(
        kernel,
        out_shape=[jax.ShapeDtypeStruct(shape, dtype) for shape, dtype in outs],
        in_specs=[vmem if not by_copy or x.size < 40000 else anywhere for x in args],
        out_specs=[anywhere if by_copy else vmem] * len(outs),
        scratch_shapes=[pltpu.VMEM(shape, dtype) for shape, dtype in scratch]
        + [pltpu.SemaphoreType.DMA((48,))]
        if by_copy
        else [],
        compiler_params=pltpu.CompilerParams(vmem_limit_bytes=20 << 20),
        cost_estimate=pl.CostEstimate(flops=0, bytes_accessed=1024, transcendentals=0),
        name=name,
    )(*args)


class Copies:
    def __init__(self, semaphores):
        self.semaphores = semaphores
        self.used = 0

    def start(self, source, target):
        copy = pltpu.make_async_copy(source, target, self.semaphores.at[self.used])
        self.used += 1
        copy.start()
        return copy

    def each(self, sources, targets, count, width):
        first = self.used
        self.used += count * len(sources)

        def copy(k, tile):
            at = pl.ds(pl.multiple_of(tile * width, width), width)
            number = first + k * count + tile
            return pltpu.make_async_copy(
                sources[k].at[:, at], targets[k].at[:, at], self.semaphores.at[number]
            )

        def start(tile):
            for k in range(len(sources)):
                copy(k, tile).start()

        def finish(tile, carry=0):
            for k in range(len(sources)):
                copy(k, tile).wait()
            return carry

        return start, finish

    def place(self, pieces, places, target):
        started = []
        for piece, place in zip(pieces, places):
            if place is None:
                started.append(self.start(piece, target))
            else:
                at = pl.multiple_of(place(lax.axis_index("dp")), 8)
                started.append(self.start(piece, target.at[pl.ds(at, piece.shape[0]), :]))
        return started


    def first_blocks(self, part, lead, outs):
        started = []
        for distance, out in zip((4 * lead, -3 * lead), outs):
            rows = out.shape[0]
            at = pl.multiple_of(ring_device_at(lax.axis_index("dp"), distance) * rows, 8)
            started.append(self.start(part.at[pl.ds(at, rows), :], out))
        return started


def wait(copies):
    for copy in copies:
        copy.wait()


def kernel_add(distances, part, *refs):
    count = len(distances)
    moved, outs, blocks, semaphores = refs[:count], refs[count : 2 * count], refs[2 * count], refs[-1]
    copies = Copies(semaphores)
    rows = outs[0].shape[0]
    arriving = []
    for k, distance in enumerate(distances):
        at = pl.multiple_of(ring_device_at(lax.axis_index("dp"), distance) * rows, 8)
        arriving.append(copies.start(part.at[pl.ds(at, rows), :], blocks.at[k]))
    step = 48 if rows % 48 == 0 else rows
    for k in range(count):
        arriving[k].wait()
        total, block, out = moved[k], blocks.at[k], outs[k]

        def add(i, carry):
            at = pl.ds(pl.multiple_of(i * step, step), step)
            out[at, :] = (total[at, :].astype(f32) + block[at, :].astype(f32)).astype(bf16)
            return carry

        lax.fori_loop(0, rows // step, add, 0)


def add_blocks(part, moved, distances):
    shape = moved[0].shape
    count = len(moved)
    vmem = pl.BlockSpec(memory_space=pltpu.VMEM)
    return pl.pallas_call(
        partial(kernel_add, distances),
        out_shape=[jax.ShapeDtypeStruct(shape, bf16)] * count,
        in_specs=[pl.BlockSpec(memory_space=pl.ANY)] + [vmem] * count,
        out_specs=[vmem] * count,
        scratch_shapes=[pltpu.VMEM((count,) + shape, bf16), pltpu.SemaphoreType.DMA((count,))],
        compiler_params=pltpu.CompilerParams(vmem_limit_bytes=8 << 20),
        cost_estimate=pl.CostEstimate(flops=0, bytes_accessed=1024, transcendentals=0),
        name="add_blocks",
    )(part, *moved)


def dot(a, b):
    return jnp.dot(a, b, preferred_element_type=f32)


def dot_last(a, b):
    return lax.dot_general(a, b, (((1,), (1,)), ((), ())), preferred_element_type=f32)


def dot_first(a, b):
    return lax.dot_general(a, b, (((0,), (0,)), ((), ())), preferred_element_type=f32)


def core_here():
    return lax.axis_index("mp") & 1


def pair_rows(total, pair):
    half = total // 2
    return pl.ds(pl.multiple_of(pair * half, half), half)


def image_rows(rows, image):
    return pl.ds(pl.multiple_of(image * rows, rows), rows)


def tiles(total):
    return total // 384 if total % 384 == 0 else 1


def chosen(index, values):
    shape = (values.shape[0], index.shape[1])
    select = lax.broadcasted_iota(jnp.int32, shape, 0) == index
    return dot_first(select.astype(f32).astype(bf16), values)


def head_values(values, local, depth, head, t):
    return values[:, t * local + head * depth : t * local + (head + 1) * depth]


def stacked_probs(values, local, depth, heads):
    scores = jnp.concatenate(
        [
            dot_last(
                head_values(values, local, depth, head, 0),
                head_values(values, local, depth, head, 1),
            )
            for head in range(heads)
        ],
        0,
    )
    scores = scores * depth ** (-0.5)
    exp_scores = jnp.exp(scores - jnp.max(scores, axis=-1, keepdims=True))
    return exp_scores / jnp.sum(exp_scores, axis=-1, keepdims=True)


def lane_start(columns):
    return columns // 128 * 128


def kernel_mods(cond, weights, out):
    for k in range(out.shape[0]):
        out[k] = dot(cond[...], weights[k].astype(bf16))


def kernel_silu(grads, weights, out):
    total = dot_last(grads[0], weights[0].astype(bf16))
    for k in range(1, grads.shape[0]):
        total = total + dot_last(grads[k], weights[k].astype(bf16))
    out[...] = total


def kernel_norm(tokens, index, own, normed):
    images, rows = index.shape
    core = core_here()

    def norm(image, carry):
        at = image_rows(rows, image)
        values = chosen(index[pl.ds(image, 1), :], tokens[image])
        normed[at, :] = layer_norm(values)[0]

        @pl.when(image // (images // 2) == core)
        def _():
            place = image_rows(rows, image - core * (images // 2))
            own[place, :] = values.astype(bf16)

        return carry

    lax.fori_loop(0, images, norm, 0)


def kernel_project(places, *refs):
    count = len(places)
    pieces, (given, mods) = refs[:count], refs[count : count + 2]
    outs, refs = refs[count + 2 : count + 4], refs[count + 4 :]
    full, normed, hidden, projected, semaphores = refs
    copies = Copies(semaphores)
    images = mods.shape[1]
    total = normed.shape[0]
    rows = total // images
    arriving = [copies.start(given, normed)]
    columns = full.shape[1]
    placed = copies.place([piece.at[:, :columns] for piece in pieces], places, full)
    wait(arriving)

    def norm(image, carry):
        at = image_rows(rows, image)
        scale = mods[1, pl.ds(image, 1), :]
        values = normed[at, :] * (1.0 + scale) + mods[0, pl.ds(image, 1), :]
        hidden[at, :] = values.astype(bf16)
        return carry

    lax.fori_loop(0, images, norm, 0)
    leaving = [copies.start(hidden, outs[0])]
    wait(placed)
    weights = full[:, : projected.shape[1]]

    def project(pair, carry):
        at = pair_rows(total, pair)
        projected[at, :] = dot(hidden[at, :], weights).astype(bf16)
        return carry

    lax.fori_loop(0, 2, project, 0)
    leaving.append(copies.start(projected, outs[1]))
    wait(leaving)


def kernel_attend(places, heads, rows, *refs):
    count = len(places)
    pieces, (given,) = refs[:count], refs[count : count + 1]
    outs, refs = refs[count + 1 : count + 4], refs[count + 4 :]
    full, projected, attended, own, other, semaphores = refs
    copies = Copies(semaphores)
    total = projected.shape[0]
    local = attended.shape[1]
    depth = local // heads
    core = core_here()
    start = lane_start(3 * local)
    arriving = [copies.start(given, projected)]
    placed = copies.place([piece.at[:, start:] for piece in pieces], places, full)
    wait(arriving)

    def attend(image, carry):
        at = image_rows(rows, image)
        values = projected[at, :]
        probs = stacked_probs(values, local, depth, heads).astype(bf16)
        attended[at, :] = jnp.concatenate(
            [
                dot(
                    probs[head * rows : (head + 1) * rows],
                    head_values(values, local, depth, head, 2),
                ).astype(bf16)
                for head in range(heads)
            ],
            1,
        )
        return carry

    lax.fori_loop(0, total // rows, attend, 0, unroll=True)
    leaving = [copies.start(attended, outs[0])]
    wait(placed)
    weights = full[:, 3 * local - start :]
    other[...] = dot_last(attended[pair_rows(total, 1 - core), :], weights).astype(bf16)
    leaving.append(copies.start(other, outs[2]))
    own[...] = dot_last(attended[pair_rows(total, core), :], weights)
    leaving.append(copies.start(own, outs[1]))
    wait(leaving)


def kernel_kept_grad(grads, index, mods, own, mlp_grad):
    core = core_here()
    images, rows = index.shape
    half = images // 2
    for place in range(images):
        pair = core if place < half else 1 - core
        image = pair * half + place % half
        values = chosen(index[pl.ds(image, 1), :], grads[image])
        at = slice(place * rows, (place + 1) * rows)
        if place < half:
            own[at, :] = values.astype(bf16)
        mlp_grad[at, :] = (mods[5, pl.ds(image, 1), :] * values).astype(bf16)


def kernel_second_norm(kept, mods, own, moved, residual, hidden_two):
    core = core_here()
    half = mods.shape[1] // 2
    rows = residual.shape[0] // half
    for image in range(half):
        at = slice(image * rows, (image + 1) * rows)
        where = core * half + image
        gate, shift, scale = [mods[k, pl.ds(where, 1), :] for k in (2, 3, 4)]
        attn_out = own[at, :].astype(f32) + moved[at, :].astype(f32)
        values = kept[at, :].astype(f32) + gate * attn_out
        residual[at, :] = values
        normed, _ = layer_norm(values)
        hidden_two[at, :] = (normed * (1.0 + scale) + shift).astype(bf16)


gelu_rate = math.sqrt(2.0 / math.pi)


def gelu_parts(values):
    tanh = jnp.tanh(gelu_rate * (values + 0.044715 * (values * values * values)))
    return 0.5 * (1.0 + tanh), tanh


def kernel_feed_forward(places, lead, *refs):
    count = len(places)
    pieces, (here, there, mlp) = refs[:count], refs[count : count + 3]
    outs, refs = refs[count + 3 : -7], refs[-7:]
    full, hidden_two, mlp_grad, pre_act, activated, fc2_grad, semaphores = refs
    copies = Copies(semaphores)
    half = here.shape[0]
    arriving = [copies.start(here, hidden_two.at[:half, :])]
    arriving.append(copies.start(there, hidden_two.at[half:, :]))
    arriving += copies.place(pieces, places, full)
    arriving.append(copies.start(mlp, mlp_grad))
    columns = full.shape[1]
    count = tiles(columns)
    width = columns // count
    leave, leave_end = copies.each([pre_act, activated, fc2_grad], outs[:3], count, width)
    wait(arriving)

    def product(tile, carry):
        at = pl.ds(pl.multiple_of(tile * width, width), width)
        values = dot(hidden_two[...], full[:, at])
        pre_act[:, at] = values
        low = (values * gelu_parts(values)[0]).astype(bf16)
        activated[:, at] = low
        fc2_grad[:, at] = dot_first(mlp_grad[...], low).astype(bf16)
        leave(tile)
        return carry

    lax.fori_loop(0, count, product, 0)
    leaving = copies.first_blocks(fc2_grad, lead, outs[3:])
    lax.fori_loop(0, count, leave_end, 0)
    wait(leaving)


def kernel_fc1_grad(lead, here, there, pre, *refs):
    outs, (hidden_two, pre_grad, fc1_grad, semaphores) = refs[:-4], refs[-4:]
    copies = Copies(semaphores)
    half = here.shape[0]
    arriving = [copies.start(here, hidden_two.at[:half, :])]
    arriving.append(copies.start(there, hidden_two.at[half:, :]))
    arriving.append(copies.start(pre, pre_grad))
    wait(arriving)
    columns = fc1_grad.shape[1]
    count = tiles(columns)
    width = columns // count
    leave, leave_end = copies.each([fc1_grad], outs[:1], count, width)

    def product(tile, carry):
        at = pl.ds(pl.multiple_of(tile * width, width), width)
        fc1_grad[:, at] = dot_first(hidden_two[...], pre_grad[:, at]).astype(bf16)
        leave(tile)
        return carry

    lax.fori_loop(0, count, product, 0)
    leaving = copies.first_blocks(fc1_grad, lead, outs[1:])
    lax.fori_loop(0, count, leave_end, 0)
    wait(leaving)


def kernel_feed_back(one_places, two_places, *refs):
    count = len(one_places)
    ones, twos, refs = refs[:count], refs[count : 2 * count], refs[2 * count :]
    (mlp, pre), outs, refs = refs[:2], refs[2:5], refs[5:]
    fc1, fc2, mlp_grad, pre_act, pre_grad, own, other, semaphores = refs
    copies = Copies(semaphores)
    arriving = [copies.start(mlp, mlp_grad)] + copies.place(twos, two_places, fc2)
    columns = fc2.shape[1]
    count = tiles(columns)
    width = columns // count
    values_in = [copies.start(pre, pre_act)]
    later = copies.place(ones, one_places, fc1)
    leave, leave_end = copies.each([pre_grad], outs[:1], count, width)
    wait(arriving + values_in)

    def product(tile, carry):
        at = pl.ds(pl.multiple_of(tile * width, width), width)
        gradient = dot(mlp_grad[...], fc2[:, at])
        values = pre_act[:, at]
        share, tanh = gelu_parts(values)
        slope = share + 0.5 * values * (1.0 - tanh * tanh) * gelu_rate * (
            1.0 + 3.0 * 0.044715 * (values * values)
        )
        pre_grad[:, at] = (gradient * slope).astype(bf16)
        leave(tile)
        return carry

    lax.fori_loop(0, count, product, 0)
    wait(later)
    back_product(copies, pre_grad, fc1, own, other, outs[1:])
    lax.fori_loop(0, count, leave_end, 0)


def back_product(copies, rows, weights, own, other, outs):
    half = own.shape[0]
    depth = weights.shape[0]
    count = tiles(depth)
    width = depth // count
    leave, leave_end = copies.each([own, other], outs, count, width)

    def product(tile, carry):
        at = pl.ds(pl.multiple_of(tile * width, width), width)
        values = dot_last(rows[...], weights[at, :])
        other[:, at] = values[half:].astype(bf16)
        own[:, at] = values[:half]
        leave(tile)
        return carry

    lax.fori_loop(0, count, product, 0)
    lax.fori_loop(0, count, leave_end, 0)


def kernel_feed_out(places, *refs):
    count = len(places)
    pieces, (low,) = refs[:count], refs[count : count + 1]
    outs, (full, activated, own, other, semaphores) = refs[count + 1 : count + 3], refs[count + 3 :]
    copies = Copies(semaphores)
    arriving = [copies.start(low, activated)] + copies.place(pieces, places, full)
    wait(arriving)
    back_product(copies, activated, full, own, other, outs)


def kernel_second_back(
    own, moved, residual, attn_own, attn_moved, grad, mods, residual_grad, attn_grad, sums
):
    core = core_here()
    half = mods.shape[1] // 2
    rows = residual.shape[0] // half
    for image in range(half):
        at = slice(image * rows, (image + 1) * rows)
        where = core * half + image
        gate, scale = [mods[k, pl.ds(where, 1), :] for k in (2, 4)]
        normed, inverse = layer_norm(residual[at, :])
        gradient = own[at, :].astype(f32) + moved[at, :].astype(f32)
        sums[1, pl.ds(image, 1), :] = jnp.sum(gradient, axis=0, keepdims=True)
        sums[2, pl.ds(image, 1), :] = jnp.sum(gradient * normed, axis=0, keepdims=True)
        values = grad[at, :].astype(f32) + norm_back(normed, inverse, gradient * (1.0 + scale))
        residual_grad[at, :] = values
        attn_out = attn_own[at, :].astype(f32) + attn_moved[at, :].astype(f32)
        sums[0, pl.ds(image, 1), :] = jnp.sum(values * attn_out, axis=0, keepdims=True)
        attn_grad[at, :] = (gate * values).astype(bf16)


def kernel_attention_back(places, heads, rows, lead, *refs):
    count = len(places)
    pieces, inputs = refs[:count], refs[count : count + 5]
    outs, refs = refs[count + 5 : -11], refs[-11:]
    here, there, projected_in, attended_in, hidden_in = inputs
    full, out_grad, projected, attended, hidden, back, grads, attn_grad, own, other = refs[:-1]
    copies = Copies(refs[-1])
    core = core_here()
    total = out_grad.shape[0]
    local = attended.shape[1]
    depth = local // heads
    arriving = [
        copies.start(here, out_grad.at[pair_rows(total, core), :]),
        copies.start(there, out_grad.at[pair_rows(total, 1 - core), :]),
    ] + copies.place(pieces, places, full)
    later = [copies.start(projected_in, projected), copies.start(attended_in, attended)]
    last = [copies.start(hidden_in, hidden)]
    wait(arriving)
    back[...] = dot(out_grad[...], full[:, 3 * local :]).astype(bf16)
    wait(later)

    def image_back(image, carry):
        at = image_rows(rows, image)
        values = projected[at, :]
        gradient = back[at, :]
        probs = stacked_probs(values, local, depth, heads)
        prob_grad = jnp.concatenate(
            [
                dot_last(
                    head_values(gradient, local, depth, head, 0),
                    head_values(values, local, depth, head, 2),
                )
                for head in range(heads)
            ],
            0,
        )
        score_grad = probs * (prob_grad - jnp.sum(prob_grad * probs, axis=-1, keepdims=True))
        score_grad = score_grad.astype(bf16)
        probs = probs.astype(bf16)
        parts = []
        for t in range(3):
            for head in range(heads):
                own_rows = slice(head * rows, (head + 1) * rows)
                if t == 0:
                    key = head_values(values, local, depth, head, 1)
                    part = dot(score_grad[own_rows], key) * depth ** (-0.5)
                elif t == 1:
                    query = head_values(values, local, depth, head, 0)
                    part = dot_first(score_grad[own_rows], query) * depth ** (-0.5)
                else:
                    part = dot_first(
                        probs[own_rows], head_values(gradient, local, depth, head, 0)
                    )
                parts.append(part.astype(bf16))
        grads[at, :] = jnp.concatenate(parts, 1)
        return carry

    lax.fori_loop(0, total // rows, image_back, 0, unroll=True)
    weights = full[:, : 3 * local]
    other[...] = dot_last(grads[pair_rows(total, 1 - core), :], weights).astype(bf16)
    leaving = [copies.start(other, outs[2])]
    own[...] = dot_last(grads[pair_rows(total, core), :], weights)
    leaving.append(copies.start(own, outs[1]))
    wait(last)
    attn_grad[:, 3 * local :] = dot_first(out_grad[...], attended[...]).astype(bf16)
    attn_grad[:, : 3 * local] = dot_first(hidden[...], grads[...]).astype(bf16)
    leaving.append(copies.start(attn_grad, outs[0]))
    leaving += copies.first_blocks(attn_grad, lead, outs[3:])
    wait(leaving)


def kernel_place(here, there, base, index, out):
    image = pl.program_id(0)
    rows = index.shape[2]
    half = here.shape[0] // rows
    pair = image // half
    at = image_rows(rows, image - pair * half)
    same = pair == core_here()
    values = jnp.where(same, here[at, :], there[at, :])
    select = lax.broadcasted_iota(jnp.int32, (base.shape[1], rows), 0) == index[0]
    select = select.astype(f32)
    kept = jnp.sum(select, axis=1, keepdims=True) > 0.5
    placed = dot(select.astype(bf16), values)
    out[0] = jnp.where(kept, placed, base[0].astype(f32)).astype(out.dtype)


def place_kept(here, there, base, index, dtype):
    images, seq, width = base.shape
    count = index.shape[1]
    whole = pl.BlockSpec(here.shape, lambda i: (0, 0))
    spec = pl.BlockSpec((1, seq, width), lambda i: (i, 0, 0))
    return pl.pallas_call(
        kernel_place,
        grid=(images,),
        out_shape=jax.ShapeDtypeStruct(base.shape, dtype),
        in_specs=[whole, whole, spec, pl.BlockSpec((1, 1, count), lambda i: (i, 0, 0))],
        out_specs=spec,
        compiler_params=pltpu.CompilerParams(vmem_limit_bytes=14 << 20),
        cost_estimate=pl.CostEstimate(flops=0, bytes_accessed=1024, transcendentals=0),
        name="place_kept",
    )(here, there, base, index.reshape(images, 1, count))


def kernel_output(own, moved, residual, grad, mods, kept_out, sums):
    core = core_here()
    half = mods.shape[1] // 2
    rows = residual.shape[0] // half
    for image in range(half):
        at = slice(image * rows, (image + 1) * rows)
        mlp_out = own[at, :].astype(f32) + moved[at, :].astype(f32)
        gate = mods[5, pl.ds(core * half + image, 1), :]
        kept_out[at, :] = (residual[at, :] + gate * mlp_out).astype(bf16)
        sums[pl.ds(image, 1), :] = jnp.sum(
            grad[at, :].astype(f32) * mlp_out, axis=0, keepdims=True
        )


def kernel_first_back(
    own, moved, residual_grad, kept, mods, late, last, kept_grad, mine, partner
):
    me = lax.axis_index("mp")
    core = me & 1
    half = mods.shape[1] // 2
    rows = residual_grad.shape[0] // half
    local = mine.shape[2]
    lines = [[], []]
    for image in range(half):
        at = slice(image * rows, (image + 1) * rows)
        normed, inverse = layer_norm(kept[at, :].astype(f32))
        gradient = own[at, :].astype(f32) + moved[at, :].astype(f32)
        lines[0].append(jnp.sum(gradient, axis=0, keepdims=True))
        lines[1].append(jnp.sum(gradient * normed, axis=0, keepdims=True))
        scale = mods[1, pl.ds(core * half + image, 1), :]
        values = residual_grad[at, :] + norm_back(normed, inverse, gradient * (1.0 + scale))
        kept_grad[at, :] = values.astype(bf16)
    planes = [jnp.concatenate(line, 0) for line in lines]
    planes += [late[0], late[1], late[2], last[...]]
    for k, plane in enumerate(planes):
        blocks = [plane[:, j * local : (j + 1) * local] for j in range(4)]
        for out, device in ((mine, me), (partner, me ^ 1)):
            picked = blocks[0]
            for j in range(1, 4):
                picked = jnp.where(device == j, blocks[j], picked)
            out[k] = picked.astype(bf16)


def new_state(weight, moment, average, gradient, rate, steps):
    decay = (1.0 + steps) / (10.0 + steps)
    new_moment = momentum_rate * moment + gradient
    master = weight - rate * (gradient + momentum_rate * new_moment)
    return master, new_moment, decay * average + (1.0 - decay) * master


def summed(given):
    total = given[0][...].astype(f32)
    for ref in given[1:]:
        total = total + ref[...].astype(f32)
    return total


def one_step(rate, count, index, steps, *refs):
    given, refs = refs[:count], refs[count:]
    values = new_state(*[ref[...] for ref in refs[:3]], summed(given), rate, steps[0].astype(f32))
    for ref, value in zip(refs[3:], values):
        ref[...] = value


def attention_step(rate, count, index, steps, *refs):
    given, refs = refs[:count], refs[count:]
    gradient = summed(given)
    counts = steps[0].astype(f32)
    qkv, proj, qkv_out, proj_out = refs[:3], refs[3:6], refs[6:9], refs[9:]
    local = proj[0].shape[1]
    for t in range(3):
        values = new_state(
            *[ref[t] for ref in qkv], gradient[:, t * local : (t + 1) * local], rate, counts
        )
        for ref, value in zip(qkv_out, values):
            ref[t] = value
    values = new_state(*[ref[...] for ref in proj], gradient[:, 3 * local :], rate, counts)
    for ref, value in zip(proj_out, values):
        ref[...] = value


def step_weights(kernel, name, state, given, rate, steps, limit=None):
    rows = given[0].shape[0]
    block = 48 if rows % 48 == 0 else rows
    count = rows // block

    def spec(x):
        if x.ndim == 3:
            return pl.BlockSpec((x.shape[0], block, x.shape[2]), lambda i, index: (0, i, 0))
        return pl.BlockSpec((block, x.shape[1]), lambda i, index: (i, 0))

    own = pl.BlockSpec((block, given[0].shape[1]), lambda i, index: (index[0] * count + i, 0))
    specs = [spec(x) for x in given[:2]] + [own] * (len(given) - 2)
    return pl.pallas_call(
        partial(kernel, rate, len(given)),
        grid_spec=pltpu.PrefetchScalarGridSpec(
            num_scalar_prefetch=1,
            grid=(count,),
            in_specs=[pl.BlockSpec(memory_space=pltpu.SMEM)] + specs + [spec(x) for x in state],
            out_specs=[spec(x) for x in state],
        ),
        out_shape=[jax.ShapeDtypeStruct(x.shape, f32) for x in state],
        compiler_params=pltpu.CompilerParams(vmem_limit_bytes=limit),
        cost_estimate=pl.CostEstimate(flops=0, bytes_accessed=1024, transcendentals=0),
        name=name,
    )(lax.axis_index("dp").astype(jnp.int32).reshape(1), steps, *given, *state)


def ada_step(rate, steps, cond, mods, weight, moment, average, master, new_moment, ema):
    counts = steps[0].astype(f32)
    for k in range(weight.shape[0]):
        gradient = dot_first(cond[...], mods[k])
        values = new_state(weight[k], moment[k], average[k], gradient, rate, counts)
        master[k], new_moment[k], ema[k] = values


def step_ada(weight, moment, average, cond, mods, rate, steps):
    count, rows, columns = weight.shape
    spec = pl.BlockSpec((2, rows, columns), lambda k: (k, 0, 0))
    return pl.pallas_call(
        partial(ada_step, rate),
        grid=(count // 2,),
        out_shape=[jax.ShapeDtypeStruct(weight.shape, f32)] * 3,
        in_specs=[
            pl.BlockSpec(memory_space=pltpu.SMEM),
            pl.BlockSpec(cond.shape, lambda k: (0, 0)),
            pl.BlockSpec((2,) + mods.shape[1:], lambda k: (k, 0, 0)),
        ]
        + [spec] * 3,
        out_specs=[spec] * 3,
        cost_estimate=pl.CostEstimate(flops=0, bytes_accessed=1024, transcendentals=0),
        name="step_ada",
    )(steps, cond, mods, weight, moment, average)


def per_device(
    tokens,
    condition,
    cotangent,
    kept_index,
    skip_index,
    step_count,
    ada_weight,
    qkv_weight,
    proj_weight,
    fc1_weight,
    fc2_weight,
    ada_moment,
    qkv_moment,
    proj_moment,
    fc1_moment,
    fc2_moment,
    ada_average,
    qkv_average,
    proj_average,
    fc1_average,
    fc2_average,
):
    images, seq, width = tokens.shape
    kept_count = kept_index.shape[1]
    own_d = ada_weight.shape[0]
    mods = ada_weight.shape[1]
    local = ada_weight.shape[2]
    units = fc1_weight.shape[1]
    local_heads = local // HEAD_DIM
    total = images * kept_count
    half = total // 2
    core = lax.axis_index("mp") % 2
    chip = lax.axis_index("mp") // 2
    dp_size = lax.axis_size("dp")
    index = lax.axis_index("dp")
    ring = dp_size == 8

    live = []

    def tick(extras, *hops):
        hops = [(one, sides) for one, sides in hops if one is not None]
        busy = [one for one, _ in hops]
        idle = [one for one in live if one not in busy]
        moving = tuple(one.start(sides) for one, sides in hops)
        work = tuple(extras())
        resting = tuple((one.held["a"], one.held["b"]) for one in idle)
        held, moved, resting = stage((work, moving, resting))
        for (one, sides), values in zip(hops, moved):
            one.finish(sides, values)
        for one, values in zip(idle, resting):
            one.finish("ab", values)
        return held

    rate = 0.02 / math.sqrt(images * dp_size * kept_count)

    attn_low = jnp.concatenate(
        [qkv_weight[0], qkv_weight[1], qkv_weight[2], proj_weight.T], 1
    ).astype(bf16)
    fc1_low = fc1_weight.astype(bf16)
    fc2_low = fc2_weight.T.astype(bf16)
    if ring:
        attn_ring, fc1_ring, fc2_ring = Gather(attn_low, 1), Gather(fc1_low, 1), Gather(fc2_low, -1)
    else:
        attn_ring = fc1_ring = fc2_ring = None
        attn_pieces, attn_places = [gather_plain(attn_low)], [None]
        fc1_pieces, fc1_places = [gather_plain(fc1_low)], [None]
        fc2_pieces, fc2_places = [gather_plain(fc2_low)], [None]
    block = [((width // 8, units), bf16)] * 2 if ring else []
    attn_block = [((width // 8, 4 * local), bf16)] * 2 if ring else []

    cond_float = condition.astype(f32)
    silu_cond = jax.nn.silu(cond_float).astype(bf16)
    small = silu_cond.reshape(images, dp_size, own_d)
    levels = len(dp_groups())
    def first_norm():
        return spread_round(small, 0, 0), *run(
            kernel_norm,
            "first_norm",
            [((half, width), bf16), ((total, width), f32)],
            (tokens, kept_index),
        )

    small, kept_own, normed = tick(first_norm, (attn_ring, "ab"))
    ada_state = [jnp.moveaxis(x, 1, 0) for x in (ada_weight, ada_moment, ada_average)]

    def rest_of_cond():
        values = small
        for level in range(1, levels):
            values = spread_round(values, 0, level)
        return (values,)

    (small,) = tick(rest_of_cond, (attn_ring, "ab"))

    def sum_of_mods():
        own = lax.dynamic_index_in_dim(small, index, 1, keepdims=False)
        (values,) = run(
            kernel_mods, "mods", [((mods, dp_size * images, local), f32)], (own, ada_state[0])
        )
        for level in reversed(range(1, levels)):
            values = sum_round(values, 1, level)
        return own, values

    cond_own, small = tick(sum_of_mods, (attn_ring, "ab"))
    (mod_local,) = tick(lambda: (sum_round(small, 1, 0),), (attn_ring, "a"))
    if ring:
        attn_pieces, attn_places = attn_ring.pieces()

    def all_mods():
        at_core = swap_core(mod_local)
        at_x = swap_x(mod_local)
        at_both = lax.ppermute(mod_local, "mp", [(j, j ^ 3) for j in range(4)])
        pairs = [join_pair(mod_local, at_core, core, 2), join_pair(at_x, at_both, core, 2)]
        return (
            jnp.where(chip == 0, jnp.concatenate(pairs, 2), jnp.concatenate(pairs[::-1], 2)),
        )

    (modulation,) = tick(all_mods, (fc1_ring, "ab"))


    def project():
        outs = [((total, width), bf16), ((total, 3 * local), bf16)]
        lanes = -(-3 * local // 128) * 128
        return run(
            partial(kernel_project, attn_places),
            "project",
            outs,
            (*attn_pieces, normed, modulation),
            [((width, lanes), bf16), ((total, width), f32)] + outs,
        )

    hidden, projected = tick(project, (fc2_ring, "ab"))

    def add_low(own, other):
        return (own + other.astype(f32)).astype(bf16)

    def attend():
        outs = [((total, local), bf16), ((half, width), f32), ((half, width), bf16)]
        lanes = 4 * local - lane_start(3 * local)
        return run(
            partial(kernel_attend, attn_places, local_heads, kept_count),
            "attend",
            outs,
            (*attn_pieces, projected),
            [((width, lanes), bf16), ((total, 3 * local), bf16)] + outs,
        )

    attended, own_part, other_part = tick(attend, (fc1_ring, "ab"))

    def attention_sums():
        own = add_low(own_part, swap_core(other_part))
        return own, swap_x(own), *kept_grads()


    def kept_grads():
        return run(
            kernel_kept_grad,
            "kept_grad",
            [((half, width), bf16), ((total, width), bf16)],
            (cotangent, kept_index, modulation),
        )

    attn_own, attn_moved, grad_own, mlp_grad = tick(
        attention_sums, (fc1_ring, "ab"), (fc2_ring, "ab")
    )

    def second_norm():
        values, low = run(
            kernel_second_norm,
            "second_norm",
            [((half, width), f32), ((half, width), bf16)],
            (kept_own, modulation, attn_own, attn_moved),
        )
        return values, low

    residual, hidden_here = tick(second_norm, (fc1_ring, "a"), (fc2_ring, "a"))
    hidden_here, hidden_there = tick(lambda: (hidden_here, swap_core(hidden_here)))
    if ring:
        fc1_pieces, fc1_places = fc1_ring.pieces()

    def feed_forward():
        outs = [((total, units), f32), ((total, units), bf16), ((width, units), bf16)]
        return run(
            partial(kernel_feed_forward, fc1_places, -1),
            "feed_forward",
            outs + block,
            (*fc1_pieces, hidden_here, hidden_there, mlp_grad),
            [((width, units), bf16), ((total, width), bf16), ((total, width), bf16)] + outs,
        )

    pre_act, activated, fc2_grad, *first = tick(feed_forward, (fc2_ring, "ba"))
    if ring:
        fc2_pieces, fc2_places = fc2_ring.pieces()
        fc2_sums = Scatter(fc2_grad, -1, first)
        live.append(fc2_sums)
    else:
        fc2_sums = fc1_sums = attn_sums = None

    def feed_back():
        outs = [((total, units), bf16), ((half, width), f32), ((half, width), bf16)]
        return run(
            partial(kernel_feed_back, fc1_places, fc2_places),
            "feed_back",
            outs,
            (*fc1_pieces, *fc2_pieces, mlp_grad, pre_act),
            [
                ((width, units), bf16),
                ((width, units), bf16),
                ((total, width), bf16),
                ((total, units), f32),
            ]
            + outs,
        )

    pre_grad, own_part, other_part = tick(feed_back, (fc2_sums, "ab"))
    moving = []

    def products():
        own_low = add_low(own_part, swap_core(other_part))
        outs = [((width, units), bf16)]
        grad, *first = run(
            partial(kernel_fc1_grad, -1),
            "fc1_grad",
            outs + block,
            (hidden_here, hidden_there, pre_grad),
            [((total, width), bf16), ((total, units), bf16)] + outs,
        )
        if ring:
            moving.append(Scatter(grad, -1, first))
            first = moving[0].start("ab")
        return own_low, swap_x(own_low), grad, activated, *first

    hidden_own, hidden_moved, fc1_grad, activated, *first = tick(
        products, (fc2_sums, "ab+")
    )
    if ring:
        (fc1_sums,) = moving
        fc1_sums.part = fc1_grad
        fc1_sums.finish("ab", first)
        live.append(fc1_sums)

    def second_back():
        values, low, lines = run(
            kernel_second_back,
            "second_back",
            [((half, width), f32), ((half, width), bf16), ((3, images // 2, width), f32)],
            (
                hidden_own,
                hidden_moved,
                residual,
                attn_own,
                attn_moved,
                grad_own,
                modulation,
            ),
        )
        outs = [((half, width), f32), ((half, width), bf16)]
        mlp = run(
            partial(kernel_feed_out, fc2_places),
            "feed_out",
            outs,
            (*fc2_pieces, activated),
            [((width, units), bf16), ((total, units), bf16)] + outs,
        )
        sums = ()
        if ring:
            held = stage((fc1_sums.held["a"], fc1_sums.held["b"], low))
            fc1_sums.finish("ab", held[:2])
            sums = fc1_sums.prepare("ab")
        return values, low, lines, *mlp, *sums

    residual_grad, out_here, late_mods, own_mlp, other_mlp, *sums = tick(
        second_back, (fc2_sums, "ab")
    )
    if ring:
        fc1_sums.finish("ab", sums)

    def between():
        sums = fc2_sums.prepare("a") if ring else ()
        low = add_low(own_mlp, swap_core(other_mlp))
        return out_here, swap_core(out_here), low, *sums

    out_here, out_there, mlp_own, *sums = tick(between)
    if ring:
        fc2_sums.finish("a", sums)

    def attention_back():
        outs = [((width, 4 * local), bf16), ((half, width), f32), ((half, width), bf16)]
        back = run(
            partial(kernel_attention_back, attn_places, local_heads, kept_count, 1),
            "attention_back",
            outs + attn_block,
            (*attn_pieces, out_here, out_there, projected, attended, hidden),
            [
                ((width, 4 * local), bf16),
                ((total, width), bf16),
                ((total, 3 * local), bf16),
                ((total, local), bf16),
                ((total, width), bf16),
                ((total, local), bf16),
                ((total, 3 * local), bf16),
            ]
            + outs,
        )
        return swap_x(mlp_own), *back

    mlp_moved, attn_grad, own_part, other_part, *first = tick(
        attention_back, (fc1_sums, "ab"), (fc2_sums, "a")
    )
    if ring:
        attn_sums = Scatter(attn_grad, 1, first)
        live.append(attn_sums)

    def output():
        return run(
            kernel_output,
            "output",
            [((half, width), bf16), ((images // 2, width), f32)],
            (mlp_own, mlp_moved, residual, grad_own, modulation),
        )

    back_own, mlp_moved = tick(
        lambda: (add_low(own_part, swap_core(other_part)), mlp_moved)
    )

    def attention_back_sums():
        given = fc2_sums.given() if ring else (scatter_plain(fc2_grad),)
        state = (fc2_weight.T, fc2_moment.T, fc2_average.T)
        new = step_weights(one_step, "step_fc2", state, given, rate, step_count, 12 << 20)
        return swap_x(back_own), *output(), *new

    if ring:
        live.remove(fc2_sums)
    back_moved, kept_out, last_mods, fc2_master, fc2_momentum, fc2_ema = tick(
        attention_back_sums, (attn_sums, "ab+"), (fc1_sums, "ab")
    )

    def first_back():
        kept, mine, partner = run(
            kernel_first_back,
            "first_back",
            [
                ((half, width), bf16),
                ((mods, images // 2, local), bf16),
                ((mods, images // 2, local), bf16),
            ],
            (
                back_own,
                back_moved,
                residual_grad,
                kept_own,
                modulation,
                late_mods,
                last_mods,
            ),
        )
        values = spread_round(join_pair(mine, swap_core(partner), core, 1), 1, 0)
        return kept, values, kept_out

    kept_grad, small, kept_out = tick(first_back, (attn_sums, "ab"))

    def last_spread():
        sums = fc1_sums.prepare("a") if ring else ()
        values = small
        for level in range(1, levels):
            values = spread_round(values, 1, level)
        there = swap_core(kept_grad), swap_core(kept_out)
        return values, kept_grad, kept_out, *there, *sums

    mod_grad_all, kept_grad, kept_out, grad_there, kept_there, *sums = tick(
        last_spread, (attn_sums, "ab")
    )
    if ring:
        fc1_sums.finish("a", sums)

    def silu_sums():
        (part,) = run(
            kernel_silu, "silu", [((dp_size * images, own_d), f32)], (mod_grad_all, ada_state[0])
        )
        grads = place_kept(kept_grad, grad_there, cotangent, kept_index, f32)
        out = place_kept(kept_out, kept_there, tokens, kept_index, bf16)
        return part + swap_core(part), grads, out, mod_grad_all

    silu_part, tokens_grad, block_out, mod_grad_all = tick(
        silu_sums, (attn_sums, "a"), (fc1_sums, "a")
    )

    def step_beside_x():
        given = attn_sums.given() if ring else (scatter_plain(attn_grad),)
        state = (qkv_weight, qkv_moment, qkv_average)
        state += (proj_weight.T, proj_moment.T, proj_average.T)
        new = step_weights(attention_step, "step_attention", state, given, rate, step_count)
        return silu_part + swap_x(silu_part), mod_grad_all, *new

    silu_part, mod_grad_all, *attn_new = tick(step_beside_x)
    silu_blocks = silu_part.reshape(dp_size, images, own_d)

    def step_beside_turn():
        blocks = silu_blocks
        for level in reversed(range(1, levels)):
            blocks = turn_round(blocks, level)
        return blocks, *step_ada(*ada_state, cond_own, mod_grad_all, rate, step_count)

    silu_blocks, *ada_new = tick(step_beside_turn)
    silu_blocks = in_order(turn_round(silu_blocks, 0))
    given = fc1_sums.given() if ring else (scatter_plain(fc1_grad),)
    state = (fc1_weight, fc1_moment, fc1_average)
    fc1_master, fc1_momentum, fc1_ema = step_weights(
        one_step, "step_fc1", state, given, rate, step_count
    )
    qkv_master, qkv_momentum, qkv_ema, proj_master, proj_momentum, proj_ema = attn_new
    ada_master, ada_momentum, ada_ema = [jnp.moveaxis(x, 0, 1) for x in ada_new]
    silu_grad = jnp.moveaxis(silu_blocks, 0, 1).reshape(images, width)
    silu_value, silu_pull = jax.vjp(jax.nn.silu, cond_float)
    condition_grad = silu_pull(silu_grad)[0]
    return (
        block_out,
        tokens_grad,
        condition_grad,
        ada_master,
        qkv_master,
        proj_master.T,
        fc1_master,
        fc2_master.T,
        ada_momentum,
        qkv_momentum,
        proj_momentum.T,
        fc1_momentum,
        fc2_momentum.T,
        ada_ema,
        qkv_ema,
        proj_ema.T,
        fc1_ema,
        fc2_ema.T,
    )


def solution(mesh):
    weights = (
        P("dp", None, "mp"),
        P(None, "dp", "mp"),
        P("mp", "dp"),
        P("dp", "mp"),
        P("mp", "dp"),
    )
    rows = P("dp", None, None)
    pairs = P("dp", None)
    return jax.shard_map(
        per_device,
        mesh=mesh,
        in_specs=(rows, pairs, rows, pairs, pairs, P()) + weights * 3,
        out_specs=(rows, rows, pairs) + weights * 3,
        check_vma=False,
    )
```

```python
from functools import partial
import math

import jax
import jax.numpy as jnp
from jax import lax
from jax.experimental import pallas as pl
from jax.experimental.pallas import tpu as pltpu
from jax.sharding import PartitionSpec as P

HEAD_DIM = 72

epsilon = 1e-06
momentum_rate = 0.9

f32 = jnp.float32
bf16 = jnp.bfloat16


def layer_norm(values):
    centered = values - jnp.mean(values, axis=-1, keepdims=True)
    inverse = lax.rsqrt(jnp.mean(centered * centered, axis=-1, keepdims=True) + epsilon)
    return (centered * inverse, inverse)


def norm_back(normed, inverse, gradient):
    return inverse * (
        gradient
        - jnp.mean(gradient, axis=-1, keepdims=True)
        - normed * jnp.mean(gradient * normed, axis=-1, keepdims=True)
    )


def swap_core(values):
    return lax.ppermute(values, "mp", [(j, j ^ 1) for j in range(4)])


def swap_x(values):
    return lax.ppermute(values, "mp", [(j, j ^ 2) for j in range(4)])


def join_pair(own, other, core, axis=0):
    return jnp.where(
        core == 0,
        jnp.concatenate([own, other], axis),
        jnp.concatenate([other, own], axis),
    )


def spread_pair(own, core):
    return join_pair(own, swap_core(own), core)


def swap_dp(values, bit):
    size = lax.axis_size("dp")
    return lax.ppermute(values, "dp", [(i, i ^ bit) for i in range(size)])


def dp_groups():
    size = lax.axis_size("dp")
    return [4] + [2] * (size.bit_length() - 3)


def spread_round(values, axis, level):
    groups = dp_groups()
    step = math.prod(groups[:level])
    others = [swap_dp(values, step * b) for b in range(1, groups[level])]
    return jnp.concatenate([values] + others, axis)


def sum_round(values, axis, level):
    groups = dp_groups()
    step = math.prod(groups[:level])
    blocks = jnp.split(values, groups[level], axis)
    total = blocks[0]
    for b in range(1, groups[level]):
        total = total + swap_dp(blocks[b], step * b)
    return total


def turn_round(values, level):
    groups = dp_groups()
    step = math.prod(groups[:level])
    shape = values.shape
    values = values.reshape((-1, groups[level], step) + shape[1:])
    blocks = [values[:, b] for b in range(groups[level])]
    blocks = [blocks[0]] + [swap_dp(blocks[b], step * b) for b in range(1, groups[level])]
    return jnp.stack(blocks, 1).reshape(shape)


def in_order(values):
    index = lax.axis_index("dp")
    shape = values.shape
    count = shape[0].bit_length() - 1
    values = values.reshape((2,) * count + shape[1:])
    for axis in range(count):
        values = jnp.where((index >> (count - 1 - axis)) & 1, jnp.flip(values, axis), values)
    return values.reshape(shape)


def ring_tables():
    cycle = [0, 2, 4, 6, 7, 5, 3, 1]
    clockwise = [(cycle[i], cycle[(i + 1) % 8]) for i in range(8)]
    return clockwise, [(b, a) for a, b in clockwise]


def ring_place_of(index):
    return jnp.where((index & 1) == 0, index >> 1, 7 - (index >> 1))


def ring_device(place):
    place = lax.rem(place, 8)
    return jnp.where(place < 4, 2 * place, 2 * (7 - place) + 1)


def hop(values, direction):
    clockwise, backward = ring_tables()
    return lax.ppermute(values, "dp", clockwise if direction > 0 else backward)


def ring_device_at(index, distance):
    return ring_device(ring_place_of(index) + distance + 8)


class Gather:
    def __init__(self, shard, lead):
        self.lead = lead
        self.shard = shard
        self.ahead = [shard]
        self.behind = [shard]

    def start(self, sides):
        moving = []
        if "a" in sides:
            moving.append(hop(self.ahead[-1], self.lead))
        if "b" in sides:
            moving.append(hop(self.behind[-1], -self.lead))
        return tuple(moving)

    def finish(self, sides, moved):
        moved = list(moved)
        if "a" in sides:
            self.ahead.append(moved.pop(0))
        if "b" in sides:
            self.behind.append(moved.pop(0))

    def pieces(self):
        rows = self.shard.shape[0]
        distances = [-self.lead * k for k in range(5)] + [self.lead * k for k in range(1, 4)]
        places = [
            partial(lambda distance, index: ring_device_at(index, distance) * rows, distance)
            for distance in distances
        ]
        return self.ahead + self.behind[1:], places


class Scatter:
    def __init__(self, part, lead, first):
        self.part, self.lead = part, lead
        self.rows = part.shape[0] // 8
        self.left = {"a": 4, "b": 3}
        self.added = {"a": False, "b": False}
        self.held = dict(zip("ab", first))

    def signs(self):
        return {"a": self.lead, "b": -self.lead}

    def add(self, values):
        full = {"a": 4, "b": 3}
        adding = [k for k in values if 0 < self.left[k] < full[k] and not self.added[k]]
        if adding:
            signs = self.signs()
            sums = add_blocks(
                self.part,
                [values[k] for k in adding],
                [signs[k] * self.left[k] for k in adding],
            )
            values = {**values, **dict(zip(adding, sums))}
            for k in adding:
                self.added[k] = True
        return values

    def prepare(self, sides):
        values = self.add({k: self.held[k] for k in sides})
        return tuple(values[k] for k in sides)

    def start(self, sides):
        values = self.add({k: self.held[k] for k in sides if k in "ab"})
        signs = self.signs()
        for k in values:
            self.left[k] -= 1
            self.added[k] = False
        values = {k: hop(value, signs[k]) for k, value in values.items()}
        if "+" in sides:
            values = self.add(values)
        return tuple(values.values())

    def finish(self, sides, moved):
        self.held.update(zip(sides, moved))

    def given(self):
        return self.held["a"], self.held["b"], self.part


def gather_plain(shard):
    return lax.all_gather(shard, "dp", axis=0, tiled=True)


def scatter_plain(part):
    return lax.psum_scatter(part.astype(f32), "dp", scatter_dimension=0, tiled=True)


stage = lax.optimization_barrier


def run(kernel, name, outs, args, scratch=None):
    vmem = pl.BlockSpec(memory_space=pltpu.VMEM)
    anywhere = pl.BlockSpec(memory_space=pl.ANY)
    by_copy = scratch is not None
    return pl.pallas_call(
        kernel,
        out_shape=[jax.ShapeDtypeStruct(shape, dtype) for shape, dtype in outs],
        in_specs=[vmem if not by_copy or x.size < 40000 else anywhere for x in args],
        out_specs=[anywhere if by_copy else vmem] * len(outs),
        scratch_shapes=[pltpu.VMEM(shape, dtype) for shape, dtype in scratch]
        + [pltpu.SemaphoreType.DMA((48,))]
        if by_copy
        else [],
        compiler_params=pltpu.CompilerParams(vmem_limit_bytes=20 << 20),
        cost_estimate=pl.CostEstimate(flops=0, bytes_accessed=1024, transcendentals=0),
        name=name,
    )(*args)


class Copies:
    def __init__(self, semaphores):
        self.semaphores = semaphores
        self.used = 0

    def start(self, source, target):
        copy = pltpu.make_async_copy(source, target, self.semaphores.at[self.used])
        self.used += 1
        copy.start()
        return copy

    def each(self, sources, targets, count, width):
        first = self.used
        self.used += count * len(sources)

        def copy(k, tile):
            at = pl.ds(pl.multiple_of(tile * width, width), width)
            number = first + k * count + tile
            return pltpu.make_async_copy(
                sources[k].at[:, at], targets[k].at[:, at], self.semaphores.at[number]
            )

        def start(tile):
            for k in range(len(sources)):
                copy(k, tile).start()

        def finish(tile, carry=0):
            for k in range(len(sources)):
                copy(k, tile).wait()
            return carry

        return start, finish

    def place(self, pieces, places, target):
        started = []
        for piece, place in zip(pieces, places):
            if place is None:
                started.append(self.start(piece, target))
            else:
                at = pl.multiple_of(place(lax.axis_index("dp")), 8)
                started.append(self.start(piece, target.at[pl.ds(at, piece.shape[0]), :]))
        return started


    def first_blocks(self, part, lead, outs):
        started = []
        for distance, out in zip((4 * lead, -3 * lead), outs):
            rows = out.shape[0]
            at = pl.multiple_of(ring_device_at(lax.axis_index("dp"), distance) * rows, 8)
            started.append(self.start(part.at[pl.ds(at, rows), :], out))
        return started


def wait(copies):
    for copy in copies:
        copy.wait()


def kernel_add(distances, part, *refs):
    count = len(distances)
    moved, outs, blocks, semaphores = refs[:count], refs[count : 2 * count], refs[2 * count], refs[-1]
    copies = Copies(semaphores)
    rows = outs[0].shape[0]
    arriving = []
    for k, distance in enumerate(distances):
        at = pl.multiple_of(ring_device_at(lax.axis_index("dp"), distance) * rows, 8)
        arriving.append(copies.start(part.at[pl.ds(at, rows), :], blocks.at[k]))
    step = 48 if rows % 48 == 0 else rows
    for k in range(count):
        arriving[k].wait()
        total, block, out = moved[k], blocks.at[k], outs[k]

        def add(i, carry):
            at = pl.ds(pl.multiple_of(i * step, step), step)
            out[at, :] = (total[at, :].astype(f32) + block[at, :].astype(f32)).astype(bf16)
            return carry

        lax.fori_loop(0, rows // step, add, 0)


def add_blocks(part, moved, distances):
    shape = moved[0].shape
    count = len(moved)
    vmem = pl.BlockSpec(memory_space=pltpu.VMEM)
    return pl.pallas_call(
        partial(kernel_add, distances),
        out_shape=[jax.ShapeDtypeStruct(shape, bf16)] * count,
        in_specs=[pl.BlockSpec(memory_space=pl.ANY)] + [vmem] * count,
        out_specs=[vmem] * count,
        scratch_shapes=[pltpu.VMEM((count,) + shape, bf16), pltpu.SemaphoreType.DMA((count,))],
        compiler_params=pltpu.CompilerParams(vmem_limit_bytes=8 << 20),
        cost_estimate=pl.CostEstimate(flops=0, bytes_accessed=1024, transcendentals=0),
        name="add_blocks",
    )(part, *moved)


def dot(a, b):
    return jnp.dot(a, b, preferred_element_type=f32)


def dot_last(a, b):
    return lax.dot_general(a, b, (((1,), (1,)), ((), ())), preferred_element_type=f32)


def dot_first(a, b):
    return lax.dot_general(a, b, (((0,), (0,)), ((), ())), preferred_element_type=f32)


def core_here():
    return lax.axis_index("mp") & 1


def pair_rows(total, pair):
    half = total // 2
    return pl.ds(pl.multiple_of(pair * half, half), half)


def image_rows(rows, image):
    return pl.ds(pl.multiple_of(image * rows, rows), rows)


def tiles(total):
    return total // 384 if total % 384 == 0 else 1


def chosen(index, values):
    shape = (values.shape[0], index.shape[1])
    select = lax.broadcasted_iota(jnp.int32, shape, 0) == index
    return dot_first(select.astype(f32).astype(bf16), values)


def head_values(values, local, depth, head, t):
    return values[:, t * local + head * depth : t * local + (head + 1) * depth]


def stacked_probs(values, local, depth, heads):
    scores = jnp.concatenate(
        [
            dot_last(
                head_values(values, local, depth, head, 0),
                head_values(values, local, depth, head, 1),
            )
            for head in range(heads)
        ],
        0,
    )
    scores = scores * depth ** (-0.5)
    exp_scores = jnp.exp(scores - jnp.max(scores, axis=-1, keepdims=True))
    return exp_scores / jnp.sum(exp_scores, axis=-1, keepdims=True)


def lane_start(columns):
    return columns // 128 * 128


def kernel_mods(cond, weights, out):
    for k in range(out.shape[0]):
        out[k] = dot(cond[...], weights[k].astype(bf16))


def kernel_silu(grads, weights, out):
    total = dot_last(grads[0], weights[0].astype(bf16))
    for k in range(1, grads.shape[0]):
        total = total + dot_last(grads[k], weights[k].astype(bf16))
    out[...] = total


def kernel_norm(tokens, index, own, normed):
    images, rows = index.shape
    core = core_here()

    def norm(image, carry):
        at = image_rows(rows, image)
        values = chosen(index[pl.ds(image, 1), :], tokens[image])
        normed[at, :] = layer_norm(values)[0]

        @pl.when(image // (images // 2) == core)
        def _():
            place = image_rows(rows, image - core * (images // 2))
            own[place, :] = values.astype(bf16)

        return carry

    lax.fori_loop(0, images, norm, 0)


def kernel_project(places, *refs):
    count = len(places)
    pieces, (given, mods) = refs[:count], refs[count : count + 2]
    outs, refs = refs[count + 2 : count + 4], refs[count + 4 :]
    full, normed, hidden, projected, semaphores = refs
    copies = Copies(semaphores)
    images = mods.shape[1]
    total = normed.shape[0]
    rows = total // images
    arriving = [copies.start(given, normed)]
    columns = full.shape[1]
    placed = copies.place([piece.at[:, :columns] for piece in pieces], places, full)
    wait(arriving)

    def norm(image, carry):
        at = image_rows(rows, image)
        scale = mods[1, pl.ds(image, 1), :]
        values = normed[at, :] * (1.0 + scale) + mods[0, pl.ds(image, 1), :]
        hidden[at, :] = values.astype(bf16)
        return carry

    lax.fori_loop(0, images, norm, 0)
    leaving = [copies.start(hidden, outs[0])]
    wait(placed)
    weights = full[:, : projected.shape[1]]

    def project(pair, carry):
        at = pair_rows(total, pair)
        projected[at, :] = dot(hidden[at, :], weights).astype(bf16)
        return carry

    lax.fori_loop(0, 2, project, 0)
    leaving.append(copies.start(projected, outs[1]))
    wait(leaving)


def kernel_attend(places, heads, rows, *refs):
    count = len(places)
    pieces, (given,) = refs[:count], refs[count : count + 1]
    outs, refs = refs[count + 1 : count + 4], refs[count + 4 :]
    full, projected, attended, own, other, semaphores = refs
    copies = Copies(semaphores)
    total = projected.shape[0]
    local = attended.shape[1]
    depth = local // heads
    core = core_here()
    start = lane_start(3 * local)
    arriving = [copies.start(given, projected)]
    placed = copies.place([piece.at[:, start:] for piece in pieces], places, full)
    wait(arriving)

    def attend(image, carry):
        at = image_rows(rows, image)
        values = projected[at, :]
        probs = stacked_probs(values, local, depth, heads).astype(bf16)
        attended[at, :] = jnp.concatenate(
            [
                dot(
                    probs[head * rows : (head + 1) * rows],
                    head_values(values, local, depth, head, 2),
                ).astype(bf16)
                for head in range(heads)
            ],
            1,
        )
        return carry

    lax.fori_loop(0, total // rows, attend, 0, unroll=True)
    leaving = [copies.start(attended, outs[0])]
    wait(placed)
    weights = full[:, 3 * local - start :]
    other[...] = dot_last(attended[pair_rows(total, 1 - core), :], weights).astype(bf16)
    leaving.append(copies.start(other, outs[2]))
    own[...] = dot_last(attended[pair_rows(total, core), :], weights)
    leaving.append(copies.start(own, outs[1]))
    wait(leaving)


def kernel_kept_grad(grads, index, mods, own, mlp_grad):
    core = core_here()
    images, rows = index.shape
    half = images // 2
    for place in range(images):
        pair = core if place < half else 1 - core
        image = pair * half + place % half
        values = chosen(index[pl.ds(image, 1), :], grads[image])
        at = slice(place * rows, (place + 1) * rows)
        if place < half:
            own[at, :] = values.astype(bf16)
        mlp_grad[at, :] = (mods[5, pl.ds(image, 1), :] * values).astype(bf16)


def kernel_second_norm(kept, mods, own, moved, residual, hidden_two):
    core = core_here()
    half = mods.shape[1] // 2
    rows = residual.shape[0] // half
    for image in range(half):
        at = slice(image * rows, (image + 1) * rows)
        where = core * half + image
        gate, shift, scale = [mods[k, pl.ds(where, 1), :] for k in (2, 3, 4)]
        attn_out = own[at, :].astype(f32) + moved[at, :].astype(f32)
        values = kept[at, :].astype(f32) + gate * attn_out
        residual[at, :] = values
        normed, _ = layer_norm(values)
        hidden_two[at, :] = (normed * (1.0 + scale) + shift).astype(bf16)


gelu_rate = math.sqrt(2.0 / math.pi)


def gelu_parts(values):
    tanh = jnp.tanh(gelu_rate * (values + 0.044715 * (values * values * values)))
    return 0.5 * (1.0 + tanh), tanh


def kernel_feed_forward(places, lead, *refs):
    count = len(places)
    pieces, (here, there, mlp) = refs[:count], refs[count : count + 3]
    outs, refs = refs[count + 3 : -7], refs[-7:]
    full, hidden_two, mlp_grad, pre_act, activated, fc2_grad, semaphores = refs
    copies = Copies(semaphores)
    half = here.shape[0]
    arriving = [copies.start(here, hidden_two.at[:half, :])]
    arriving.append(copies.start(there, hidden_two.at[half:, :]))
    arriving += copies.place(pieces, places, full)
    arriving.append(copies.start(mlp, mlp_grad))
    columns = full.shape[1]
    count = tiles(columns)
    width = columns // count
    leave, leave_end = copies.each([pre_act, activated, fc2_grad], outs[:3], count, width)
    wait(arriving)

    def product(tile, carry):
        at = pl.ds(pl.multiple_of(tile * width, width), width)
        values = dot(hidden_two[...], full[:, at])
        pre_act[:, at] = values
        low = (values * gelu_parts(values)[0]).astype(bf16)
        activated[:, at] = low
        fc2_grad[:, at] = dot_first(mlp_grad[...], low).astype(bf16)
        leave(tile)
        return carry

    lax.fori_loop(0, count, product, 0)
    leaving = copies.first_blocks(fc2_grad, lead, outs[3:])
    lax.fori_loop(0, count, leave_end, 0)
    wait(leaving)


def kernel_fc1_grad(lead, here, there, pre, *refs):
    outs, (hidden_two, pre_grad, fc1_grad, semaphores) = refs[:-4], refs[-4:]
    copies = Copies(semaphores)
    half = here.shape[0]
    arriving = [copies.start(here, hidden_two.at[:half, :])]
    arriving.append(copies.start(there, hidden_two.at[half:, :]))
    arriving.append(copies.start(pre, pre_grad))
    wait(arriving)
    columns = fc1_grad.shape[1]
    count = tiles(columns)
    width = columns // count
    leave, leave_end = copies.each([fc1_grad], outs[:1], count, width)

    def product(tile, carry):
        at = pl.ds(pl.multiple_of(tile * width, width), width)
        fc1_grad[:, at] = dot_first(hidden_two[...], pre_grad[:, at]).astype(bf16)
        leave(tile)
        return carry

    lax.fori_loop(0, count, product, 0)
    leaving = copies.first_blocks(fc1_grad, lead, outs[1:])
    lax.fori_loop(0, count, leave_end, 0)
    wait(leaving)


def kernel_feed_back(one_places, two_places, *refs):
    count = len(one_places)
    ones, twos, refs = refs[:count], refs[count : 2 * count], refs[2 * count :]
    (mlp, pre), outs, refs = refs[:2], refs[2:5], refs[5:]
    fc1, fc2, mlp_grad, pre_act, pre_grad, own, other, semaphores = refs
    copies = Copies(semaphores)
    arriving = [copies.start(mlp, mlp_grad)] + copies.place(twos, two_places, fc2)
    columns = fc2.shape[1]
    count = tiles(columns)
    width = columns // count
    values_in = [copies.start(pre, pre_act)]
    later = copies.place(ones, one_places, fc1)
    leave, leave_end = copies.each([pre_grad], outs[:1], count, width)
    wait(arriving + values_in)

    def product(tile, carry):
        at = pl.ds(pl.multiple_of(tile * width, width), width)
        gradient = dot(mlp_grad[...], fc2[:, at])
        values = pre_act[:, at]
        share, tanh = gelu_parts(values)
        slope = share + 0.5 * values * (1.0 - tanh * tanh) * gelu_rate * (
            1.0 + 3.0 * 0.044715 * (values * values)
        )
        pre_grad[:, at] = (gradient * slope).astype(bf16)
        leave(tile)
        return carry

    lax.fori_loop(0, count, product, 0)
    wait(later)
    back_product(copies, pre_grad, fc1, own, other, outs[1:])
    lax.fori_loop(0, count, leave_end, 0)


def back_product(copies, rows, weights, own, other, outs):
    half = own.shape[0]
    depth = weights.shape[0]
    count = tiles(depth)
    width = depth // count
    leave, leave_end = copies.each([own, other], outs, count, width)

    def product(tile, carry):
        at = pl.ds(pl.multiple_of(tile * width, width), width)
        values = dot_last(rows[...], weights[at, :])
        other[:, at] = values[half:].astype(bf16)
        own[:, at] = values[:half]
        leave(tile)
        return carry

    lax.fori_loop(0, count, product, 0)
    lax.fori_loop(0, count, leave_end, 0)


def kernel_feed_out(places, *refs):
    count = len(places)
    pieces, (low,) = refs[:count], refs[count : count + 1]
    outs, (full, activated, own, other, semaphores) = refs[count + 1 : count + 3], refs[count + 3 :]
    copies = Copies(semaphores)
    arriving = [copies.start(low, activated)] + copies.place(pieces, places, full)
    wait(arriving)
    back_product(copies, activated, full, own, other, outs)


def kernel_second_back(
    own, moved, residual, attn_own, attn_moved, grad, mods, residual_grad, attn_grad, sums
):
    core = core_here()
    half = mods.shape[1] // 2
    rows = residual.shape[0] // half
    for image in range(half):
        at = slice(image * rows, (image + 1) * rows)
        where = core * half + image
        gate, scale = [mods[k, pl.ds(where, 1), :] for k in (2, 4)]
        normed, inverse = layer_norm(residual[at, :])
        gradient = own[at, :].astype(f32) + moved[at, :].astype(f32)
        sums[1, pl.ds(image, 1), :] = jnp.sum(gradient, axis=0, keepdims=True)
        sums[2, pl.ds(image, 1), :] = jnp.sum(gradient * normed, axis=0, keepdims=True)
        values = grad[at, :].astype(f32) + norm_back(normed, inverse, gradient * (1.0 + scale))
        residual_grad[at, :] = values
        attn_out = attn_own[at, :].astype(f32) + attn_moved[at, :].astype(f32)
        sums[0, pl.ds(image, 1), :] = jnp.sum(values * attn_out, axis=0, keepdims=True)
        attn_grad[at, :] = (gate * values).astype(bf16)


def kernel_attention_back(places, heads, rows, lead, *refs):
    count = len(places)
    pieces, inputs = refs[:count], refs[count : count + 5]
    outs, refs = refs[count + 5 : -11], refs[-11:]
    here, there, projected_in, attended_in, hidden_in = inputs
    full, out_grad, projected, attended, hidden, back, grads, attn_grad, own, other = refs[:-1]
    copies = Copies(refs[-1])
    core = core_here()
    total = out_grad.shape[0]
    local = attended.shape[1]
    depth = local // heads
    arriving = [
        copies.start(here, out_grad.at[pair_rows(total, core), :]),
        copies.start(there, out_grad.at[pair_rows(total, 1 - core), :]),
    ] + copies.place(pieces, places, full)
    later = [copies.start(projected_in, projected), copies.start(attended_in, attended)]
    last = [copies.start(hidden_in, hidden)]
    wait(arriving)
    back[...] = dot(out_grad[...], full[:, 3 * local :]).astype(bf16)
    wait(later)

    def image_back(image, carry):
        at = image_rows(rows, image)
        values = projected[at, :]
        gradient = back[at, :]
        probs = stacked_probs(values, local, depth, heads)
        prob_grad = jnp.concatenate(
            [
                dot_last(
                    head_values(gradient, local, depth, head, 0),
                    head_values(values, local, depth, head, 2),
                )
                for head in range(heads)
            ],
            0,
        )
        score_grad = probs * (prob_grad - jnp.sum(prob_grad * probs, axis=-1, keepdims=True))
        score_grad = score_grad.astype(bf16)
        probs = probs.astype(bf16)
        parts = []
        for t in range(3):
            for head in range(heads):
                own_rows = slice(head * rows, (head + 1) * rows)
                if t == 0:
                    key = head_values(values, local, depth, head, 1)
                    part = dot(score_grad[own_rows], key) * depth ** (-0.5)
                elif t == 1:
                    query = head_values(values, local, depth, head, 0)
                    part = dot_first(score_grad[own_rows], query) * depth ** (-0.5)
                else:
                    part = dot_first(
                        probs[own_rows], head_values(gradient, local, depth, head, 0)
                    )
                parts.append(part.astype(bf16))
        grads[at, :] = jnp.concatenate(parts, 1)
        return carry

    lax.fori_loop(0, total // rows, image_back, 0, unroll=True)
    weights = full[:, : 3 * local]
    other[...] = dot_last(grads[pair_rows(total, 1 - core), :], weights).astype(bf16)
    leaving = [copies.start(other, outs[2])]
    own[...] = dot_last(grads[pair_rows(total, core), :], weights)
    leaving.append(copies.start(own, outs[1]))
    wait(last)
    attn_grad[:, 3 * local :] = dot_first(out_grad[...], attended[...]).astype(bf16)
    attn_grad[:, : 3 * local] = dot_first(hidden[...], grads[...]).astype(bf16)
    leaving.append(copies.start(attn_grad, outs[0]))
    leaving += copies.first_blocks(attn_grad, lead, outs[3:])
    wait(leaving)


def kernel_place(here, there, base, index, out):
    image = pl.program_id(0)
    rows = index.shape[2]
    half = here.shape[0] // rows
    pair = image // half
    at = image_rows(rows, image - pair * half)
    same = pair == core_here()
    values = jnp.where(same, here[at, :], there[at, :])
    select = lax.broadcasted_iota(jnp.int32, (base.shape[1], rows), 0) == index[0]
    select = select.astype(f32)
    kept = jnp.sum(select, axis=1, keepdims=True) > 0.5
    placed = dot(select.astype(bf16), values)
    out[0] = jnp.where(kept, placed, base[0].astype(f32)).astype(out.dtype)


def place_kept(here, there, base, index, dtype):
    images, seq, width = base.shape
    count = index.shape[1]
    whole = pl.BlockSpec(here.shape, lambda i: (0, 0))
    spec = pl.BlockSpec((1, seq, width), lambda i: (i, 0, 0))
    return pl.pallas_call(
        kernel_place,
        grid=(images,),
        out_shape=jax.ShapeDtypeStruct(base.shape, dtype),
        in_specs=[whole, whole, spec, pl.BlockSpec((1, 1, count), lambda i: (i, 0, 0))],
        out_specs=spec,
        compiler_params=pltpu.CompilerParams(vmem_limit_bytes=14 << 20),
        cost_estimate=pl.CostEstimate(flops=0, bytes_accessed=1024, transcendentals=0),
        name="place_kept",
    )(here, there, base, index.reshape(images, 1, count))


def kernel_output(own, moved, residual, grad, mods, kept_out, sums):
    core = core_here()
    half = mods.shape[1] // 2
    rows = residual.shape[0] // half
    for image in range(half):
        at = slice(image * rows, (image + 1) * rows)
        mlp_out = own[at, :].astype(f32) + moved[at, :].astype(f32)
        gate = mods[5, pl.ds(core * half + image, 1), :]
        kept_out[at, :] = (residual[at, :] + gate * mlp_out).astype(bf16)
        sums[pl.ds(image, 1), :] = jnp.sum(
            grad[at, :].astype(f32) * mlp_out, axis=0, keepdims=True
        )


def kernel_first_back(
    own, moved, residual_grad, kept, mods, late, last, kept_grad, mine, partner
):
    me = lax.axis_index("mp")
    core = me & 1
    half = mods.shape[1] // 2
    rows = residual_grad.shape[0] // half
    local = mine.shape[2]
    lines = [[], []]
    for image in range(half):
        at = slice(image * rows, (image + 1) * rows)
        normed, inverse = layer_norm(kept[at, :].astype(f32))
        gradient = own[at, :].astype(f32) + moved[at, :].astype(f32)
        lines[0].append(jnp.sum(gradient, axis=0, keepdims=True))
        lines[1].append(jnp.sum(gradient * normed, axis=0, keepdims=True))
        scale = mods[1, pl.ds(core * half + image, 1), :]
        values = residual_grad[at, :] + norm_back(normed, inverse, gradient * (1.0 + scale))
        kept_grad[at, :] = values.astype(bf16)
    planes = [jnp.concatenate(line, 0) for line in lines]
    planes += [late[0], late[1], late[2], last[...]]
    for k, plane in enumerate(planes):
        blocks = [plane[:, j * local : (j + 1) * local] for j in range(4)]
        for out, device in ((mine, me), (partner, me ^ 1)):
            picked = blocks[0]
            for j in range(1, 4):
                picked = jnp.where(device == j, blocks[j], picked)
            out[k] = picked.astype(bf16)


def new_state(weight, moment, average, gradient, rate, steps):
    decay = (1.0 + steps) / (10.0 + steps)
    new_moment = momentum_rate * moment + gradient
    master = weight - rate * (gradient + momentum_rate * new_moment)
    return master, new_moment, decay * average + (1.0 - decay) * master


def summed(given):
    total = given[0][...].astype(f32)
    for ref in given[1:]:
        total = total + ref[...].astype(f32)
    return total


def one_step(rate, count, index, steps, *refs):
    given, refs = refs[:count], refs[count:]
    values = new_state(*[ref[...] for ref in refs[:3]], summed(given), rate, steps[0].astype(f32))
    for ref, value in zip(refs[3:], values):
        ref[...] = value


def attention_step(rate, count, index, steps, *refs):
    given, refs = refs[:count], refs[count:]
    gradient = summed(given)
    counts = steps[0].astype(f32)
    qkv, proj, qkv_out, proj_out = refs[:3], refs[3:6], refs[6:9], refs[9:]
    local = proj[0].shape[1]
    for t in range(3):
        values = new_state(
            *[ref[t] for ref in qkv], gradient[:, t * local : (t + 1) * local], rate, counts
        )
        for ref, value in zip(qkv_out, values):
            ref[t] = value
    values = new_state(*[ref[...] for ref in proj], gradient[:, 3 * local :], rate, counts)
    for ref, value in zip(proj_out, values):
        ref[...] = value


def step_weights(kernel, name, state, given, rate, steps, limit=None):
    rows = given[0].shape[0]
    block = 48 if rows % 48 == 0 else rows
    count = rows // block

    def spec(x):
        if x.ndim == 3:
            return pl.BlockSpec((x.shape[0], block, x.shape[2]), lambda i, index: (0, i, 0))
        return pl.BlockSpec((block, x.shape[1]), lambda i, index: (i, 0))

    own = pl.BlockSpec((block, given[0].shape[1]), lambda i, index: (index[0] * count + i, 0))
    specs = [spec(x) for x in given[:2]] + [own] * (len(given) - 2)
    return pl.pallas_call(
        partial(kernel, rate, len(given)),
        grid_spec=pltpu.PrefetchScalarGridSpec(
            num_scalar_prefetch=1,
            grid=(count,),
            in_specs=[pl.BlockSpec(memory_space=pltpu.SMEM)] + specs + [spec(x) for x in state],
            out_specs=[spec(x) for x in state],
        ),
        out_shape=[jax.ShapeDtypeStruct(x.shape, f32) for x in state],
        compiler_params=pltpu.CompilerParams(vmem_limit_bytes=limit),
        cost_estimate=pl.CostEstimate(flops=0, bytes_accessed=1024, transcendentals=0),
        name=name,
    )(lax.axis_index("dp").astype(jnp.int32).reshape(1), steps, *given, *state)


def ada_step(rate, steps, cond, mods, weight, moment, average, master, new_moment, ema):
    counts = steps[0].astype(f32)
    for k in range(weight.shape[0]):
        gradient = dot_first(cond[...], mods[k])
        values = new_state(weight[k], moment[k], average[k], gradient, rate, counts)
        master[k], new_moment[k], ema[k] = values


def step_ada(weight, moment, average, cond, mods, rate, steps):
    count, rows, columns = weight.shape
    spec = pl.BlockSpec((2, rows, columns), lambda k: (k, 0, 0))
    return pl.pallas_call(
        partial(ada_step, rate),
        grid=(count // 2,),
        out_shape=[jax.ShapeDtypeStruct(weight.shape, f32)] * 3,
        in_specs=[
            pl.BlockSpec(memory_space=pltpu.SMEM),
            pl.BlockSpec(cond.shape, lambda k: (0, 0)),
            pl.BlockSpec((2,) + mods.shape[1:], lambda k: (k, 0, 0)),
        ]
        + [spec] * 3,
        out_specs=[spec] * 3,
        cost_estimate=pl.CostEstimate(flops=0, bytes_accessed=1024, transcendentals=0),
        name="step_ada",
    )(steps, cond, mods, weight, moment, average)


def per_device(
    tokens,
    condition,
    cotangent,
    kept_index,
    skip_index,
    step_count,
    ada_weight,
    qkv_weight,
    proj_weight,
    fc1_weight,
    fc2_weight,
    ada_moment,
    qkv_moment,
    proj_moment,
    fc1_moment,
    fc2_moment,
    ada_average,
    qkv_average,
    proj_average,
    fc1_average,
    fc2_average,
):
    images, seq, width = tokens.shape
    kept_count = kept_index.shape[1]
    own_d = ada_weight.shape[0]
    mods = ada_weight.shape[1]
    local = ada_weight.shape[2]
    units = fc1_weight.shape[1]
    local_heads = local // HEAD_DIM
    total = images * kept_count
    half = total // 2
    core = lax.axis_index("mp") % 2
    chip = lax.axis_index("mp") // 2
    dp_size = lax.axis_size("dp")
    index = lax.axis_index("dp")
    ring = dp_size == 8

    live = []

    def tick(extras, *hops):
        hops = [(one, sides) for one, sides in hops if one is not None]
        busy = [one for one, _ in hops]
        idle = [one for one in live if one not in busy]
        moving = tuple(one.start(sides) for one, sides in hops)
        work = tuple(extras())
        resting = tuple((one.held["a"], one.held["b"]) for one in idle)
        held, moved, resting = stage((work, moving, resting))
        for (one, sides), values in zip(hops, moved):
            one.finish(sides, values)
        for one, values in zip(idle, resting):
            one.finish("ab", values)
        return held

    rate = 0.02 / math.sqrt(images * dp_size * kept_count)

    attn_low = jnp.concatenate(
        [qkv_weight[0], qkv_weight[1], qkv_weight[2], proj_weight.T], 1
    ).astype(bf16)
    fc1_low = fc1_weight.astype(bf16)
    fc2_low = fc2_weight.T.astype(bf16)
    if ring:
        attn_ring, fc1_ring, fc2_ring = Gather(attn_low, 1), Gather(fc1_low, 1), Gather(fc2_low, -1)
    else:
        attn_ring = fc1_ring = fc2_ring = None
        attn_pieces, attn_places = [gather_plain(attn_low)], [None]
        fc1_pieces, fc1_places = [gather_plain(fc1_low)], [None]
        fc2_pieces, fc2_places = [gather_plain(fc2_low)], [None]
    block = [((width // 8, units), bf16)] * 2 if ring else []
    attn_block = [((width // 8, 4 * local), bf16)] * 2 if ring else []

    cond_float = condition.astype(f32)
    silu_cond = jax.nn.silu(cond_float).astype(bf16)
    small = silu_cond.reshape(images, dp_size, own_d)
    levels = len(dp_groups())
    def first_norm():
        return spread_round(small, 0, 0), *run(
            kernel_norm,
            "first_norm",
            [((half, width), bf16), ((total, width), f32)],
            (tokens, kept_index),
        )

    small, kept_own, normed = tick(first_norm, (attn_ring, "ab"))
    ada_state = [jnp.moveaxis(x, 1, 0) for x in (ada_weight, ada_moment, ada_average)]

    def rest_of_cond():
        values = small
        for level in range(1, levels):
            values = spread_round(values, 0, level)
        return (values,)

    (small,) = tick(rest_of_cond, (attn_ring, "ab"))

    def sum_of_mods():
        own = lax.dynamic_index_in_dim(small, index, 1, keepdims=False)
        (values,) = run(
            kernel_mods, "mods", [((mods, dp_size * images, local), f32)], (own, ada_state[0])
        )
        for level in reversed(range(1, levels)):
            values = sum_round(values, 1, level)
        return own, values

    cond_own, small = tick(sum_of_mods, (attn_ring, "ab"))
    (mod_local,) = tick(lambda: (sum_round(small, 1, 0),), (attn_ring, "a"))
    if ring:
        attn_pieces, attn_places = attn_ring.pieces()

    def all_mods():
        at_core = swap_core(mod_local)
        at_x = swap_x(mod_local)
        at_both = lax.ppermute(mod_local, "mp", [(j, j ^ 3) for j in range(4)])
        pairs = [join_pair(mod_local, at_core, core, 2), join_pair(at_x, at_both, core, 2)]
        return (
            jnp.where(chip == 0, jnp.concatenate(pairs, 2), jnp.concatenate(pairs[::-1], 2)),
        )

    (modulation,) = tick(all_mods, (fc1_ring, "ab"))


    def project():
        outs = [((total, width), bf16), ((total, 3 * local), bf16)]
        lanes = -(-3 * local // 128) * 128
        return run(
            partial(kernel_project, attn_places),
            "project",
            outs,
            (*attn_pieces, normed, modulation),
            [((width, lanes), bf16), ((total, width), f32)] + outs,
        )

    hidden, projected = tick(project, (fc2_ring, "ab"))

    def add_low(own, other):
        return (own + other.astype(f32)).astype(bf16)

    def attend():
        outs = [((total, local), bf16), ((half, width), f32), ((half, width), bf16)]
        lanes = 4 * local - lane_start(3 * local)
        return run(
            partial(kernel_attend, attn_places, local_heads, kept_count),
            "attend",
            outs,
            (*attn_pieces, projected),
            [((width, lanes), bf16), ((total, 3 * local), bf16)] + outs,
        )

    attended, own_part, other_part = tick(attend, (fc1_ring, "ab"))

    def attention_sums():
        own = add_low(own_part, swap_core(other_part))
        return own, swap_x(own), *kept_grads()


    def kept_grads():
        return run(
            kernel_kept_grad,
            "kept_grad",
            [((half, width), bf16), ((total, width), bf16)],
            (cotangent, kept_index, modulation),
        )

    attn_own, attn_moved, grad_own, mlp_grad = tick(
        attention_sums, (fc1_ring, "ab"), (fc2_ring, "ab")
    )

    def second_norm():
        values, low = run(
            kernel_second_norm,
            "second_norm",
            [((half, width), f32), ((half, width), bf16)],
            (kept_own, modulation, attn_own, attn_moved),
        )
        return values, low

    residual, hidden_here = tick(second_norm, (fc1_ring, "a"), (fc2_ring, "a"))
    hidden_here, hidden_there = tick(lambda: (hidden_here, swap_core(hidden_here)))
    if ring:
        fc1_pieces, fc1_places = fc1_ring.pieces()

    def feed_forward():
        outs = [((total, units), f32), ((total, units), bf16), ((width, units), bf16)]
        return run(
            partial(kernel_feed_forward, fc1_places, -1),
            "feed_forward",
            outs + block,
            (*fc1_pieces, hidden_here, hidden_there, mlp_grad),
            [((width, units), bf16), ((total, width), bf16), ((total, width), bf16)] + outs,
        )

    pre_act, activated, fc2_grad, *first = tick(feed_forward, (fc2_ring, "ba"))
    if ring:
        fc2_pieces, fc2_places = fc2_ring.pieces()
        fc2_sums = Scatter(fc2_grad, -1, first)
        live.append(fc2_sums)
    else:
        fc2_sums = fc1_sums = attn_sums = None

    def feed_back():
        outs = [((total, units), bf16), ((half, width), f32), ((half, width), bf16)]
        return run(
            partial(kernel_feed_back, fc1_places, fc2_places),
            "feed_back",
            outs,
            (*fc1_pieces, *fc2_pieces, mlp_grad, pre_act),
            [
                ((width, units), bf16),
                ((width, units), bf16),
                ((total, width), bf16),
                ((total, units), f32),
            ]
            + outs,
        )

    pre_grad, own_part, other_part = tick(feed_back, (fc2_sums, "ab"))
    moving = []

    def products():
        own_low = add_low(own_part, swap_core(other_part))
        outs = [((width, units), bf16)]
        grad, *first = run(
            partial(kernel_fc1_grad, -1),
            "fc1_grad",
            outs + block,
            (hidden_here, hidden_there, pre_grad),
            [((total, width), bf16), ((total, units), bf16)] + outs,
        )
        if ring:
            moving.append(Scatter(grad, -1, first))
            first = moving[0].start("ab")
        return own_low, swap_x(own_low), grad, activated, *first

    hidden_own, hidden_moved, fc1_grad, activated, *first = tick(
        products, (fc2_sums, "ab+")
    )
    if ring:
        (fc1_sums,) = moving
        fc1_sums.part = fc1_grad
        fc1_sums.finish("ab", first)
        live.append(fc1_sums)

    def second_back():
        values, low, lines = run(
            kernel_second_back,
            "second_back",
            [((half, width), f32), ((half, width), bf16), ((3, images // 2, width), f32)],
            (
                hidden_own,
                hidden_moved,
                residual,
                attn_own,
                attn_moved,
                grad_own,
                modulation,
            ),
        )
        outs = [((half, width), f32), ((half, width), bf16)]
        mlp = run(
            partial(kernel_feed_out, fc2_places),
            "feed_out",
            outs,
            (*fc2_pieces, activated),
            [((width, units), bf16), ((total, units), bf16)] + outs,
        )
        sums = ()
        if ring:
            held = stage((fc1_sums.held["a"], fc1_sums.held["b"], low))
            fc1_sums.finish("ab", held[:2])
            sums = fc1_sums.prepare("ab")
        return values, low, lines, *mlp, *sums

    residual_grad, out_here, late_mods, own_mlp, other_mlp, *sums = tick(
        second_back, (fc2_sums, "ab")
    )
    if ring:
        fc1_sums.finish("ab", sums)

    def between():
        sums = fc2_sums.prepare("a") if ring else ()
        low = add_low(own_mlp, swap_core(other_mlp))
        return out_here, swap_core(out_here), low, *sums

    out_here, out_there, mlp_own, *sums = tick(between)
    if ring:
        fc2_sums.finish("a", sums)

    def attention_back():
        outs = [((width, 4 * local), bf16), ((half, width), f32), ((half, width), bf16)]
        back = run(
            partial(kernel_attention_back, attn_places, local_heads, kept_count, 1),
            "attention_back",
            outs + attn_block,
            (*attn_pieces, out_here, out_there, projected, attended, hidden),
            [
                ((width, 4 * local), bf16),
                ((total, width), bf16),
                ((total, 3 * local), bf16),
                ((total, local), bf16),
                ((total, width), bf16),
                ((total, local), bf16),
                ((total, 3 * local), bf16),
            ]
            + outs,
        )
        return swap_x(mlp_own), *back

    mlp_moved, attn_grad, own_part, other_part, *first = tick(
        attention_back, (fc1_sums, "ab"), (fc2_sums, "a")
    )
    if ring:
        attn_sums = Scatter(attn_grad, 1, first)
        live.append(attn_sums)

    def output():
        return run(
            kernel_output,
            "output",
            [((half, width), bf16), ((images // 2, width), f32)],
            (mlp_own, mlp_moved, residual, grad_own, modulation),
        )

    back_own, mlp_moved = tick(
        lambda: (add_low(own_part, swap_core(other_part)), mlp_moved)
    )

    def attention_back_sums():
        given = fc2_sums.given() if ring else (scatter_plain(fc2_grad),)
        state = (fc2_weight.T, fc2_moment.T, fc2_average.T)
        new = step_weights(one_step, "step_fc2", state, given, rate, step_count, 12 << 20)
        return swap_x(back_own), *output(), *new

    if ring:
        live.remove(fc2_sums)
    back_moved, kept_out, last_mods, fc2_master, fc2_momentum, fc2_ema = tick(
        attention_back_sums, (attn_sums, "ab+"), (fc1_sums, "ab")
    )

    def first_back():
        kept, mine, partner = run(
            kernel_first_back,
            "first_back",
            [
                ((half, width), bf16),
                ((mods, images // 2, local), bf16),
                ((mods, images // 2, local), bf16),
            ],
            (
                back_own,
                back_moved,
                residual_grad,
                kept_own,
                modulation,
                late_mods,
                last_mods,
            ),
        )
        values = spread_round(join_pair(mine, swap_core(partner), core, 1), 1, 0)
        return kept, values, kept_out

    kept_grad, small, kept_out = tick(first_back, (attn_sums, "ab"))

    def last_spread():
        sums = fc1_sums.prepare("a") if ring else ()
        values = small
        for level in range(1, levels):
            values = spread_round(values, 1, level)
        there = swap_core(kept_grad), swap_core(kept_out)
        return values, kept_grad, kept_out, *there, *sums

    mod_grad_all, kept_grad, kept_out, grad_there, kept_there, *sums = tick(
        last_spread, (attn_sums, "ab+")
    )
    if ring:
        fc1_sums.finish("a", sums)

    def silu_sums():
        (part,) = run(
            kernel_silu, "silu", [((dp_size * images, own_d), f32)], (mod_grad_all, ada_state[0])
        )
        grads = place_kept(kept_grad, grad_there, cotangent, kept_index, f32)
        out = place_kept(kept_out, kept_there, tokens, kept_index, bf16)
        return part + swap_core(part), grads, out, mod_grad_all

    silu_part, tokens_grad, block_out, mod_grad_all = tick(
        silu_sums, (attn_sums, "a"), (fc1_sums, "a")
    )

    def step_beside_x():
        given = attn_sums.given() if ring else (scatter_plain(attn_grad),)
        state = (qkv_weight, qkv_moment, qkv_average)
        state += (proj_weight.T, proj_moment.T, proj_average.T)
        new = step_weights(attention_step, "step_attention", state, given, rate, step_count)
        return silu_part + swap_x(silu_part), mod_grad_all, *new

    silu_part, mod_grad_all, *attn_new = tick(step_beside_x)
    silu_blocks = silu_part.reshape(dp_size, images, own_d)

    def step_beside_turn():
        blocks = silu_blocks
        for level in reversed(range(1, levels)):
            blocks = turn_round(blocks, level)
        return blocks, *step_ada(*ada_state, cond_own, mod_grad_all, rate, step_count)

    silu_blocks, *ada_new = tick(step_beside_turn)
    silu_blocks = in_order(turn_round(silu_blocks, 0))
    given = fc1_sums.given() if ring else (scatter_plain(fc1_grad),)
    state = (fc1_weight, fc1_moment, fc1_average)
    fc1_master, fc1_momentum, fc1_ema = step_weights(
        one_step, "step_fc1", state, given, rate, step_count
    )
    qkv_master, qkv_momentum, qkv_ema, proj_master, proj_momentum, proj_ema = attn_new
    ada_master, ada_momentum, ada_ema = [jnp.moveaxis(x, 0, 1) for x in ada_new]
    silu_grad = jnp.moveaxis(silu_blocks, 0, 1).reshape(images, width)
    silu_value, silu_pull = jax.vjp(jax.nn.silu, cond_float)
    condition_grad = silu_pull(silu_grad)[0]
    return (
        block_out,
        tokens_grad,
        condition_grad,
        ada_master,
        qkv_master,
        proj_master.T,
        fc1_master,
        fc2_master.T,
        ada_momentum,
        qkv_momentum,
        proj_momentum.T,
        fc1_momentum,
        fc2_momentum.T,
        ada_ema,
        qkv_ema,
        proj_ema.T,
        fc1_ema,
        fc2_ema.T,
    )


def solution(mesh):
    weights = (
        P("dp", None, "mp"),
        P(None, "dp", "mp"),
        P("mp", "dp"),
        P("dp", "mp"),
        P("mp", "dp"),
    )
    rows = P("dp", None, None)
    pairs = P("dp", None)
    return jax.shard_map(
        per_device,
        mesh=mesh,
        in_specs=(rows, pairs, rows, pairs, pairs, P()) + weights * 3,
        out_specs=(rows, rows, pairs) + weights * 3,
        check_vma=False,
    )
```
